256 devices in a mesh: box: 4 (over z_lo), tile: 64 (over z_hi, y, x, core).
Axes of the slice: x: 4, y: 4, z: 8 (z_hi: 2, z_lo: 4; z = z_hi * 4 + z_lo), core: 2. Of those that a mesh axis runs over, the one named last changes fastest.
Arguments:
- box_maps: float32 [4, 6, 448, 2688], P('box', None, 'tile'), may hold values from -4.01 to 4.01, as said below
- face_slots: int32 [4, 6], replicated, may hold values from 0 to 5, each once within a row
Outputs:
- final_map: float32 [7168, 7168], P('tile', 'box')
The draws below stay inside these ranges and needn't reach their ends.
Inputs may be any that keep to these rules, and one draw needn't show every extreme that they name: `box_maps`: read as a matrix of order 6 * 448 with rows and columns ordered by stored block and node, each box's map is exactly symmetric and positive definite. `face_slots`: each row is a permutation of the six stored blocks.
All inputs are finite; a program needn't handle non-finite values.
Results may differ from the reference program's by a relative error of at most 0.0001.
Values sent between devices are 32-bit elements; how exact they have to be, the bound alone decides.
No kernel may reach another device: no remote copies, remote signals or barrier semaphores. Data moves between devices by JAX's collectives and lax.ppermute only.
A program may use at most 64 MiB of HBM per device.

```python
import math
import jax
import jax.numpy as jnp
from jax import lax

F = 448


def draw_box_maps(key, part):
    extent = 6 * F
    factor_key, weight_key = jax.random.split(jax.random.fold_in(key, 11), 2)
    factors = jax.random.truncated_normal(factor_key, -3.0, 3.0, (4, extent, extent), jnp.float32)
    weights = jnp.exp(jax.random.uniform(weight_key, (4, 1, extent), jnp.float32, math.log(0.05), math.log(5.0)))
    gramian = jnp.einsum('bik,bjk->bij', factors * weights, factors, precision=lax.Precision.HIGHEST) / extent
    matrices = gramian + 0.1 * jnp.eye(extent, dtype=jnp.float32)
    largest = jnp.max(jnp.diagonal(matrices, 0, 1, 2), axis=1)
    matrices = matrices * (4.0 / largest)[:, None, None]
    matrices = (matrices + jnp.swapaxes(matrices, 1, 2)) * 0.5
    return matrices.reshape(4, 6, F, extent)


def setup_inputs(seed: int = 0) -> dict:
    keys = jax.random.split(jax.random.key(seed), 3)
    return {
        "box_maps": draw_box_maps(jax.random.fold_in(keys[2], 71), 0),
        "face_slots": jax.vmap(lambda own: jax.random.permutation(own, 6))(jax.random.split(keys[1], 4)).reshape((4, 6)).astype(jnp.int32),
    }


def matmul(left, right):
    return jnp.dot(left.astype(jnp.float32), right.astype(jnp.float32), precision=lax.Precision.HIGHEST, preferred_element_type=jnp.float32)

def lower_solve(factor, coupled):
    return jax.scipy.linalg.solve_triangular(factor, coupled.T, lower=True).T

def reference(box_maps, face_slots):
    matrices = box_maps.reshape(4, 6 * F, 6 * F)

    def face_block(box_id, row_face, col_face):
        row_start = (face_slots[box_id, row_face] * F).astype(jnp.int32)
        col_start = (face_slots[box_id, col_face] * F).astype(jnp.int32)
        return lax.dynamic_slice(matrices[box_id], (row_start, col_start), (F, F))
    layouts = []
    for box_id in range(4):
        along_x, along_y = (box_id % 2, box_id // 2)
        layouts.append((1 - along_x, [along_x, 2 + along_y, 4, 5], 3 - along_y))
    level_one = []
    for pair_id in range(2):
        left_box, right_box = (2 * pair_id, 2 * pair_id + 1)
        summed = face_block(left_box, layouts[left_box][0], layouts[left_box][0]) + face_block(right_box, layouts[right_box][0], layouts[right_box][0])
        factor = jnp.linalg.cholesky(summed)
        for box_id in (left_box, right_box):
            x_shared, finals, y_shared = layouts[box_id]
            coupled = jnp.concatenate([face_block(box_id, surface, x_shared) for surface in finals + [y_shared]], 0)
            level_one.append(lower_solve(factor, coupled))
    zero_block = jnp.zeros((F, F), jnp.float32)
    pair_terms = []
    shared_rows = []
    for pair_id in range(2):
        left_box, right_box = (2 * pair_id, 2 * pair_id + 1)
        stacked = jnp.concatenate([level_one[left_box][4 * F:], level_one[right_box][4 * F:]], 0)
        shared_rows.append(stacked)
        left_face = face_block(left_box, layouts[left_box][2], layouts[left_box][2])
        right_face = face_block(right_box, layouts[right_box][2], layouts[right_box][2])
        diagonal = jnp.concatenate([jnp.concatenate([left_face, zero_block], 1), jnp.concatenate([zero_block, right_face], 1)], 0)
        pair_terms.append(diagonal - matmul(stacked, stacked.T))
    factor_two = jnp.linalg.cholesky(pair_terms[0] + pair_terms[1])
    level_two = []
    for box_id in range(4):
        x_shared, finals, y_shared = layouts[box_id]
        direct = jnp.concatenate([face_block(box_id, surface, y_shared) for surface in finals], 0)
        empty_part = jnp.zeros_like(direct)
        placed = jnp.concatenate([direct, empty_part] if box_id % 2 == 0 else [empty_part, direct], 1)
        coupled = placed - matmul(level_one[box_id][:4 * F], shared_rows[box_id // 2].T)
        level_two.append(lower_solve(factor_two, coupled))
    row_blocks = []
    for box_id in range(4):
        finals = layouts[box_id][1]
        entries = []
        for column_box in range(4):
            entry_block = jnp.zeros((4 * F, 4 * F), jnp.float32)
            if column_box == box_id:
                entry_block = entry_block + jnp.concatenate([jnp.concatenate([face_block(box_id, surface, other_face) for other_face in finals], 1) for surface in finals], 0)
            if column_box // 2 == box_id // 2:
                entry_block = entry_block - matmul(level_one[box_id][:4 * F], level_one[column_box][:4 * F].T)
            entry_block = entry_block - matmul(level_two[box_id], level_two[column_box].T)
            entries.append(entry_block)
        row_blocks.append(jnp.concatenate(entries, 1))
    return jnp.concatenate(row_blocks, 0)
```

```python
import functools

import jax
import jax.numpy as jnp
from jax import lax
from jax.experimental import pallas as pl
from jax.experimental.pallas import tpu as pltpu
from jax.sharding import PartitionSpec as P

F = 448
NODES = 7
LANES = 128
MICRO = 16
VMEM_BYTES = 56 * 1024 * 1024


def tile_of(z, y, x, core):
    return ((z * 4 + y) * 4 + x) * 2 + core


PLANES = [
    [tile_of(z, y, x, core) for y in range(4) for x in range(4)]
    for z in range(2)
    for core in range(2)
]
QUARTERS = [[16 * quarter + own for own in range(16)] for quarter in range(4)]


def matmul(left, right):
    return jnp.dot(left, right, precision=lax.Precision.HIGHEST, preferred_element_type=jnp.float32)


def matmul_nt(left, right):
    return lax.dot_general(
        left,
        right,
        (((1,), (1,)), ((), ())),
        precision=lax.Precision.HIGHEST,
        preferred_element_type=jnp.float32,
    )


def invert(stack):
    full = (8, LANES)
    lane = lax.broadcasted_iota(jnp.int32, full, 1)
    sub = lax.broadcasted_iota(jnp.int32, full, 0)

    def along_rows(value, row):
        return jnp.broadcast_to(value[row : row + 1, :], full)

    def along_lanes(value, column):
        return jnp.broadcast_to(value[:, column : column + 1], full)

    stack = [list(rows) for rows in stack]
    count = len(stack[0])
    which = range(len(stack))
    for start in range(0, 8 * count, MICRO):
        first = start // 8
        inside = (lane >= start) & (lane < start + MICRO)
        following = [group for group in (first + 2, first + 3) if group < count]
        rest = [g for g in range(count) if g not in (first, first + 1, *following)]
        pivots = [
            [[along_lanes(stack[n][first + h], start + k) for h in range(2)] for k in range(MICRO)]
            for n in which
        ]
        rows = [
            [
                jnp.where(
                    inside,
                    jnp.where(lane == start + 8 * h + sub, 1.0, 0.0),
                    stack[n][first + h],
                )
                for h in range(2)
            ]
            for n in which
        ]
        ahead = [
            [[along_lanes(stack[n][group], start + k) for k in range(MICRO)] for group in following]
            for n in which
        ]
        for j in range(MICRO):
            half, row = divmod(j, 8)
            chosen = sub == row
            for n in which:
                scale = 1.0 / along_rows(pivots[n][j][half], row)
                pivot_row = along_rows(rows[n][half], row) * scale
                for k in range(j + 1, MICRO):
                    scaled = along_rows(pivots[n][k][half], row) * scale
                    for h in range(2):
                        value = pivots[n][k][h] - pivots[n][j][h] * scaled
                        pivots[n][k][h] = jnp.where(chosen, scaled, value) if h == half else value
                for h in range(2):
                    value = rows[n][h] - pivots[n][j][h] * pivot_row
                    rows[n][h] = jnp.where(chosen, pivot_row, value) if h == half else value
        for n in which:
            spread = [along_rows(rows[n][k // 8], k % 8) for k in range(MICRO)]
            for position, group in enumerate(following):
                terms = [ahead[n][position][k] * spread[k] for k in range(MICRO)]
                while len(terms) > 1:
                    terms = [terms[i] + terms[i + 1] for i in range(0, len(terms), 2)]
                stack[n][group] = jnp.where(inside, 0.0, stack[n][group]) - terms[0]
            if rest:
                zero = jnp.zeros(full, jnp.float32)
                held = jnp.concatenate([stack[n][group] for group in rest], 0)
                panel = jnp.concatenate(
                    [zero] * first + rows[n] + [zero] * (LANES // 8 - first - 2), 0
                )
                update = matmul(held, panel)
                for i, group in enumerate(rest):
                    stack[n][group] = (
                        jnp.where(inside, 0.0, stack[n][group]) - update[8 * i : 8 * i + 8]
                    )
            stack[n][first], stack[n][first + 1] = rows[n]
    return stack


def groups_of(value):
    return [value[8 * g : 8 * g + 8, :] for g in range(value.shape[0] // 8)]


def node_orders(z, core):
    shape = (F, 256)
    target = lax.broadcasted_iota(jnp.int32, shape, 0)
    source = lax.broadcasted_iota(jnp.int32, shape, 1)
    inner = source % 8
    half = (source // 8) % 2
    place = source // 16
    half = jnp.where(z == 1, 1 - half, half)
    orders = []
    for held_core in (core, 1 - core):
        node = NODES * ((half * 16 + place) * 2 + held_core) + inner
        hit = (node == target) & (inner < NODES)
        orders.append(jnp.where(hit, 1.0, 0.0).astype(jnp.bfloat16))
    return orders


def in_node_order(orders, pieces):
    total = None
    for order, piece in zip(orders, pieces):
        for _ in range(3):
            part = piece.astype(jnp.bfloat16)
            piece = piece - part.astype(jnp.float32)
            term = jnp.dot(order, part, preferred_element_type=jnp.float32)
            total = term if total is None else total + term
    return total


def pair_kernel(place_ref, own_ref, other_ref, inverse_ref, work, panel):
    orders = node_orders(place_ref[0], place_ref[1])
    work[...] = jnp.zeros_like(work)
    for n in range(2):
        pieces = [ref[:, :, n].reshape(256, F) for ref in (own_ref, other_ref)]
        work[n, :F, :F] = in_node_order(orders, pieces)

    def eliminate(block, height):
        at = pl.ds(pl.multiple_of(block * LANES, LANES), LANES)
        squares = [groups_of(work[n, at, at])[: height // 8] for n in range(2)]
        inverses = invert(squares)
        for n in range(2):
            square = jnp.concatenate(inverses[n], 0)
            if height < LANES:
                square = jnp.concatenate(
                    [square, jnp.zeros((LANES - height, LANES), jnp.float32)], 0
                )
            panel[n] = matmul(square, work[n, at, :])
            panel[n, :, at] = square

        def update(step, carry):
            index = step + jnp.where(step >= block, 1, 0)
            rows = pl.ds(pl.multiple_of(index * LANES, LANES), LANES)
            for n in range(2):
                left = work[n, rows, at]
                work[n, rows, at] = jnp.zeros((LANES, LANES), jnp.float32)
                work[n, rows, :] = work[n, rows, :] - matmul(left, panel[n])
            return carry

        lax.fori_loop(0, 3, update, 0)
        for n in range(2):
            work[n, at, :] = panel[n]

    def step(block, carry):
        eliminate(block, LANES)
        return carry

    lax.fori_loop(0, 3, step, 0)
    eliminate(jnp.int32(3), F - 3 * LANES)
    inverse_ref[...] = work[:, :F, :F]


def merge_kernel(
    place_ref,
    own_ref,
    other_ref,
    inverse_ref,
    coupled_ref,
    direct_ref,
    first_ref,
    second_ref,
    coupling,
    weighted,
    system,
    panel,
):
    orders = node_orders(place_ref[0], place_ref[1])

    def ordered(index):
        pieces = [ref[:, :, index].reshape(256, 512) for ref in (own_ref, other_ref)]
        return in_node_order(orders, pieces)

    for pair in range(2):
        for side in range(2):
            coupling[pair, side * F : side * F + F, :] = ordered(2 * pair + side)[:, :F]

    def weigh(index, carry):
        rows = pl.ds(pl.multiple_of(index * LANES, LANES), LANES)
        for pair in range(2):
            weighted[pair, rows, :] = matmul(coupling[pair, rows, :], inverse_ref[pair])
        return carry

    lax.fori_loop(0, 7, weigh, 0)

    def build(index, carry):
        rows = pl.ds(pl.multiple_of(index * LANES, LANES), LANES)
        total = matmul_nt(coupling[0, rows, :], weighted[0])
        total = total + matmul_nt(coupling[1, rows, :], weighted[1])
        system[rows, :] = -total
        return carry

    lax.fori_loop(0, 7, build, 0)
    system[:F, :512] = system[:F, :512] + ordered(4)
    system[F : 2 * F, 384:] = system[F : 2 * F, 384:] + ordered(5)
    coupled = coupled_ref[...].reshape(LANES, F)
    direct = direct_ref[...].reshape(LANES, 2 * F)
    system[2 * F :, :] = direct - matmul_nt(coupled, weighted[place_ref[2]])

    def eliminate(block, carry):
        at = pl.ds(pl.multiple_of(block * LANES, LANES), LANES)
        square = jnp.concatenate(invert([groups_of(system[at, at])])[0], 0)
        panel[...] = matmul(square, system[at, :])
        panel[:, at] = -square

        def update(index, inner):
            rows = pl.ds(pl.multiple_of(index * LANES, LANES), LANES)
            left = system[rows, at]
            system[rows, at] = jnp.zeros((LANES, LANES), jnp.float32)
            system[rows, :] = system[rows, :] - matmul(left, panel[...])
            return inner

        lax.fori_loop(block + 1, 8, update, 0)
        return carry

    lax.fori_loop(0, 7, eliminate, 0)
    solved = system[2 * F :, :]
    same_pair = jnp.where(place_ref[2] == 0, 1.0, 0.0)
    first_ref[...] = same_pair * matmul(coupled, inverse_ref[0]) - matmul(solved, weighted[0])
    second_ref[...] = solved[:, :F]


def output_kernel(first_ref, second_ref, columns_ref, own_ref, out_ref):
    target = lax.broadcasted_iota(jnp.int32, (112, LANES), 0)
    source = lax.broadcasted_iota(jnp.int32, (112, LANES), 1)
    hit = (NODES * (source // 8) + source % 8 == target) & (source % 8 < NODES)
    compact = jnp.where(hit, 1.0, 0.0)
    node = lax.broadcasted_iota(jnp.int32, (F, 512), 0)
    place = lax.broadcasted_iota(jnp.int32, (F, 512), 1)
    hit = (NODES * (place // 8) + place % 8 == node) & (place % 8 < NODES)
    widen = jnp.where(hit, 1.0, 0.0)
    total = matmul(compact, own_ref[...].reshape(LANES, -1))
    for index, ref in enumerate((first_ref, second_ref)):
        rows = matmul(matmul(compact, ref[...]), widen)
        columns = columns_ref[:, index].reshape(512, -1)
        total = total - matmul(rows, columns)
    out_ref[...] = total


def padded(value):
    return jnp.pad(value, [(0, 0)] * (value.ndim - 2) + [(0, 1), (0, 0)])


def other_half(value, axis_part):
    flip = 32 if axis_part == "z" else 1
    return lax.ppermute(value, "tile", [(tile, tile ^ flip) for tile in range(64)])


def to_plane(value):
    value = jnp.stack([value, other_half(value, "z")])
    copies = jnp.broadcast_to(value, (16, *value.shape))
    return lax.all_to_all(
        copies, "tile", split_axis=0, concat_axis=0, tiled=True, axis_index_groups=PLANES
    )


def per_device(box_maps, face_slots):
    stored = box_maps[0]
    box_id = lax.axis_index("box")
    tile_id = lax.axis_index("tile")
    along_x = box_id % 2
    along_y = box_id // 2
    slot_row = lax.dynamic_index_in_dim(face_slots, box_id, 0, keepdims=False)

    def slot_of(surface):
        return lax.dynamic_index_in_dim(slot_row, surface, 0, keepdims=False)

    x_shared = slot_of(1 - along_x)
    y_shared = slot_of(3 - along_y)
    finals = [slot_of(along_x), slot_of(2 + along_y), slot_row[4], slot_row[5]]

    def block(row_slot, col_slot):
        return lax.dynamic_slice(stored, (row_slot, 0, col_slot * F), (1, NODES, F))[0]

    mine = padded(
        jnp.stack([block(x_shared, x_shared), block(y_shared, x_shared), block(y_shared, y_shared)])
    )
    beside_x, other_pair, across = (
        lax.ppermute(mine, "box", [(source, source ^ mask) for source in range(4)])
        for mask in (1, 2, 3)
    )
    squares = jnp.stack([mine[0] + beside_x[0], other_pair[0] + across[0]])
    wide = [(0, 0), (0, 512 - F)]
    shifted = [(0, 0), (512 - F, 0)]
    links = jnp.stack(
        [jnp.pad(part[1], wide) for part in (mine, beside_x, other_pair, across)]
        + [
            jnp.pad(mine[2] + other_pair[2], wide),
            jnp.pad(beside_x[2] + across[2], shifted),
        ]
    )
    squares_own = to_plane(squares)
    squares_other = other_half(squares_own, "core")
    links_own = to_plane(links)
    links_other = other_half(links_own, "core")

    source_box = tile_id // 16
    pair_slot = (source_box // 2) ^ along_y
    side_slot = (source_box % 2) ^ along_x
    places = jnp.stack([tile_id // 32, tile_id % 2, pair_slot]).astype(jnp.int32)

    shared_rows = jnp.stack(
        [
            jnp.concatenate([block(row_slot, col_slot) for col_slot in finals], 1)
            for row_slot in (x_shared, y_shared)
        ]
    )
    columns = lax.all_gather(padded(shared_rows), "tile", axis=0, tiled=False)

    chunks = jnp.stack(
        [
            jnp.stack(
                [
                    jnp.concatenate(
                        [block(row, x_shared), block(row, y_shared), block(row, col)], 1
                    )
                    for col in finals
                ]
            )
            for row in finals
        ]
    ).reshape(16, NODES, 3 * F)
    received = lax.all_to_all(
        padded(chunks),
        "tile",
        split_axis=0,
        concat_axis=0,
        tiled=True,
        axis_index_groups=QUARTERS,
    )
    spread = [
        (64 * box + 16 * quarter + 4 * face + goal, 64 * goal + 16 * box + 4 * face + quarter)
        for box in range(4)
        for quarter in range(4)
        for face in range(4)
        for goal in range(4)
    ]
    row_parts = lax.ppermute(received[:, :, : 2 * F], ("box", "tile"), spread)
    own_parts = []
    for goal in range(4):
        pairs = [
            (64 * box + 16 * quarter + 4 * face + goal, 64 * box + 16 * box + 4 * face + quarter)
            for box in range(4)
            for quarter in range(4)
            for face in range(4)
        ]
        own_parts.append(lax.ppermute(received[:, :, 2 * F :], ("box", "tile"), pairs))
    own_rows = jnp.concatenate(own_parts, 2)
    coupled = row_parts[:, :, :F]
    direct = row_parts[:, :, F:]
    nothing = jnp.zeros_like(direct)
    direct = jnp.where(
        side_slot == 0,
        jnp.concatenate([direct, nothing], 2),
        jnp.concatenate([nothing, direct], 2),
    )

    params = pltpu.CompilerParams(vmem_limit_bytes=VMEM_BYTES)
    smem = pl.BlockSpec(memory_space=pltpu.SMEM)
    vmem = pl.BlockSpec(memory_space=pltpu.VMEM)
    inverse = pl.pallas_call(
        pair_kernel,
        out_shape=jax.ShapeDtypeStruct((2, F, F), jnp.float32),
        in_specs=[smem, vmem, vmem],
        out_specs=vmem,
        scratch_shapes=[
            pltpu.VMEM((2, 512, 512), jnp.float32),
            pltpu.VMEM((2, LANES, 512), jnp.float32),
        ],
        compiler_params=params,
        cost_estimate=pl.CostEstimate(
            flops=20 * 10**9, bytes_accessed=4 * 10**6, transcendentals=0
        ),
        name="invert_pairs",
    )(places, squares_own, squares_other)
    first, second = pl.pallas_call(
        merge_kernel,
        out_shape=[jax.ShapeDtypeStruct((LANES, F), jnp.float32)] * 2,
        in_specs=[smem] + [vmem] * 5,
        out_specs=[vmem] * 2,
        scratch_shapes=[
            pltpu.VMEM((2, 2 * F, F), jnp.float32),
            pltpu.VMEM((2, 2 * F, F), jnp.float32),
            pltpu.VMEM((2 * F + LANES, 2 * F), jnp.float32),
            pltpu.VMEM((LANES, 2 * F), jnp.float32),
        ],
        compiler_params=params,
        cost_estimate=pl.CostEstimate(
            flops=40 * 10**9, bytes_accessed=10 * 10**6, transcendentals=0
        ),
        name="merge_pairs",
    )(places, links_own, links_other, inverse, coupled, direct)
    return pl.pallas_call(
        output_kernel,
        out_shape=jax.ShapeDtypeStruct((112, 4 * F), jnp.float32),
        grid=(7,),
        in_specs=[
            pl.BlockSpec((LANES, F), lambda i: (0, 0)),
            pl.BlockSpec((LANES, F), lambda i: (0, 0)),
            pl.BlockSpec((64, 2, 8, 256), lambda i: (0, 0, 0, i)),
            pl.BlockSpec((16, 8, 256), lambda i: (0, 0, i)),
        ],
        out_specs=pl.BlockSpec((112, 256), lambda i: (0, i)),
        compiler_params=params,
        cost_estimate=pl.CostEstimate(
            flops=4 * 10**9, bytes_accessed=9 * 10**6, transcendentals=0
        ),
        name="final_map",
    )(first, second, columns, own_rows)


def solution(mesh):
    return jax.shard_map(
        per_device,
        mesh=mesh,
        in_specs=(P("box", None, "tile", None), P()),
        out_specs=P("tile", "box"),
        check_vma=False,
    )
```

```python
import functools

import jax
import jax.numpy as jnp
from jax import lax
from jax.experimental import pallas as pl
from jax.experimental.pallas import tpu as pltpu
from jax.sharding import PartitionSpec as P

F = 448
NODES = 7
LANES = 128
MICRO = 16
VMEM_BYTES = 56 * 1024 * 1024


def tile_of(z, y, x, core):
    return ((z * 4 + y) * 4 + x) * 2 + core


PLANES = [
    [tile_of(z, y, x, core) for y in range(4) for x in range(4)]
    for z in range(2)
    for core in range(2)
]
QUARTERS = [[16 * quarter + own for own in range(16)] for quarter in range(4)]


def matmul(left, right):
    return jnp.dot(left, right, precision=lax.Precision.HIGHEST, preferred_element_type=jnp.float32)


def halves(value):
    high = value.astype(jnp.bfloat16)
    return high, (value - high.astype(jnp.float32)).astype(jnp.bfloat16)


def left_parts(value):
    high, low = halves(value)
    return jnp.concatenate([high, high, low], 1)


def right_parts(value, dim=0):
    high, low = halves(value)
    return jnp.concatenate([high, low, high], dim)


def split_matmul(left, right):
    return jnp.dot(left, right, preferred_element_type=jnp.float32)


def split_matmul_nt(left, right):
    return lax.dot_general(
        left, right, (((1,), (1,)), ((), ())), preferred_element_type=jnp.float32
    )


def invert(stack):
    full = (8, LANES)
    lane = lax.broadcasted_iota(jnp.int32, full, 1)
    sub = lax.broadcasted_iota(jnp.int32, full, 0)

    def along_rows(value, row):
        return jnp.broadcast_to(value[row : row + 1, :], full)

    def along_lanes(value, column):
        return jnp.broadcast_to(value[:, column : column + 1], full)

    stack = [list(rows) for rows in stack]
    count = len(stack[0])
    which = range(len(stack))
    for start in range(0, 8 * count, MICRO):
        first = start // 8
        inside = (lane >= start) & (lane < start + MICRO)
        following = [group for group in (first + 2, first + 3) if group < count]
        rest = [g for g in range(count) if g not in (first, first + 1, *following)]
        pivots = [
            [[along_lanes(stack[n][first + h], start + k) for h in range(2)] for k in range(MICRO)]
            for n in which
        ]
        rows = [
            [
                jnp.where(
                    inside,
                    jnp.where(lane == start + 8 * h + sub, 1.0, 0.0),
                    stack[n][first + h],
                )
                for h in range(2)
            ]
            for n in which
        ]
        ahead = [
            [[along_lanes(stack[n][group], start + k) for k in range(MICRO)] for group in following]
            for n in which
        ]
        for j in range(MICRO):
            half, row = divmod(j, 8)
            chosen = sub == row
            for n in which:
                scale = 1.0 / along_rows(pivots[n][j][half], row)
                pivot_row = along_rows(rows[n][half], row) * scale
                for k in range(j + 1, MICRO):
                    scaled = along_rows(pivots[n][k][half], row) * scale
                    for h in range(2):
                        value = pivots[n][k][h] - pivots[n][j][h] * scaled
                        pivots[n][k][h] = jnp.where(chosen, scaled, value) if h == half else value
                for h in range(2):
                    value = rows[n][h] - pivots[n][j][h] * pivot_row
                    rows[n][h] = jnp.where(chosen, pivot_row, value) if h == half else value
        for n in which:
            spread = [along_rows(rows[n][k // 8], k % 8) for k in range(MICRO)]
            for position, group in enumerate(following):
                terms = [ahead[n][position][k] * spread[k] for k in range(MICRO)]
                while len(terms) > 1:
                    terms = [terms[i] + terms[i + 1] for i in range(0, len(terms), 2)]
                stack[n][group] = jnp.where(inside, 0.0, stack[n][group]) - terms[0]
            if rest:
                zero = jnp.zeros(full, jnp.float32)
                held = jnp.concatenate([stack[n][group] for group in rest], 0)
                panel = jnp.concatenate(
                    [zero] * first + rows[n] + [zero] * (LANES // 8 - first - 2), 0
                )
                update = matmul(held, panel)
                for i, group in enumerate(rest):
                    stack[n][group] = (
                        jnp.where(inside, 0.0, stack[n][group]) - update[8 * i : 8 * i + 8]
                    )
            stack[n][first], stack[n][first + 1] = rows[n]
    return stack


def groups_of(value):
    return [value[8 * g : 8 * g + 8, :] for g in range(value.shape[0] // 8)]


def node_orders():
    tile = lax.axis_index("tile")
    core = tile % 2
    shape = (F, 256)
    target = lax.broadcasted_iota(jnp.int32, shape, 0)
    source = lax.broadcasted_iota(jnp.int32, shape, 1)
    inner = source % 8
    half = (source // 8) % 2
    half = jnp.where(tile >= 32, 1 - half, half)
    orders = []
    for held_core in (core, 1 - core):
        node = NODES * ((half * 16 + source // 16) * 2 + held_core) + inner
        hit = (node == target) & (inner < NODES)
        orders.append(jnp.where(hit, 1.0, 0.0).astype(jnp.bfloat16))
    return orders


def in_node_order(orders, pieces):
    total = None
    for order, piece in zip(orders, pieces):
        for _ in range(3):
            part = piece.astype(jnp.bfloat16)
            piece = piece - part.astype(jnp.float32)
            term = jnp.dot(order, part, preferred_element_type=jnp.float32)
            total = term if total is None else total + term
    return total


def pair_kernel(own_ref, other_ref, inverse_ref, work, panel):
    orders = node_orders()
    for n in range(2):
        pieces = [ref[:, :, n].reshape(256, 512) for ref in (own_ref, other_ref)]
        work[n, :F, :] = in_node_order(orders, pieces)
        work[n, F:, :] = jnp.zeros((512 - F, 512), jnp.float32)

    def eliminate(block, height):
        at = pl.ds(pl.multiple_of(block * LANES, LANES), LANES)
        squares = [groups_of(work[n, at, at])[: height // 8] for n in range(2)]
        inverses = invert(squares)
        for n in range(2):
            square = jnp.concatenate(inverses[n], 0)
            if height < LANES:
                square = jnp.concatenate(
                    [square, jnp.zeros((LANES - height, LANES), jnp.float32)], 0
                )
            left = left_parts(work[n, :, at])
            scaled = split_matmul(left_parts(square), right_parts(work[n, at, :]))
            work[n, :, at] = jnp.zeros((512, LANES), jnp.float32)
            panel[n] = scaled
            panel[n, :, at] = square
            scaled = panel[n]
            work[n] = work[n] - split_matmul(left, right_parts(scaled))
            work[n, at, :] = scaled

    def step(block, carry):
        eliminate(block, LANES)
        return carry

    lax.fori_loop(0, 3, step, 0)
    eliminate(jnp.int32(3), F - 3 * LANES)
    inverse_ref[...] = work[:, :F, :]


def merge_kernel(
    own_ref,
    other_ref,
    inverse_ref,
    rows_ref,
    first_ref,
    second_ref,
    coupling,
    weighted,
    system,
    panel,
):
    tile = lax.axis_index("tile")
    box = lax.axis_index("box")
    source_box = tile // 16
    pair_slot = jnp.where(source_box // 2 == box // 2, 0, 1)
    side_slot = jnp.where(source_box % 2 == box % 2, 0, 1)
    orders = node_orders()

    def ordered(index):
        pieces = [ref[:, :, index].reshape(256, 512) for ref in (own_ref, other_ref)]
        return in_node_order(orders, pieces)

    for pair in range(2):
        square = right_parts(
            jnp.concatenate([inverse_ref[pair], jnp.zeros((512 - F, 512), jnp.float32)], 0)
        )
        for side in range(2):
            at = pl.ds(side * F, F)
            left = left_parts(ordered(2 * pair + side))
            coupling[pair, at, :] = left
            weighted[pair, at, :] = right_parts(split_matmul(left, square), 1)

    for half in range(2):
        at = pl.ds(half * F, F)
        total = split_matmul_nt(coupling[0, at, :], weighted[0])
        system[at, :] = -total - split_matmul_nt(coupling[1, at, :], weighted[1])
    system[:F, :512] = system[:F, :512] + ordered(4)
    system[F : 2 * F, 384:] = system[F : 2 * F, 384:] + ordered(5)
    coupled = jnp.concatenate(
        [rows_ref[:, :, :F].reshape(LANES, F), jnp.zeros((LANES, 512 - F), jnp.float32)], 1
    )
    coupled_parts = left_parts(coupled)
    system[2 * F :, :] = -split_matmul_nt(coupled_parts, weighted[pair_slot])
    direct = rows_ref[:, :, F : 2 * F].reshape(LANES, F)
    gap = jnp.zeros((LANES, 512 - F), jnp.float32)

    @pl.when(side_slot == 0)
    def _():
        system[2 * F :, :512] = system[2 * F :, :512] + jnp.concatenate([direct, gap], 1)

    @pl.when(side_slot == 1)
    def _():
        system[2 * F :, 384:] = system[2 * F :, 384:] + jnp.concatenate([gap, direct], 1)

    def eliminate(block, carry):
        at = pl.ds(pl.multiple_of(block * LANES, LANES), LANES)
        square = jnp.concatenate(invert([groups_of(system[at, at])])[0], 0)
        scaled = split_matmul(left_parts(square), right_parts(system[at, :]))
        high, low = halves(scaled)
        panel[:LANES] = high
        panel[LANES : 2 * LANES] = low
        high, low = halves(-square)
        panel[:LANES, at] = high
        panel[LANES : 2 * LANES, at] = low
        panel[2 * LANES :] = panel[:LANES]

        def update(start, count):
            rows = pl.ds(pl.multiple_of(start * LANES, LANES), count * LANES)
            left = left_parts(system[rows, at])
            system[rows, at] = jnp.zeros((count * LANES, LANES), jnp.float32)
            system[rows, :] = system[rows, :] - split_matmul(left, panel[...])

        def pairwise(index, inner):
            update(6 - 2 * index, 2)
            return inner

        lax.fori_loop(0, (7 - block) // 2, pairwise, 0)

        @pl.when((7 - block) % 2 == 1)
        def _():
            update(block + 1, 1)

        return carry

    lax.fori_loop(0, 7, eliminate, 0)
    solved = system[2 * F :, :]
    same_pair = jnp.where(pair_slot == 0, 1.0, 0.0)
    square = right_parts(
        jnp.concatenate([inverse_ref[0], jnp.zeros((512 - F, 512), jnp.float32)], 0)
    )
    high = weighted[0, :, :512]
    low = weighted[0, :, 512:1024]
    first = same_pair * split_matmul(coupled_parts, square)
    first = first - split_matmul(left_parts(solved), jnp.concatenate([high, low, high], 0))
    first_ref[...] = first[:, :F]
    second_ref[...] = solved[:, :F]


def output_kernel(first_ref, second_ref, own_ref, other_ref, rows_ref, out_ref, spread):
    @pl.when(pl.program_id(0) == 0)
    def _():
        target = lax.broadcasted_iota(jnp.int32, (112, LANES), 0)
        source = lax.broadcasted_iota(jnp.int32, (112, LANES), 1)
        hit = (NODES * (source // 8) + source % 8 == target) & (source % 8 < NODES)
        compact = jnp.where(hit, 1.0, 0.0)
        orders = node_orders()
        for index, ref in enumerate((first_ref, second_ref)):
            high, low = halves(matmul(compact, ref[...]))
            for place, order in enumerate(orders):
                for part, value in enumerate((high, high, low)):
                    moved = jnp.dot(value, order, preferred_element_type=jnp.float32)
                    spread[index, place, part] = moved.astype(jnp.bfloat16)

    target = lax.broadcasted_iota(jnp.int32, (112, LANES), 0)
    source = lax.broadcasted_iota(jnp.int32, (112, LANES), 1)
    hit = (NODES * (source // 8) + source % 8 == target) & (source % 8 < NODES)
    compact = jnp.where(hit, 1.0, 0.0)
    total = matmul(compact, rows_ref[...].reshape(LANES, -1))
    lefts = []
    rights = []
    for index in range(2):
        for place, ref in enumerate((own_ref, other_ref)):
            lefts += [spread[index, place, part] for part in range(3)]
            rights.append(right_parts(ref[:, :, index].reshape(256, -1)))
    total = total - split_matmul(jnp.concatenate(lefts, 1), jnp.concatenate(rights, 0))
    out_ref[...] = total


def select_kernel(slots_ref, stored_ref, mine_ref, shared_ref, rows_ref):
    box = lax.axis_index("box")
    along_x = box % 2
    along_y = box // 2
    x_shared = slots_ref[box, 1 - along_x]
    y_shared = slots_ref[box, 3 - along_y]
    finals = [
        slots_ref[box, along_x],
        slots_ref[box, 2 + along_y],
        slots_ref[box, 4],
        slots_ref[box, 5],
    ]
    lane = lax.broadcasted_iota(jnp.int32, (8, 512), 1)

    def block(row_slot, col_slot):
        start = pl.multiple_of(((col_slot * 7) // 2) * LANES, LANES)
        value = stored_ref[row_slot, :, pl.ds(start, 512)]
        value = jnp.concatenate([value, jnp.zeros((1, 512), jnp.float32)], 0)
        value = jnp.where(col_slot % 2 == 1, pltpu.roll(value, F, 1), value)
        return jnp.where(lane < F, value, 0.0)

    mine_ref[0] = block(x_shared, x_shared)
    mine_ref[1] = block(y_shared, x_shared)
    mine_ref[2] = block(y_shared, y_shared)
    for index, row_slot in enumerate((x_shared, y_shared)):
        for place, col_slot in enumerate(finals):
            shared_ref[index, :, place * F : place * F + F] = block(row_slot, col_slot)[:, :F]
    for index, row_slot in enumerate(finals):
        for place, col_slot in enumerate((x_shared, y_shared, *finals)):
            rows_ref[index, :, place * F : place * F + F] = block(row_slot, col_slot)[:, :F]


def combine_kernel(mine_ref, beside_ref, other_ref, across_ref, out_ref):
    out_ref[0] = mine_ref[0] + beside_ref[0]
    out_ref[1] = other_ref[0] + across_ref[0]
    for index, ref in enumerate((mine_ref, beside_ref, other_ref, across_ref)):
        out_ref[2 + index] = ref[1]
    out_ref[6] = mine_ref[2] + other_ref[2]
    out_ref[7] = pltpu.roll(beside_ref[2] + across_ref[2], 512 - F, 1)


def other_half(value, axis_part):
    flip = 32 if axis_part == "z" else 1
    return lax.ppermute(value, "tile", [(tile, tile ^ flip) for tile in range(64)])


def to_plane(value):
    copies = jnp.broadcast_to(value, (16, *value.shape))
    return lax.all_to_all(
        copies, "tile", split_axis=0, concat_axis=0, tiled=True, axis_index_groups=PLANES
    )


def kernel_call(body, out_shapes, name, micros, **options):
    return pl.pallas_call(
        body,
        out_shape=[jax.ShapeDtypeStruct(shape, jnp.float32) for shape in out_shapes],
        compiler_params=pltpu.CompilerParams(vmem_limit_bytes=VMEM_BYTES),
        cost_estimate=pl.CostEstimate(
            flops=micros * 10**9, bytes_accessed=10**6, transcendentals=0
        ),
        name=name,
        **options,
    )


def per_device(box_maps, face_slots):
    smem = pl.BlockSpec(memory_space=pltpu.SMEM)
    vmem = pl.BlockSpec(memory_space=pltpu.VMEM)
    mine, shared_rows, outer_rows = kernel_call(
        select_kernel,
        [(3, 8, 512), (2, 8, 4 * F), (4, 8, 6 * F)],
        "select_rows",
        2,
        in_specs=[smem, vmem],
        out_specs=[vmem] * 3,
    )(face_slots, box_maps[0])
    parts = [
        lax.ppermute(mine, "box", [(source, source ^ mask) for source in range(4)])
        for mask in (1, 2, 3)
    ]
    (raw,) = kernel_call(
        combine_kernel, [(8, 8, 512)], "combine_boxes", 1, in_specs=[vmem] * 4, out_specs=[vmem]
    )(mine, *parts)
    raw = jnp.stack([raw, other_half(raw, "z")])
    squares_own = to_plane(raw[:, :2])
    squares_other = other_half(squares_own, "core")
    links_own = to_plane(raw[:, 2:])

    goals = jnp.broadcast_to(outer_rows[:, None], (4, 4, 8, 6 * F)).reshape(16, 8, 6 * F)
    received = lax.all_to_all(
        goals, "tile", split_axis=0, concat_axis=0, tiled=True, axis_index_groups=QUARTERS
    )
    spread = [
        (64 * box + 16 * quarter + 4 * face + goal, 64 * goal + 16 * box + 4 * face + quarter)
        for box in range(4)
        for quarter in range(4)
        for face in range(4)
        for goal in range(4)
    ]
    row_parts = lax.ppermute(received[:, :, : 2 * F], ("box", "tile"), spread)
    own_rows = lax.ppermute(
        received[:, :, 2 * F :],
        ("box", "tile"),
        [pair for pair in spread if pair[0] // 64 == pair[1] // 64],
    )
    columns_own = to_plane(jnp.stack([shared_rows, other_half(shared_rows, "z")]))

    (inverse,) = kernel_call(
        pair_kernel,
        [(2, F, 512)],
        "invert_pairs",
        20,
        in_specs=[vmem] * 2,
        out_specs=[vmem],
        scratch_shapes=[
            pltpu.VMEM((2, 512, 512), jnp.float32),
            pltpu.VMEM((2, LANES, 512), jnp.float32),
        ],
    )(squares_own, squares_other)
    inverse, links_own = lax.optimization_barrier((inverse, links_own))
    links_other = other_half(links_own, "core")
    columns_other = other_half(columns_own, "core")
    first, second = kernel_call(
        merge_kernel,
        [(LANES, F)] * 2,
        "merge_pairs",
        45,
        in_specs=[vmem] * 4,
        out_specs=[vmem] * 2,
        scratch_shapes=[
            pltpu.VMEM((2, 2 * F, 3 * 512), jnp.bfloat16),
            pltpu.VMEM((2, 2 * F, 3 * 512), jnp.bfloat16),
            pltpu.VMEM((2 * F + LANES, 2 * F), jnp.float32),
            pltpu.VMEM((3 * LANES, 2 * F), jnp.bfloat16),
        ],
    )(links_own, links_other, inverse, row_parts)
    (out,) = kernel_call(
        output_kernel,
        [(112, 4 * F)],
        "final_map",
        6,
        grid=(7,),
        in_specs=[
            pl.BlockSpec((LANES, F), lambda i: (0, 0)),
            pl.BlockSpec((LANES, F), lambda i: (0, 0)),
            pl.BlockSpec((16, 2, 2, 8, 256), lambda i: (0, 0, 0, 0, i)),
            pl.BlockSpec((16, 2, 2, 8, 256), lambda i: (0, 0, 0, 0, i)),
            pl.BlockSpec((16, 8, 256), lambda i: (0, 0, i)),
        ],
        out_specs=[pl.BlockSpec((112, 256), lambda i: (0, i))],
        scratch_shapes=[pltpu.VMEM((2, 2, 3, 112, 256), jnp.bfloat16)],
    )(first, second, columns_own, columns_other, own_rows)
    return out


def solution(mesh):
    return jax.shard_map(
        per_device,
        mesh=mesh,
        in_specs=(P("box", None, "tile", None), P()),
        out_specs=P("tile", "box"),
        check_vma=False,
    )
```

```python
import functools

import jax
import jax.numpy as jnp
from jax import lax
from jax.experimental import pallas as pl
from jax.experimental.pallas import tpu as pltpu
from jax.sharding import PartitionSpec as P

F = 448
NODES = 7
LANES = 128
MICRO = 16
VMEM_BYTES = 56 * 1024 * 1024


def tile_of(z, y, x, core):
    return ((z * 4 + y) * 4 + x) * 2 + core


PLANES = [
    [tile_of(z, y, x, core) for y in range(4) for x in range(4)]
    for z in range(2)
    for core in range(2)
]
QUARTERS = [[16 * quarter + own for own in range(16)] for quarter in range(4)]


def matmul(left, right):
    return jnp.dot(left, right, precision=lax.Precision.HIGHEST, preferred_element_type=jnp.float32)


def halves(value):
    high = value.astype(jnp.bfloat16)
    return high, (value - high.astype(jnp.float32)).astype(jnp.bfloat16)


def left_parts(value):
    high, low = halves(value)
    return jnp.concatenate([high, high, low], 1)


def right_parts(value, dim=0):
    high, low = halves(value)
    return jnp.concatenate([high, low, high], dim)


def split_matmul(left, right):
    return jnp.dot(left, right, preferred_element_type=jnp.float32)


def split_matmul_nt(left, right):
    return lax.dot_general(
        left, right, (((1,), (1,)), ((), ())), preferred_element_type=jnp.float32
    )


def invert(stack):
    full = (8, LANES)
    lane = lax.broadcasted_iota(jnp.int32, full, 1)
    sub = lax.broadcasted_iota(jnp.int32, full, 0)

    def along_rows(value, row):
        return jnp.broadcast_to(value[row : row + 1, :], full)

    def along_lanes(value, column):
        return jnp.broadcast_to(value[:, column : column + 1], full)

    stack = [list(rows) for rows in stack]
    count = len(stack[0])
    which = range(len(stack))
    for start in range(0, 8 * count, MICRO):
        first = start // 8
        inside = (lane >= start) & (lane < start + MICRO)
        following = [group for group in (first + 2, first + 3) if group < count]
        rest = [g for g in range(count) if g not in (first, first + 1, *following)]
        pivots = [
            [[along_lanes(stack[n][first + h], start + k) for h in range(2)] for k in range(MICRO)]
            for n in which
        ]
        rows = [
            [
                jnp.where(
                    inside,
                    jnp.where(lane == start + 8 * h + sub, 1.0, 0.0),
                    stack[n][first + h],
                )
                for h in range(2)
            ]
            for n in which
        ]
        ahead = [
            [[along_lanes(stack[n][group], start + k) for k in range(MICRO)] for group in following]
            for n in which
        ]
        for j in range(MICRO):
            half, row = divmod(j, 8)
            chosen = sub == row
            for n in which:
                scale = 1.0 / along_rows(pivots[n][j][half], row)
                pivot_row = along_rows(rows[n][half], row) * scale
                for k in range(j + 1, MICRO):
                    scaled = along_rows(pivots[n][k][half], row) * scale
                    for h in range(2):
                        value = pivots[n][k][h] - pivots[n][j][h] * scaled
                        pivots[n][k][h] = jnp.where(chosen, scaled, value) if h == half else value
                for h in range(2):
                    value = rows[n][h] - pivots[n][j][h] * pivot_row
                    rows[n][h] = jnp.where(chosen, pivot_row, value) if h == half else value
        for n in which:
            spread = [along_rows(rows[n][k // 8], k % 8) for k in range(MICRO)]
            for position, group in enumerate(following):
                terms = [ahead[n][position][k] * spread[k] for k in range(MICRO)]
                while len(terms) > 1:
                    terms = [terms[i] + terms[i + 1] for i in range(0, len(terms), 2)]
                stack[n][group] = jnp.where(inside, 0.0, stack[n][group]) - terms[0]
            if rest:
                zero = jnp.zeros(full, jnp.float32)
                held = jnp.concatenate([stack[n][group] for group in rest], 0)
                panel = jnp.concatenate(
                    [zero] * first + rows[n] + [zero] * (LANES // 8 - first - 2), 0
                )
                update = matmul(held, panel)
                for i, group in enumerate(rest):
                    stack[n][group] = (
                        jnp.where(inside, 0.0, stack[n][group]) - update[8 * i : 8 * i + 8]
                    )
            stack[n][first], stack[n][first + 1] = rows[n]
    return stack


def groups_of(value):
    return [value[8 * g : 8 * g + 8, :] for g in range(value.shape[0] // 8)]


def node_orders(relative=False):
    tile = lax.axis_index("tile")
    core = tile % 2
    shape = (F, 256)
    target = lax.broadcasted_iota(jnp.int32, shape, 0)
    source = lax.broadcasted_iota(jnp.int32, shape, 1)
    inner = source % 8
    place = source // 16
    if relative:
        in_x = place // 4
        in_y = place % 4
        in_x = (tile // 2) % 4 + jnp.where(in_x == 1, 3, jnp.where(in_x == 2, 1, jnp.where(in_x == 3, 2, 0)))
        in_y = (tile // 8) % 4 + jnp.where(in_y == 1, 3, jnp.where(in_y == 2, 1, jnp.where(in_y == 3, 2, 0)))
        place = (in_y % 4) * 4 + in_x % 4
    half = (source // 8) % 2
    half = jnp.where(tile >= 32, 1 - half, half)
    orders = []
    for held_core in (core, 1 - core):
        node = NODES * ((half * 16 + place) * 2 + held_core) + inner
        hit = (node == target) & (inner < NODES)
        orders.append(jnp.where(hit, 1.0, 0.0).astype(jnp.bfloat16))
    return orders


def in_node_order(orders, pieces):
    total = None
    for order, piece in zip(orders, pieces):
        for _ in range(3):
            part = piece.astype(jnp.bfloat16)
            piece = piece - part.astype(jnp.float32)
            term = jnp.dot(order, part, preferred_element_type=jnp.float32)
            total = term if total is None else total + term
    return total


def pair_kernel(own_ref, other_ref, inverse_ref, work, panel):
    orders = node_orders()
    for n in range(2):
        pieces = [ref[:, :, n].reshape(256, 512) for ref in (own_ref, other_ref)]
        work[n, :F, :] = in_node_order(orders, pieces)
        work[n, F:, :] = jnp.zeros((512 - F, 512), jnp.float32)

    def eliminate(block, height):
        at = pl.ds(pl.multiple_of(block * LANES, LANES), LANES)
        squares = [groups_of(work[n, at, at])[: height // 8] for n in range(2)]
        inverses = invert(squares)
        for n in range(2):
            square = jnp.concatenate(inverses[n], 0)
            if height < LANES:
                square = jnp.concatenate(
                    [square, jnp.zeros((LANES - height, LANES), jnp.float32)], 0
                )
            left = left_parts(work[n, :, at])
            scaled = split_matmul(left_parts(square), right_parts(work[n, at, :]))
            work[n, :, at] = jnp.zeros((512, LANES), jnp.float32)
            panel[n] = scaled
            panel[n, :, at] = square
            scaled = panel[n]
            work[n] = work[n] - split_matmul(left, right_parts(scaled))
            work[n, at, :] = scaled

    def step(block, carry):
        eliminate(block, LANES)
        return carry

    lax.fori_loop(0, 3, step, 0)
    eliminate(jnp.int32(3), F - 3 * LANES)
    inverse_ref[...] = work[:, :F, :]


def merge_kernel(
    own_ref,
    other_ref,
    inverse_ref,
    rows_ref,
    first_ref,
    second_ref,
    coupling,
    weighted,
    system,
    panel,
):
    tile = lax.axis_index("tile")
    box = lax.axis_index("box")
    source_box = tile // 16
    pair_slot = jnp.where(source_box // 2 == box // 2, 0, 1)
    side_slot = jnp.where(source_box % 2 == box % 2, 0, 1)
    orders = node_orders()

    def ordered(index):
        pieces = [ref[:, :, index].reshape(256, 512) for ref in (own_ref, other_ref)]
        return in_node_order(orders, pieces)

    for pair in range(2):
        square = right_parts(
            jnp.concatenate([inverse_ref[pair], jnp.zeros((512 - F, 512), jnp.float32)], 0)
        )
        for side in range(2):
            at = pl.ds(side * F, F)
            left = left_parts(ordered(2 * pair + side))
            coupling[pair, at, :] = left
            weighted[pair, at, :] = right_parts(split_matmul(left, square), 1)

    for half in range(2):
        at = pl.ds(half * F, F)
        total = split_matmul_nt(coupling[0, at, :], weighted[0])
        system[at, :] = -total - split_matmul_nt(coupling[1, at, :], weighted[1])
    system[:F, :512] = system[:F, :512] + ordered(4)
    system[F : 2 * F, 384:] = system[F : 2 * F, 384:] + ordered(5)
    coupled = jnp.concatenate(
        [rows_ref[:, :, :F].reshape(LANES, F), jnp.zeros((LANES, 512 - F), jnp.float32)], 1
    )
    coupled_parts = left_parts(coupled)
    system[2 * F :, :] = -split_matmul_nt(coupled_parts, weighted[pair_slot])
    direct = rows_ref[:, :, F : 2 * F].reshape(LANES, F)
    gap = jnp.zeros((LANES, 512 - F), jnp.float32)

    @pl.when(side_slot == 0)
    def _():
        system[2 * F :, :512] = system[2 * F :, :512] + jnp.concatenate([direct, gap], 1)

    @pl.when(side_slot == 1)
    def _():
        system[2 * F :, 384:] = system[2 * F :, 384:] + jnp.concatenate([gap, direct], 1)

    def eliminate(block, carry):
        at = pl.ds(pl.multiple_of(block * LANES, LANES), LANES)
        square = jnp.concatenate(invert([groups_of(system[at, at])])[0], 0)
        scaled = split_matmul(left_parts(square), right_parts(system[at, :]))
        high, low = halves(scaled)
        panel[:LANES] = high
        panel[LANES : 2 * LANES] = low
        high, low = halves(-square)
        panel[:LANES, at] = high
        panel[LANES : 2 * LANES, at] = low
        panel[2 * LANES :] = panel[:LANES]

        def update(start, count):
            rows = pl.ds(pl.multiple_of(start * LANES, LANES), count * LANES)
            left = left_parts(system[rows, at])
            system[rows, at] = jnp.zeros((count * LANES, LANES), jnp.float32)
            system[rows, :] = system[rows, :] - split_matmul(left, panel[...])

        def pairwise(index, inner):
            update(6 - 2 * index, 2)
            return inner

        lax.fori_loop(0, (7 - block) // 2, pairwise, 0)

        @pl.when((7 - block) % 2 == 1)
        def _():
            update(block + 1, 1)

        return carry

    lax.fori_loop(0, 7, eliminate, 0)
    solved = system[2 * F :, :]
    same_pair = jnp.where(pair_slot == 0, 1.0, 0.0)
    square = right_parts(
        jnp.concatenate([inverse_ref[0], jnp.zeros((512 - F, 512), jnp.float32)], 0)
    )
    high = weighted[0, :, :512]
    low = weighted[0, :, 512:1024]
    first = same_pair * split_matmul(coupled_parts, square)
    first = first - split_matmul(left_parts(solved), jnp.concatenate([high, low, high], 0))
    first_ref[...] = first[:, :F]
    second_ref[...] = solved[:, :F]


def output_kernel(first_ref, second_ref, own_ref, other_ref, rows_ref, out_ref, spread):
    @pl.when(pl.program_id(0) == 0)
    def _():
        target = lax.broadcasted_iota(jnp.int32, (112, LANES), 0)
        source = lax.broadcasted_iota(jnp.int32, (112, LANES), 1)
        hit = (NODES * (source // 8) + source % 8 == target) & (source % 8 < NODES)
        compact = jnp.where(hit, 1.0, 0.0)
        orders = node_orders(relative=True)
        for index, ref in enumerate((first_ref, second_ref)):
            high, low = halves(matmul(compact, ref[...]))
            for place, order in enumerate(orders):
                for part, value in enumerate((high, high, low)):
                    moved = jnp.dot(value, order, preferred_element_type=jnp.float32)
                    spread[index, place, part] = moved.astype(jnp.bfloat16)

    target = lax.broadcasted_iota(jnp.int32, (112, LANES), 0)
    source = lax.broadcasted_iota(jnp.int32, (112, LANES), 1)
    hit = (NODES * (source // 8) + source % 8 == target) & (source % 8 < NODES)
    compact = jnp.where(hit, 1.0, 0.0)
    total = matmul(compact, rows_ref[...].reshape(LANES, -1))
    lefts = []
    rights = []
    for index in range(2):
        for place, ref in enumerate((own_ref, other_ref)):
            lefts += [spread[index, place, part] for part in range(3)]
            rights.append(right_parts(ref[:, :, index].reshape(256, -1)))
    total = total - split_matmul(jnp.concatenate(lefts, 1), jnp.concatenate(rights, 0))
    out_ref[...] = total


def select_kernel(slots_ref, stored_ref, mine_ref, shared_ref, goals_ref):
    box = lax.axis_index("box")
    along_x = box % 2
    along_y = box // 2
    x_shared = slots_ref[box, 1 - along_x]
    y_shared = slots_ref[box, 3 - along_y]
    finals = [
        slots_ref[box, along_x],
        slots_ref[box, 2 + along_y],
        slots_ref[box, 4],
        slots_ref[box, 5],
    ]
    lane = lax.broadcasted_iota(jnp.int32, (8, 512), 1)

    def block(row_slot, col_slot):
        start = pl.multiple_of(((col_slot * 7) // 2) * LANES, LANES)
        value = stored_ref[row_slot, :, pl.ds(start, 512)]
        value = jnp.concatenate([value, jnp.zeros((1, 512), jnp.float32)], 0)
        value = jnp.where(col_slot % 2 == 1, pltpu.roll(value, F, 1), value)
        return jnp.where(lane < F, value, 0.0)

    mine_ref[0] = block(x_shared, x_shared)
    mine_ref[1] = block(y_shared, x_shared)
    mine_ref[2] = block(y_shared, y_shared)
    for index, row_slot in enumerate((x_shared, y_shared)):
        for place, col_slot in enumerate(finals):
            shared_ref[index, :, place * F : place * F + F] = block(row_slot, col_slot)[:, :F]
    for index, row_slot in enumerate(finals):
        for place, col_slot in enumerate((x_shared, y_shared)):
            value = block(row_slot, col_slot)[:, :F]
            for goal in range(4):
                goals_ref[4 * index + goal, :, place * F : place * F + F] = value
        for goal, col_slot in enumerate(finals):
            goals_ref[4 * index + goal, :, 2 * F :] = block(row_slot, col_slot)[:, :F]


def combine_kernel(mine_ref, beside_ref, other_ref, across_ref, out_ref):
    out_ref[0] = mine_ref[0] + beside_ref[0]
    out_ref[1] = other_ref[0] + across_ref[0]
    for index, ref in enumerate((mine_ref, beside_ref, other_ref, across_ref)):
        out_ref[2 + index] = ref[1]
    out_ref[6] = mine_ref[2] + other_ref[2]
    out_ref[7] = pltpu.roll(beside_ref[2] + across_ref[2], 512 - F, 1)


def other_half(value, axis_part):
    flip = 32 if axis_part == "z" else 1
    return lax.ppermute(value, "tile", [(tile, tile ^ flip) for tile in range(64)])


def to_plane(value):
    copies = jnp.broadcast_to(value, (16, *value.shape))
    return lax.all_to_all(
        copies, "tile", split_axis=0, concat_axis=0, tiled=True, axis_index_groups=PLANES
    )


def ring_shift(value, axis_part, step):
    unit, length = {"x": (2, 4), "y": (8, 4)}[axis_part]
    pairs = []
    for tile in range(64):
        place = (tile // unit) % length
        pairs.append((tile, tile + ((place + step) % length - place) * unit))
    return lax.ppermute(value, "tile", pairs)


def ring_near(value, axis_part):
    return ring_shift(value, axis_part, 1), ring_shift(value, axis_part, -1)


def ring_far(before, after, axis_part):
    return (
        ring_shift(before[..., 0, :, :], axis_part, 1),
        ring_shift(after[..., 1, :, :], axis_part, -1),
    )


def ring_stack(own, before, after, far):
    return jnp.stack([own, before, after, jnp.stack(far, -3)])


def kernel_call(body, out_shapes, name, micros, **options):
    return pl.pallas_call(
        body,
        out_shape=[jax.ShapeDtypeStruct(shape, jnp.float32) for shape in out_shapes],
        compiler_params=pltpu.CompilerParams(vmem_limit_bytes=VMEM_BYTES),
        cost_estimate=pl.CostEstimate(
            flops=micros * 10**9, bytes_accessed=10**6, transcendentals=0
        ),
        name=name,
        **options,
    )


def per_device(box_maps, face_slots):
    smem = pl.BlockSpec(memory_space=pltpu.SMEM)
    vmem = pl.BlockSpec(memory_space=pltpu.VMEM)
    mine, shared_rows, goals = kernel_call(
        select_kernel,
        [(3, 8, 512), (2, 8, 4 * F), (16, 8, 3 * F)],
        "select_rows",
        2,
        in_specs=[smem, vmem],
        out_specs=[vmem] * 3,
    )(face_slots, box_maps[0])
    spread = [
        (64 * box + 16 * quarter + 4 * face + goal, 64 * goal + 16 * box + 4 * face + quarter)
        for box in range(4)
        for quarter in range(4)
        for face in range(4)
        for goal in range(4)
    ]

    parts = [
        lax.ppermute(mine, "box", [(source, source ^ mask) for source in range(4)])
        for mask in (1, 2, 3)
    ]
    shared_far = other_half(shared_rows, "z")
    row_goals = lax.all_to_all(
        goals, "tile", split_axis=0, concat_axis=0, tiled=True, axis_index_groups=QUARTERS
    )
    parts, shared_far, row_goals = lax.optimization_barrier((parts, shared_far, row_goals))

    (raw,) = kernel_call(
        combine_kernel, [(8, 8, 512)], "combine_boxes", 1, in_specs=[vmem] * 4, out_specs=[vmem]
    )(mine, *parts)
    raw_far = other_half(raw, "z")
    columns = jnp.stack([shared_rows, shared_far])
    near = ring_near(columns, "y")
    raw_far, near = lax.optimization_barrier((raw_far, near))

    raw = jnp.stack([raw, raw_far])
    row_parts = lax.ppermute(row_goals[:, :, : 2 * F], ("box", "tile"), spread)
    far = ring_far(*near, "y")
    squares_own = to_plane(raw[:, :2])
    squares_own, far = lax.optimization_barrier((squares_own, far))

    columns = ring_stack(columns, *near, far)
    squares_other = other_half(squares_own, "core")
    links_own = to_plane(raw[:, 2:])
    near = ring_near(columns, "x")
    squares_other, near = lax.optimization_barrier((squares_other, near))

    far = ring_far(*near, "x")

    (inverse,) = kernel_call(
        pair_kernel,
        [(2, F, 512)],
        "invert_pairs",
        20,
        in_specs=[vmem] * 2,
        out_specs=[vmem],
        scratch_shapes=[
            pltpu.VMEM((2, 512, 512), jnp.float32),
            pltpu.VMEM((2, LANES, 512), jnp.float32),
        ],
    )(squares_own, squares_other)
    inverse, links_own, far, row_parts = lax.optimization_barrier(
        (inverse, links_own, far, row_parts)
    )
    links_other = other_half(links_own, "core")
    columns_own = ring_stack(columns, *near, far).reshape(16, 2, 2, 8, 4 * F)
    columns_other = other_half(columns_own, "core")
    own_rows = []
    for goal in range(4):
        pairs = [
            (64 * box + 16 * quarter + 4 * face + goal, 64 * box + 16 * box + 4 * face + quarter)
            for box in range(4)
            for quarter in range(4)
            for face in range(4)
        ]
        own_rows.append(lax.ppermute(row_goals[:, :, 2 * F :], ("box", "tile"), pairs))
    own_rows = jnp.concatenate(own_rows, 2)
    first, second = kernel_call(
        merge_kernel,
        [(LANES, F)] * 2,
        "merge_pairs",
        45,
        in_specs=[vmem] * 4,
        out_specs=[vmem] * 2,
        scratch_shapes=[
            pltpu.VMEM((2, 2 * F, 3 * 512), jnp.bfloat16),
            pltpu.VMEM((2, 2 * F, 3 * 512), jnp.bfloat16),
            pltpu.VMEM((2 * F + LANES, 2 * F), jnp.float32),
            pltpu.VMEM((3 * LANES, 2 * F), jnp.bfloat16),
        ],
    )(links_own, links_other, inverse, row_parts)
    (out,) = kernel_call(
        output_kernel,
        [(112, 4 * F)],
        "final_map",
        6,
        grid=(7,),
        in_specs=[
            pl.BlockSpec((LANES, F), lambda i: (0, 0)),
            pl.BlockSpec((LANES, F), lambda i: (0, 0)),
            pl.BlockSpec((16, 2, 2, 8, 256), lambda i: (0, 0, 0, 0, i)),
            pl.BlockSpec((16, 2, 2, 8, 256), lambda i: (0, 0, 0, 0, i)),
            pl.BlockSpec((16, 8, 256), lambda i: (0, 0, i)),
        ],
        out_specs=[pl.BlockSpec((112, 256), lambda i: (0, i))],
        scratch_shapes=[pltpu.VMEM((2, 2, 3, 112, 256), jnp.bfloat16)],
    )(first, second, columns_own, columns_other, own_rows)
    return out


def solution(mesh):
    return jax.shard_map(
        per_device,
        mesh=mesh,
        in_specs=(P("box", None, "tile", None), P()),
        out_specs=P("tile", "box"),
        check_vma=False,
    )
```

```python
import functools

import jax
import jax.numpy as jnp
from jax import lax
from jax.experimental import pallas as pl
from jax.experimental.pallas import tpu as pltpu
from jax.sharding import PartitionSpec as P

F = 448
NODES = 7
LANES = 128
MICRO = 16
VMEM_BYTES = 56 * 1024 * 1024


def tile_of(z, y, x, core):
    return ((z * 4 + y) * 4 + x) * 2 + core


PLANES = [
    [tile_of(z, y, x, core) for y in range(4) for x in range(4)]
    for z in range(2)
    for core in range(2)
]
QUARTERS = [[16 * quarter + own for own in range(16)] for quarter in range(4)]


def matmul(left, right):
    return jnp.dot(left, right, precision=lax.Precision.HIGHEST, preferred_element_type=jnp.float32)


def halves(value):
    high = value.astype(jnp.bfloat16)
    return high, (value - high.astype(jnp.float32)).astype(jnp.bfloat16)


def left_parts(value):
    high, low = halves(value)
    return jnp.concatenate([high, high, low], 1)


def right_parts(value, dim=0):
    high, low = halves(value)
    return jnp.concatenate([high, low, high], dim)


def split_matmul(left, right):
    return jnp.dot(left, right, preferred_element_type=jnp.float32)


def split_matmul_nt(left, right):
    return lax.dot_general(
        left, right, (((1,), (1,)), ((), ())), preferred_element_type=jnp.float32
    )


def invert(stack):
    full = (8, LANES)
    lane = lax.broadcasted_iota(jnp.int32, full, 1)
    sub = lax.broadcasted_iota(jnp.int32, full, 0)

    def along_rows(value, row):
        return jnp.broadcast_to(value[row : row + 1, :], full)

    def along_lanes(value, column):
        return jnp.broadcast_to(value[:, column : column + 1], full)

    stack = [list(rows) for rows in stack]
    count = len(stack[0])
    which = range(len(stack))
    for start in range(0, 8 * count, MICRO):
        first = start // 8
        inside = (lane >= start) & (lane < start + MICRO)
        following = [group for group in (first + 2, first + 3) if group < count]
        rest = [g for g in range(count) if g not in (first, first + 1, *following)]
        pivots = [
            [[along_lanes(stack[n][first + h], start + k) for h in range(2)] for k in range(MICRO)]
            for n in which
        ]
        rows = [
            [
                jnp.where(
                    inside,
                    jnp.where(lane == start + 8 * h + sub, 1.0, 0.0),
                    stack[n][first + h],
                )
                for h in range(2)
            ]
            for n in which
        ]
        ahead = [
            [[along_lanes(stack[n][group], start + k) for k in range(MICRO)] for group in following]
            for n in which
        ]
        for j in range(MICRO):
            half, row = divmod(j, 8)
            chosen = sub == row
            for n in which:
                scale = 1.0 / along_rows(pivots[n][j][half], row)
                pivot_row = along_rows(rows[n][half], row) * scale
                for k in range(j + 1, MICRO):
                    scaled = along_rows(pivots[n][k][half], row) * scale
                    for h in range(2):
                        value = pivots[n][k][h] - pivots[n][j][h] * scaled
                        pivots[n][k][h] = jnp.where(chosen, scaled, value) if h == half else value
                for h in range(2):
                    value = rows[n][h] - pivots[n][j][h] * pivot_row
                    rows[n][h] = jnp.where(chosen, pivot_row, value) if h == half else value
        for n in which:
            spread = [along_rows(rows[n][k // 8], k % 8) for k in range(MICRO)]
            for position, group in enumerate(following):
                terms = [ahead[n][position][k] * spread[k] for k in range(MICRO)]
                while len(terms) > 1:
                    terms = [terms[i] + terms[i + 1] for i in range(0, len(terms), 2)]
                stack[n][group] = jnp.where(inside, 0.0, stack[n][group]) - terms[0]
            if rest:
                zero = jnp.zeros(full, jnp.float32)
                held = jnp.concatenate([stack[n][group] for group in rest], 0)
                panel = jnp.concatenate(
                    [zero] * first + rows[n] + [zero] * (LANES // 8 - first - 2), 0
                )
                update = matmul(held, panel)
                for i, group in enumerate(rest):
                    stack[n][group] = (
                        jnp.where(inside, 0.0, stack[n][group]) - update[8 * i : 8 * i + 8]
                    )
            stack[n][first], stack[n][first + 1] = rows[n]
    return stack


def groups_of(value):
    return [value[8 * g : 8 * g + 8, :] for g in range(value.shape[0] // 8)]


def node_orders(relative=False):
    tile = lax.axis_index("tile")
    core = tile % 2
    shape = (F, 256)
    target = lax.broadcasted_iota(jnp.int32, shape, 0)
    source = lax.broadcasted_iota(jnp.int32, shape, 1)
    inner = source % 8
    place = source // 16
    if relative:
        in_x = place // 4
        in_y = place % 4
        in_x = (tile // 2) % 4 + jnp.where(in_x == 1, 3, jnp.where(in_x == 2, 1, jnp.where(in_x == 3, 2, 0)))
        in_y = (tile // 8) % 4 + jnp.where(in_y == 1, 3, jnp.where(in_y == 2, 1, jnp.where(in_y == 3, 2, 0)))
        place = (in_y % 4) * 4 + in_x % 4
    half = (source // 8) % 2
    half = jnp.where(tile >= 32, 1 - half, half)
    orders = []
    for held_core in (core, 1 - core):
        node = NODES * ((half * 16 + place) * 2 + held_core) + inner
        hit = (node == target) & (inner < NODES)
        orders.append(jnp.where(hit, 1.0, 0.0).astype(jnp.bfloat16))
    return orders


def in_node_order(orders, pieces):
    total = None
    for order, piece in zip(orders, pieces):
        for _ in range(3):
            part = piece.astype(jnp.bfloat16)
            piece = piece - part.astype(jnp.float32)
            term = jnp.dot(order, part, preferred_element_type=jnp.float32)
            total = term if total is None else total + term
    return total


def pair_kernel(own_ref, other_ref, inverse_ref, work, panel):
    orders = node_orders()
    for n in range(2):
        pieces = [ref[:, :, n].reshape(256, 512) for ref in (own_ref, other_ref)]
        work[n, :F, :] = in_node_order(orders, pieces)
        work[n, F:, :] = jnp.zeros((512 - F, 512), jnp.float32)

    def eliminate(block, height):
        at = pl.ds(pl.multiple_of(block * LANES, LANES), LANES)
        squares = [groups_of(work[n, at, at])[: height // 8] for n in range(2)]
        inverses = invert(squares)
        for n in range(2):
            square = jnp.concatenate(inverses[n], 0)
            if height < LANES:
                square = jnp.concatenate(
                    [square, jnp.zeros((LANES - height, LANES), jnp.float32)], 0
                )
            left = left_parts(work[n, :, at])
            scaled = split_matmul(left_parts(square), right_parts(work[n, at, :]))
            work[n, :, at] = jnp.zeros((512, LANES), jnp.float32)
            panel[n] = scaled
            panel[n, :, at] = square
            scaled = panel[n]
            work[n] = work[n] - split_matmul(left, right_parts(scaled))
            work[n, at, :] = scaled

    def step(block, carry):
        eliminate(block, LANES)
        return carry

    lax.fori_loop(0, 3, step, 0)
    eliminate(jnp.int32(3), F - 3 * LANES)
    inverse_ref[...] = work[:, :F, :]


def merge_kernel(
    own_ref,
    other_ref,
    inverse_ref,
    rows_ref,
    first_ref,
    second_ref,
    coupling,
    weighted,
    system,
    panel,
):
    tile = lax.axis_index("tile")
    box = lax.axis_index("box")
    source_box = tile // 16
    pair_slot = jnp.where(source_box // 2 == box // 2, 0, 1)
    side_slot = jnp.where(source_box % 2 == box % 2, 0, 1)
    orders = node_orders()

    def ordered(index):
        pieces = [ref[:, :, index].reshape(256, 512) for ref in (own_ref, other_ref)]
        return in_node_order(orders, pieces)

    for pair in range(2):
        square = right_parts(
            jnp.concatenate([inverse_ref[pair], jnp.zeros((512 - F, 512), jnp.float32)], 0)
        )
        for side in range(2):
            at = pl.ds(side * F, F)
            left = left_parts(ordered(2 * pair + side))
            coupling[pair, at, :] = left
            weighted[pair, at, :] = right_parts(split_matmul(left, square), 1)

    for half in range(2):
        at = pl.ds(half * F, F)
        total = split_matmul_nt(coupling[0, at, :], weighted[0])
        system[at, :] = -total - split_matmul_nt(coupling[1, at, :], weighted[1])
    system[:F, :512] = system[:F, :512] + ordered(4)
    system[F : 2 * F, 384:] = system[F : 2 * F, 384:] + ordered(5)
    coupled = jnp.concatenate(
        [rows_ref[:, :, :F].reshape(LANES, F), jnp.zeros((LANES, 512 - F), jnp.float32)], 1
    )
    coupled_parts = left_parts(coupled)
    system[2 * F :, :] = -split_matmul_nt(coupled_parts, weighted[pair_slot])
    direct = rows_ref[:, :, F : 2 * F].reshape(LANES, F)
    gap = jnp.zeros((LANES, 512 - F), jnp.float32)

    @pl.when(side_slot == 0)
    def _():
        system[2 * F :, :512] = system[2 * F :, :512] + jnp.concatenate([direct, gap], 1)

    @pl.when(side_slot == 1)
    def _():
        system[2 * F :, 384:] = system[2 * F :, 384:] + jnp.concatenate([gap, direct], 1)

    def eliminate(block, carry):
        at = pl.ds(pl.multiple_of(block * LANES, LANES), LANES)
        square = jnp.concatenate(invert([groups_of(system[at, at])])[0], 0)
        scaled = split_matmul(left_parts(square), right_parts(system[at, :]))
        high, low = halves(scaled)
        panel[:LANES] = high
        panel[LANES : 2 * LANES] = low
        high, low = halves(-square)
        panel[:LANES, at] = high
        panel[LANES : 2 * LANES, at] = low
        panel[2 * LANES :] = panel[:LANES]

        def update(start, count):
            rows = pl.ds(pl.multiple_of(start * LANES, LANES), count * LANES)
            left = left_parts(system[rows, at])
            system[rows, at] = jnp.zeros((count * LANES, LANES), jnp.float32)
            system[rows, :] = system[rows, :] - split_matmul(left, panel[...])

        def pairwise(index, inner):
            update(6 - 2 * index, 2)
            return inner

        lax.fori_loop(0, (7 - block) // 2, pairwise, 0)

        @pl.when((7 - block) % 2 == 1)
        def _():
            update(block + 1, 1)

        return carry

    lax.fori_loop(0, 7, eliminate, 0)
    solved = system[2 * F :, :]
    same_pair = jnp.where(pair_slot == 0, 1.0, 0.0)
    square = right_parts(
        jnp.concatenate([inverse_ref[0], jnp.zeros((512 - F, 512), jnp.float32)], 0)
    )
    high = weighted[0, :, :512]
    low = weighted[0, :, 512:1024]
    first = same_pair * split_matmul(coupled_parts, square)
    first = first - split_matmul(left_parts(solved), jnp.concatenate([high, low, high], 0))
    first_ref[...] = first[:, :F]
    second_ref[...] = solved[:, :F]


def output_kernel(first_ref, second_ref, own_ref, other_ref, rows_ref, out_ref, spread):
    @pl.when(pl.program_id(0) == 0)
    def _():
        target = lax.broadcasted_iota(jnp.int32, (112, LANES), 0)
        source = lax.broadcasted_iota(jnp.int32, (112, LANES), 1)
        hit = (NODES * (source // 8) + source % 8 == target) & (source % 8 < NODES)
        compact = jnp.where(hit, 1.0, 0.0)
        orders = node_orders(relative=True)
        for index, ref in enumerate((first_ref, second_ref)):
            high, low = halves(matmul(compact, ref[...]))
            for place, order in enumerate(orders):
                for part, value in enumerate((high, high, low)):
                    moved = jnp.dot(value, order, preferred_element_type=jnp.float32)
                    spread[index, place, part] = moved.astype(jnp.bfloat16)

    target = lax.broadcasted_iota(jnp.int32, (112, LANES), 0)
    source = lax.broadcasted_iota(jnp.int32, (112, LANES), 1)
    hit = (NODES * (source // 8) + source % 8 == target) & (source % 8 < NODES)
    compact = jnp.where(hit, 1.0, 0.0)
    total = matmul(compact, rows_ref[...].reshape(LANES, -1))
    lefts = []
    rights = []
    for index in range(2):
        for place, ref in enumerate((own_ref, other_ref)):
            lefts += [spread[index, place, part] for part in range(3)]
            rights.append(right_parts(ref[:, :, index].reshape(256, -1)))
    total = total - split_matmul(jnp.concatenate(lefts, 1), jnp.concatenate(rights, 0))
    out_ref[...] = total


def select_kernel(slots_ref, stored_ref, mine_ref, shared_ref, goals_ref):
    box = lax.axis_index("box")
    along_x = box % 2
    along_y = box // 2
    x_shared = slots_ref[box, 1 - along_x]
    y_shared = slots_ref[box, 3 - along_y]
    finals = [
        slots_ref[box, along_x],
        slots_ref[box, 2 + along_y],
        slots_ref[box, 4],
        slots_ref[box, 5],
    ]
    lane = lax.broadcasted_iota(jnp.int32, (8, 512), 1)

    def block(row_slot, col_slot):
        start = pl.multiple_of(((col_slot * 7) // 2) * LANES, LANES)
        value = stored_ref[row_slot, :, pl.ds(start, 512)]
        value = jnp.concatenate([value, jnp.zeros((1, 512), jnp.float32)], 0)
        value = jnp.where(col_slot % 2 == 1, pltpu.roll(value, F, 1), value)
        return jnp.where(lane < F, value, 0.0)

    mine_ref[0] = block(x_shared, x_shared)
    mine_ref[1] = block(y_shared, x_shared)
    mine_ref[2] = block(y_shared, y_shared)
    for index, row_slot in enumerate((x_shared, y_shared)):
        for place, col_slot in enumerate(finals):
            shared_ref[index, :, place * F : place * F + F] = block(row_slot, col_slot)[:, :F]
    for index, row_slot in enumerate(finals):
        for place, col_slot in enumerate((x_shared, y_shared)):
            value = block(row_slot, col_slot)[:, :F]
            for goal in range(4):
                goals_ref[4 * index + goal, :, place * F : place * F + F] = value
        for goal, col_slot in enumerate(finals):
            goals_ref[4 * index + goal, :, 2 * F :] = block(row_slot, col_slot)[:, :F]


def combine_kernel(*refs):
    squares_ref, links_ref = refs[-2:]
    for half in range(2):
        mine, beside, other, across = refs[4 * half : 4 * half + 4]
        first = mine[0] + beside[0]
        second = other[0] + across[0]
        for copy in range(16):
            squares_ref[copy, half, 0] = first
            squares_ref[copy, half, 1] = second
        for index, ref in enumerate((mine, beside, other, across)):
            links_ref[half, index] = ref[1]
        links_ref[half, 4] = mine[2] + other[2]
        links_ref[half, 5] = pltpu.roll(beside[2] + across[2], 512 - F, 1)


def other_half(value, axis_part):
    flip = 32 if axis_part == "z" else 1
    return lax.ppermute(value, "tile", [(tile, tile ^ flip) for tile in range(64)])


def to_plane(copies):
    return lax.all_to_all(
        copies, "tile", split_axis=0, concat_axis=0, tiled=True, axis_index_groups=PLANES
    )


def ring_shift(value, axis_part, step):
    unit, length = {"x": (2, 4), "y": (8, 4)}[axis_part]
    pairs = []
    for tile in range(64):
        place = (tile // unit) % length
        pairs.append((tile, tile + ((place + step) % length - place) * unit))
    return lax.ppermute(value, "tile", pairs)


def ring_near(value, axis_part):
    return ring_shift(value, axis_part, 1), ring_shift(value, axis_part, -1)


def ring_far(before, after, axis_part):
    return (
        ring_shift(before[..., 0, :, :], axis_part, 1),
        ring_shift(after[..., 1, :, :], axis_part, -1),
    )


def ring_stack(own, before, after, far):
    return jnp.stack([own, before, after, jnp.stack(far, -3)])


def kernel_call(body, out_shapes, name, micros, **options):
    return pl.pallas_call(
        body,
        out_shape=[jax.ShapeDtypeStruct(shape, jnp.float32) for shape in out_shapes],
        compiler_params=pltpu.CompilerParams(vmem_limit_bytes=VMEM_BYTES),
        cost_estimate=pl.CostEstimate(
            flops=micros * 10**9, bytes_accessed=10**6, transcendentals=0
        ),
        name=name,
        **options,
    )


def per_device(box_maps, face_slots):
    smem = pl.BlockSpec(memory_space=pltpu.SMEM)
    vmem = pl.BlockSpec(memory_space=pltpu.VMEM)
    mine, shared_rows, goals = kernel_call(
        select_kernel,
        [(3, 8, 512), (2, 8, 4 * F), (16, 8, 3 * F)],
        "select_rows",
        2,
        in_specs=[smem, vmem],
        out_specs=[vmem] * 3,
    )(face_slots, box_maps[0])
    spread = [
        (64 * box + 16 * quarter + 4 * face + goal, 64 * goal + 16 * box + 4 * face + quarter)
        for box in range(4)
        for quarter in range(4)
        for face in range(4)
        for goal in range(4)
    ]

    parts = [mine] + [
        lax.ppermute(
            mine,
            ("box", "tile"),
            [
                (64 * box + tile, 64 * (box ^ mask) + (tile ^ flip))
                for box in range(4)
                for tile in range(64)
            ],
        )
        for flip in (0, 32)
        for mask in range(4)
        if flip or mask
    ]
    shared_far = other_half(shared_rows, "z")
    row_goals = lax.all_to_all(
        goals, "tile", split_axis=0, concat_axis=0, tiled=True, axis_index_groups=QUARTERS
    )
    parts, shared_far, row_goals = lax.optimization_barrier((parts, shared_far, row_goals))

    squares, links = kernel_call(
        combine_kernel,
        [(16, 2, 2, 8, 512), (2, 6, 8, 512)],
        "combine_boxes",
        1,
        in_specs=[vmem] * 8,
        out_specs=[vmem] * 2,
    )(*parts)
    columns = jnp.stack([shared_rows, shared_far])
    near = ring_near(columns, "y")
    row_parts = lax.ppermute(row_goals[:, :, : 2 * F], ("box", "tile"), spread)
    squares_own = to_plane(squares)
    squares_own, near = lax.optimization_barrier((squares_own, near))

    squares_other = other_half(squares_own, "core")
    links_own = to_plane(jnp.broadcast_to(links, (16, *links.shape)))
    far = ring_far(*near, "y")
    squares_other, far = lax.optimization_barrier((squares_other, far))
    columns = ring_stack(columns, *near, far)
    near = ring_near(columns, "x")

    (inverse,) = kernel_call(
        pair_kernel,
        [(2, F, 512)],
        "invert_pairs",
        20,
        in_specs=[vmem] * 2,
        out_specs=[vmem],
        scratch_shapes=[
            pltpu.VMEM((2, 512, 512), jnp.float32),
            pltpu.VMEM((2, LANES, 512), jnp.float32),
        ],
    )(squares_own, squares_other)
    inverse, links_own, near, row_parts = lax.optimization_barrier(
        (inverse, links_own, near, row_parts)
    )
    links_other = other_half(links_own, "core")
    far = ring_far(*near, "x")
    links_other, far = lax.optimization_barrier((links_other, far))
    columns_own = ring_stack(columns, *near, far).reshape(16, 2, 2, 8, 4 * F)
    columns_other = other_half(columns_own, "core")
    own_rows = []
    for goal in range(4):
        pairs = [
            (64 * box + 16 * quarter + 4 * face + goal, 64 * box + 16 * box + 4 * face + quarter)
            for box in range(4)
            for quarter in range(4)
            for face in range(4)
        ]
        own_rows.append(lax.ppermute(row_goals[:, :, 2 * F :], ("box", "tile"), pairs))
    first, second = kernel_call(
        merge_kernel,
        [(LANES, F)] * 2,
        "merge_pairs",
        45,
        in_specs=[vmem] * 4,
        out_specs=[vmem] * 2,
        scratch_shapes=[
            pltpu.VMEM((2, 2 * F, 3 * 512), jnp.bfloat16),
            pltpu.VMEM((2, 2 * F, 3 * 512), jnp.bfloat16),
            pltpu.VMEM((2 * F + LANES, 2 * F), jnp.float32),
            pltpu.VMEM((3 * LANES, 2 * F), jnp.bfloat16),
        ],
    )(links_own, links_other, inverse, row_parts)
    first, second, own_rows = lax.optimization_barrier((first, second, own_rows))
    own_rows = jnp.concatenate(own_rows, 2)
    (out,) = kernel_call(
        output_kernel,
        [(112, 4 * F)],
        "final_map",
        6,
        grid=(7,),
        in_specs=[
            pl.BlockSpec((LANES, F), lambda i: (0, 0)),
            pl.BlockSpec((LANES, F), lambda i: (0, 0)),
            pl.BlockSpec((16, 2, 2, 8, 256), lambda i: (0, 0, 0, 0, i)),
            pl.BlockSpec((16, 2, 2, 8, 256), lambda i: (0, 0, 0, 0, i)),
            pl.BlockSpec((16, 8, 256), lambda i: (0, 0, i)),
        ],
        out_specs=[pl.BlockSpec((112, 256), lambda i: (0, i))],
        scratch_shapes=[pltpu.VMEM((2, 2, 3, 112, 256), jnp.bfloat16)],
    )(first, second, columns_own, columns_other, own_rows)
    return out


def solution(mesh):
    return jax.shard_map(
        per_device,
        mesh=mesh,
        in_specs=(P("box", None, "tile", None), P()),
        out_specs=P("tile", "box"),
        check_vma=False,
    )
```

```python
import functools

import jax
import jax.numpy as jnp
from jax import lax
from jax.experimental import pallas as pl
from jax.experimental.pallas import tpu as pltpu
from jax.sharding import PartitionSpec as P

F = 448
NODES = 7
LANES = 128
MICRO = 16
VMEM_BYTES = 56 * 1024 * 1024


def tile_of(z, y, x, core):
    return ((z * 4 + y) * 4 + x) * 2 + core


PLANES = [
    [tile_of(z, y, x, core) for y in range(4) for x in range(4)]
    for z in range(2)
    for core in range(2)
]
QUARTERS = [[16 * quarter + own for own in range(16)] for quarter in range(4)]


def matmul(left, right):
    return jnp.dot(left, right, precision=lax.Precision.HIGHEST, preferred_element_type=jnp.float32)


def halves(value):
    high = value.astype(jnp.bfloat16)
    return high, (value - high.astype(jnp.float32)).astype(jnp.bfloat16)


def left_parts(value):
    high, low = halves(value)
    return jnp.concatenate([high, high, low], 1)


def right_parts(value, dim=0):
    high, low = halves(value)
    return jnp.concatenate([high, low, high], dim)


def split_matmul(left, right):
    return jnp.dot(left, right, preferred_element_type=jnp.float32)


def split_matmul_nt(left, right):
    return lax.dot_general(
        left, right, (((1,), (1,)), ((), ())), preferred_element_type=jnp.float32
    )


def invert(stack):
    full = (8, LANES)
    lane = lax.broadcasted_iota(jnp.int32, full, 1)
    sub = lax.broadcasted_iota(jnp.int32, full, 0)

    def along_rows(value, row):
        return jnp.broadcast_to(value[row : row + 1, :], full)

    def along_lanes(value, column):
        return jnp.broadcast_to(value[:, column : column + 1], full)

    stack = [list(rows) for rows in stack]
    count = len(stack[0])
    which = range(len(stack))
    for start in range(0, 8 * count, MICRO):
        first = start // 8
        inside = (lane >= start) & (lane < start + MICRO)
        following = [group for group in (first + 2, first + 3) if group < count]
        rest = [g for g in range(count) if g not in (first, first + 1, *following)]
        pivots = [
            [[along_lanes(stack[n][first + h], start + k) for h in range(2)] for k in range(MICRO)]
            for n in which
        ]
        rows = [
            [
                jnp.where(
                    inside,
                    jnp.where(lane == start + 8 * h + sub, 1.0, 0.0),
                    stack[n][first + h],
                )
                for h in range(2)
            ]
            for n in which
        ]
        ahead = [
            [[along_lanes(stack[n][group], start + k) for k in range(MICRO)] for group in following]
            for n in which
        ]
        for j in range(MICRO):
            half, row = divmod(j, 8)
            chosen = sub == row
            for n in which:
                scale = 1.0 / along_rows(pivots[n][j][half], row)
                pivot_row = along_rows(rows[n][half], row) * scale
                for k in range(j + 1, MICRO):
                    scaled = along_rows(pivots[n][k][half], row) * scale
                    for h in range(2):
                        value = pivots[n][k][h] - pivots[n][j][h] * scaled
                        pivots[n][k][h] = jnp.where(chosen, scaled, value) if h == half else value
                for h in range(2):
                    value = rows[n][h] - pivots[n][j][h] * pivot_row
                    rows[n][h] = jnp.where(chosen, pivot_row, value) if h == half else value
        for n in which:
            spread = [along_rows(rows[n][k // 8], k % 8) for k in range(MICRO)]
            for position, group in enumerate(following):
                terms = [ahead[n][position][k] * spread[k] for k in range(MICRO)]
                while len(terms) > 1:
                    terms = [terms[i] + terms[i + 1] for i in range(0, len(terms), 2)]
                stack[n][group] = jnp.where(inside, 0.0, stack[n][group]) - terms[0]
            if rest:
                zero = jnp.zeros(full, jnp.float32)
                held = jnp.concatenate([stack[n][group] for group in rest], 0)
                panel = jnp.concatenate(
                    [zero] * first + rows[n] + [zero] * (LANES // 8 - first - 2), 0
                )
                update = matmul(held, panel)
                for i, group in enumerate(rest):
                    stack[n][group] = (
                        jnp.where(inside, 0.0, stack[n][group]) - update[8 * i : 8 * i + 8]
                    )
            stack[n][first], stack[n][first + 1] = rows[n]
    return stack


def groups_of(value):
    return [value[8 * g : 8 * g + 8, :] for g in range(value.shape[0] // 8)]


def node_orders(relative=False):
    tile = lax.axis_index("tile")
    core = tile % 2
    shape = (F, 256)
    target = lax.broadcasted_iota(jnp.int32, shape, 0)
    source = lax.broadcasted_iota(jnp.int32, shape, 1)
    inner = source % 8
    place = source // 16
    if relative:
        in_x = place // 4
        in_y = place % 4
        in_x = (tile // 2) % 4 + jnp.where(in_x == 1, 3, jnp.where(in_x == 2, 1, jnp.where(in_x == 3, 2, 0)))
        in_y = (tile // 8) % 4 + jnp.where(in_y == 1, 3, jnp.where(in_y == 2, 1, jnp.where(in_y == 3, 2, 0)))
        place = (in_y % 4) * 4 + in_x % 4
    half = (source // 8) % 2
    half = jnp.where(tile >= 32, 1 - half, half)
    orders = []
    for held_core in (core, 1 - core):
        node = NODES * ((half * 16 + place) * 2 + held_core) + inner
        hit = (node == target) & (inner < NODES)
        orders.append(jnp.where(hit, 1.0, 0.0).astype(jnp.bfloat16))
    return orders


def in_node_order(orders, pieces):
    total = None
    for order, piece in zip(orders, pieces):
        for _ in range(3):
            part = piece.astype(jnp.bfloat16)
            piece = piece - part.astype(jnp.float32)
            term = jnp.dot(order, part, preferred_element_type=jnp.float32)
            total = term if total is None else total + term
    return total


def pair_kernel(own_ref, other_ref, inverse_ref, work, panel):
    orders = node_orders()
    for n in range(2):
        pieces = [ref[:, :, n].reshape(256, 512) for ref in (own_ref, other_ref)]
        work[n, :F, :] = in_node_order(orders, pieces)
        work[n, F:, :] = jnp.zeros((512 - F, 512), jnp.float32)

    def eliminate(block, height):
        at = pl.ds(pl.multiple_of(block * LANES, LANES), LANES)
        squares = [groups_of(work[n, at, at])[: height // 8] for n in range(2)]
        inverses = invert(squares)
        for n in range(2):
            square = jnp.concatenate(inverses[n], 0)
            if height < LANES:
                square = jnp.concatenate(
                    [square, jnp.zeros((LANES - height, LANES), jnp.float32)], 0
                )
            left = left_parts(work[n, :, at])
            scaled = split_matmul(left_parts(square), right_parts(work[n, at, :]))
            work[n, :, at] = jnp.zeros((512, LANES), jnp.float32)
            panel[n] = scaled
            panel[n, :, at] = square
            scaled = panel[n]
            work[n] = work[n] - split_matmul(left, right_parts(scaled))
            work[n, at, :] = scaled

    def step(block, carry):
        eliminate(block, LANES)
        return carry

    lax.fori_loop(0, 3, step, 0)
    eliminate(jnp.int32(3), F - 3 * LANES)
    inverse_ref[...] = work[:, :F, :]


def merge_kernel(
    own_ref,
    other_ref,
    inverse_ref,
    rows_ref,
    first_ref,
    second_ref,
    coupling,
    weighted,
    system,
    panel,
):
    tile = lax.axis_index("tile")
    box = lax.axis_index("box")
    source_box = tile // 16
    pair_slot = jnp.where(source_box // 2 == box // 2, 0, 1)
    side_slot = jnp.where(source_box % 2 == box % 2, 0, 1)
    orders = node_orders()

    def ordered(index):
        pieces = [ref[:, :, index].reshape(256, 512) for ref in (own_ref, other_ref)]
        return in_node_order(orders, pieces)

    for pair in range(2):
        square = right_parts(
            jnp.concatenate([inverse_ref[pair], jnp.zeros((512 - F, 512), jnp.float32)], 0)
        )
        for side in range(2):
            at = pl.ds(side * F, F)
            left = left_parts(ordered(2 * pair + side))
            coupling[pair, at, :] = left
            weighted[pair, at, :] = right_parts(split_matmul(left, square), 1)

    for half in range(2):
        at = pl.ds(half * F, F)
        total = split_matmul_nt(coupling[0, at, :], weighted[0])
        system[at, :] = -total - split_matmul_nt(coupling[1, at, :], weighted[1])
    system[:F, :512] = system[:F, :512] + ordered(4)
    system[F : 2 * F, 384:] = system[F : 2 * F, 384:] + ordered(5)
    coupled = jnp.concatenate(
        [rows_ref[:, :, :F].reshape(LANES, F), jnp.zeros((LANES, 512 - F), jnp.float32)], 1
    )
    coupled_parts = left_parts(coupled)
    system[2 * F :, :] = -split_matmul_nt(coupled_parts, weighted[pair_slot])
    direct = rows_ref[:, :, F : 2 * F].reshape(LANES, F)
    gap = jnp.zeros((LANES, 512 - F), jnp.float32)

    @pl.when(side_slot == 0)
    def _():
        system[2 * F :, :512] = system[2 * F :, :512] + jnp.concatenate([direct, gap], 1)

    @pl.when(side_slot == 1)
    def _():
        system[2 * F :, 384:] = system[2 * F :, 384:] + jnp.concatenate([gap, direct], 1)

    def eliminate(block, carry):
        at = pl.ds(pl.multiple_of(block * LANES, LANES), LANES)
        square = jnp.concatenate(invert([groups_of(system[at, at])])[0], 0)
        scaled = split_matmul(left_parts(square), right_parts(system[at, :]))
        high, low = halves(scaled)
        panel[:LANES] = high
        panel[LANES : 2 * LANES] = low
        high, low = halves(-square)
        panel[:LANES, at] = high
        panel[LANES : 2 * LANES, at] = low
        panel[2 * LANES :] = panel[:LANES]

        def update(start, count):
            rows = pl.ds(pl.multiple_of(start * LANES, LANES), count * LANES)
            left = left_parts(system[rows, at])
            system[rows, at] = jnp.zeros((count * LANES, LANES), jnp.float32)
            system[rows, :] = system[rows, :] - split_matmul(left, panel[...])

        def pairwise(index, inner):
            update(6 - 2 * index, 2)
            return inner

        lax.fori_loop(0, (7 - block) // 2, pairwise, 0)

        @pl.when((7 - block) % 2 == 1)
        def _():
            update(block + 1, 1)

        return carry

    lax.fori_loop(0, 7, eliminate, 0)
    solved = system[2 * F :, :]
    same_pair = jnp.where(pair_slot == 0, 1.0, 0.0)
    square = right_parts(
        jnp.concatenate([inverse_ref[0], jnp.zeros((512 - F, 512), jnp.float32)], 0)
    )
    high = weighted[0, :, :512]
    low = weighted[0, :, 512:1024]
    first = same_pair * split_matmul(coupled_parts, square)
    first = first - split_matmul(left_parts(solved), jnp.concatenate([high, low, high], 0))
    first_ref[...] = first[:, :F]
    second_ref[...] = solved[:, :F]


def output_kernel(first_ref, second_ref, own_ref, other_ref, rows_ref, out_ref, spread):
    @pl.when(pl.program_id(0) == 0)
    def _():
        target = lax.broadcasted_iota(jnp.int32, (112, LANES), 0)
        source = lax.broadcasted_iota(jnp.int32, (112, LANES), 1)
        hit = (NODES * (source // 8) + source % 8 == target) & (source % 8 < NODES)
        compact = jnp.where(hit, 1.0, 0.0)
        orders = node_orders(relative=True)
        for index, ref in enumerate((first_ref, second_ref)):
            high, low = halves(matmul(compact, ref[...]))
            for place, order in enumerate(orders):
                for part, value in enumerate((high, high, low)):
                    moved = jnp.dot(value, order, preferred_element_type=jnp.float32)
                    spread[index, place, part] = moved.astype(jnp.bfloat16)

    target = lax.broadcasted_iota(jnp.int32, (112, LANES), 0)
    source = lax.broadcasted_iota(jnp.int32, (112, LANES), 1)
    hit = (NODES * (source // 8) + source % 8 == target) & (source % 8 < NODES)
    compact = jnp.where(hit, 1.0, 0.0)
    total = matmul(compact, rows_ref[...].reshape(LANES, -1))
    lefts = []
    rights = []
    for index in range(2):
        for place, ref in enumerate((own_ref, other_ref)):
            lefts += [spread[index, place, part] for part in range(3)]
            rights.append(right_parts(ref[:, :, index].reshape(256, -1)))
    total = total - split_matmul(jnp.concatenate(lefts, 1), jnp.concatenate(rights, 0))
    out_ref[...] = total


def select_kernel(slots_ref, stored_ref, mine_ref, shared_ref, goals_ref):
    box = lax.axis_index("box")
    along_x = box % 2
    along_y = box // 2
    x_shared = slots_ref[box, 1 - along_x]
    y_shared = slots_ref[box, 3 - along_y]
    finals = [
        slots_ref[box, along_x],
        slots_ref[box, 2 + along_y],
        slots_ref[box, 4],
        slots_ref[box, 5],
    ]
    lane = lax.broadcasted_iota(jnp.int32, (8, 512), 1)

    def block(row_slot, col_slot):
        start = pl.multiple_of(((col_slot * 7) // 2) * LANES, LANES)
        value = stored_ref[row_slot, :, pl.ds(start, 512)]
        value = jnp.concatenate([value, jnp.zeros((1, 512), jnp.float32)], 0)
        value = jnp.where(col_slot % 2 == 1, pltpu.roll(value, F, 1), value)
        return jnp.where(lane < F, value, 0.0)

    mine_ref[0] = block(x_shared, x_shared)
    mine_ref[1] = block(y_shared, x_shared)
    mine_ref[2] = block(y_shared, y_shared)
    for index, row_slot in enumerate((x_shared, y_shared)):
        for place, col_slot in enumerate(finals):
            shared_ref[index, :, place * F : place * F + F] = block(row_slot, col_slot)[:, :F]
    for index, row_slot in enumerate(finals):
        for place, col_slot in enumerate((x_shared, y_shared, *finals)):
            value = block(row_slot, col_slot)[:, :F]
            for goal in range(4):
                goals_ref[4 * index + goal, :, place * F : place * F + F] = value


def combine_kernel(*refs):
    squares_ref, links_ref = refs[-2:]
    for half in range(2):
        mine, beside, other, across = refs[4 * half : 4 * half + 4]
        first = mine[0] + beside[0]
        second = other[0] + across[0]
        for copy in range(16):
            squares_ref[copy, half, 0] = first
            squares_ref[copy, half, 1] = second
        for index, ref in enumerate((mine, beside, other, across)):
            links_ref[half, index] = ref[1]
        links_ref[half, 4] = mine[2] + other[2]
        links_ref[half, 5] = pltpu.roll(beside[2] + across[2], 512 - F, 1)


def other_half(value, axis_part):
    flip = 32 if axis_part == "z" else 1
    return lax.ppermute(value, "tile", [(tile, tile ^ flip) for tile in range(64)])


def to_plane(copies):
    return lax.all_to_all(
        copies, "tile", split_axis=0, concat_axis=0, tiled=True, axis_index_groups=PLANES
    )


def ring_shift(value, axis_part, step):
    unit, length = {"x": (2, 4), "y": (8, 4)}[axis_part]
    pairs = []
    for tile in range(64):
        place = (tile // unit) % length
        pairs.append((tile, tile + ((place + step) % length - place) * unit))
    return lax.ppermute(value, "tile", pairs)


def ring_near(value, axis_part):
    return ring_shift(value, axis_part, 1), ring_shift(value, axis_part, -1)


def ring_far(before, after, axis_part):
    return (
        ring_shift(before[..., 0, :, :], axis_part, 1),
        ring_shift(after[..., 1, :, :], axis_part, -1),
    )


def ring_stack(own, before, after, far):
    return jnp.stack([own, before, after, jnp.stack(far, -3)])


def kernel_call(body, out_shapes, name, micros, **options):
    return pl.pallas_call(
        body,
        out_shape=[jax.ShapeDtypeStruct(shape, jnp.float32) for shape in out_shapes],
        compiler_params=pltpu.CompilerParams(vmem_limit_bytes=VMEM_BYTES),
        cost_estimate=pl.CostEstimate(
            flops=micros * 10**9, bytes_accessed=10**6, transcendentals=0
        ),
        name=name,
        **options,
    )


def per_device(box_maps, face_slots):
    smem = pl.BlockSpec(memory_space=pltpu.SMEM)
    vmem = pl.BlockSpec(memory_space=pltpu.VMEM)
    mine, shared_rows, goals = kernel_call(
        select_kernel,
        [(3, 8, 512), (2, 8, 4 * F), (16, 8, 6 * F)],
        "select_rows",
        2,
        in_specs=[smem, vmem],
        out_specs=[vmem] * 3,
    )(face_slots, box_maps[0])
    spread = [
        (64 * box + 16 * quarter + 4 * face + goal, 64 * goal + 16 * box + 4 * face + quarter)
        for box in range(4)
        for quarter in range(4)
        for face in range(4)
        for goal in range(4)
    ]

    parts = [mine] + [
        lax.ppermute(
            mine,
            ("box", "tile"),
            [
                (64 * box + tile, 64 * (box ^ mask) + (tile ^ flip))
                for box in range(4)
                for tile in range(64)
            ],
        )
        for flip in (0, 32)
        for mask in range(4)
        if flip or mask
    ]
    shared_far = other_half(shared_rows, "z")
    row_goals = lax.all_to_all(
        goals, "tile", split_axis=0, concat_axis=0, tiled=True, axis_index_groups=QUARTERS
    )
    parts, shared_far, row_goals = lax.optimization_barrier((parts, shared_far, row_goals))

    squares, links = kernel_call(
        combine_kernel,
        [(16, 2, 2, 8, 512), (2, 6, 8, 512)],
        "combine_boxes",
        1,
        in_specs=[vmem] * 8,
        out_specs=[vmem] * 2,
    )(*parts)
    columns = jnp.stack([shared_rows, shared_far])
    near = ring_near(columns, "y")
    row_parts = lax.ppermute(row_goals[:, :, : 2 * F], ("box", "tile"), spread)
    squares_own = to_plane(squares)
    squares_own, near = lax.optimization_barrier((squares_own, near))

    squares_other = other_half(squares_own, "core")
    links_own = to_plane(jnp.broadcast_to(links, (16, *links.shape)))
    far = ring_far(*near, "y")
    (inverse,) = kernel_call(
        pair_kernel,
        [(2, F, 512)],
        "invert_pairs",
        20,
        in_specs=[vmem] * 2,
        out_specs=[vmem],
        scratch_shapes=[
            pltpu.VMEM((2, 512, 512), jnp.float32),
            pltpu.VMEM((2, LANES, 512), jnp.float32),
        ],
    )(squares_own, squares_other)
    inverse, far = lax.optimization_barrier((inverse, far))
    columns = ring_stack(columns, *near, far)
    near = ring_near(columns, "x")
    inverse, links_own, near, row_parts = lax.optimization_barrier(
        (inverse, links_own, near, row_parts)
    )
    links_other = other_half(links_own, "core")
    far = ring_far(*near, "x")
    links_other, far = lax.optimization_barrier((links_other, far))
    columns_own = ring_stack(columns, *near, far).reshape(16, 2, 2, 8, 4 * F)
    columns_other = other_half(columns_own, "core")
    own_rows = lax.ppermute(
        row_goals[:, :, 2 * F :],
        ("box", "tile"),
        [pair for pair in spread if pair[0] // 64 == pair[1] // 64],
    )
    first, second = kernel_call(
        merge_kernel,
        [(LANES, F)] * 2,
        "merge_pairs",
        45,
        in_specs=[vmem] * 4,
        out_specs=[vmem] * 2,
        scratch_shapes=[
            pltpu.VMEM((2, 2 * F, 3 * 512), jnp.bfloat16),
            pltpu.VMEM((2, 2 * F, 3 * 512), jnp.bfloat16),
            pltpu.VMEM((2 * F + LANES, 2 * F), jnp.float32),
            pltpu.VMEM((3 * LANES, 2 * F), jnp.bfloat16),
        ],
    )(links_own, links_other, inverse, row_parts)
    (out,) = kernel_call(
        output_kernel,
        [(112, 4 * F)],
        "final_map",
        6,
        grid=(7,),
        in_specs=[
            pl.BlockSpec((LANES, F), lambda i: (0, 0)),
            pl.BlockSpec((LANES, F), lambda i: (0, 0)),
            pl.BlockSpec((16, 2, 2, 8, 256), lambda i: (0, 0, 0, 0, i)),
            pl.BlockSpec((16, 2, 2, 8, 256), lambda i: (0, 0, 0, 0, i)),
            pl.BlockSpec((16, 8, 256), lambda i: (0, 0, i)),
        ],
        out_specs=[pl.BlockSpec((112, 256), lambda i: (0, i))],
        scratch_shapes=[pltpu.VMEM((2, 2, 3, 112, 256), jnp.bfloat16)],
    )(first, second, columns_own, columns_other, own_rows)
    return out


def solution(mesh):
    return jax.shard_map(
        per_device,
        mesh=mesh,
        in_specs=(P("box", None, "tile", None), P()),
        out_specs=P("tile", "box"),
        check_vma=False,
    )
```

```python
import functools

import jax
import jax.numpy as jnp
from jax import lax
from jax.experimental import pallas as pl
from jax.experimental.pallas import tpu as pltpu
from jax.sharding import PartitionSpec as P

F = 448
NODES = 7
LANES = 128
MICRO = 16
VMEM_BYTES = 56 * 1024 * 1024


def tile_of(z, y, x, core):
    return ((z * 4 + y) * 4 + x) * 2 + core


PLANES = [
    [tile_of(z, y, x, core) for y in range(4) for x in range(4)]
    for z in range(2)
    for core in range(2)
]
QUARTERS = [[16 * quarter + own for own in range(16)] for quarter in range(4)]


def matmul(left, right):
    return jnp.dot(left, right, precision=lax.Precision.HIGHEST, preferred_element_type=jnp.float32)


def halves(value):
    high = value.astype(jnp.bfloat16)
    return high, (value - high.astype(jnp.float32)).astype(jnp.bfloat16)


def left_parts(value):
    high, low = halves(value)
    return jnp.concatenate([high, high, low], 1)


def right_parts(value, dim=0):
    high, low = halves(value)
    return jnp.concatenate([high, low, high], dim)


def split_matmul(left, right):
    return jnp.dot(left, right, preferred_element_type=jnp.float32)


def split_matmul_nt(left, right):
    return lax.dot_general(
        left, right, (((1,), (1,)), ((), ())), preferred_element_type=jnp.float32
    )


def invert(stack):
    full = (8, LANES)
    lane = lax.broadcasted_iota(jnp.int32, full, 1)
    sub = lax.broadcasted_iota(jnp.int32, full, 0)

    def along_rows(value, row):
        return jnp.broadcast_to(value[row : row + 1, :], full)

    def along_lanes(value, column):
        return jnp.broadcast_to(value[:, column : column + 1], full)

    stack = [list(rows) for rows in stack]
    count = len(stack[0])
    which = range(len(stack))
    for start in range(0, 8 * count, MICRO):
        first = start // 8
        inside = (lane >= start) & (lane < start + MICRO)
        following = [group for group in (first + 2, first + 3) if group < count]
        rest = [g for g in range(count) if g not in (first, first + 1, *following)]
        pivots = [
            [[along_lanes(stack[n][first + h], start + k) for h in range(2)] for k in range(MICRO)]
            for n in which
        ]
        rows = [
            [
                jnp.where(
                    inside,
                    jnp.where(lane == start + 8 * h + sub, 1.0, 0.0),
                    stack[n][first + h],
                )
                for h in range(2)
            ]
            for n in which
        ]
        ahead = [
            [[along_lanes(stack[n][group], start + k) for k in range(MICRO)] for group in following]
            for n in which
        ]
        for j in range(MICRO):
            half, row = divmod(j, 8)
            chosen = sub == row
            for n in which:
                scale = 1.0 / along_rows(pivots[n][j][half], row)
                pivot_row = along_rows(rows[n][half], row) * scale
                for k in range(j + 1, MICRO):
                    scaled = along_rows(pivots[n][k][half], row) * scale
                    for h in range(2):
                        value = pivots[n][k][h] - pivots[n][j][h] * scaled
                        pivots[n][k][h] = jnp.where(chosen, scaled, value) if h == half else value
                for h in range(2):
                    value = rows[n][h] - pivots[n][j][h] * pivot_row
                    rows[n][h] = jnp.where(chosen, pivot_row, value) if h == half else value
        for n in which:
            spread = [along_rows(rows[n][k // 8], k % 8) for k in range(MICRO)]
            for position, group in enumerate(following):
                terms = [ahead[n][position][k] * spread[k] for k in range(MICRO)]
                while len(terms) > 1:
                    terms = [terms[i] + terms[i + 1] for i in range(0, len(terms), 2)]
                stack[n][group] = jnp.where(inside, 0.0, stack[n][group]) - terms[0]
            if rest:
                zero = jnp.zeros(full, jnp.float32)
                held = jnp.concatenate([stack[n][group] for group in rest], 0)
                panel = jnp.concatenate(
                    [zero] * first + rows[n] + [zero] * (LANES // 8 - first - 2), 0
                )
                update = matmul(held, panel)
                for i, group in enumerate(rest):
                    stack[n][group] = (
                        jnp.where(inside, 0.0, stack[n][group]) - update[8 * i : 8 * i + 8]
                    )
            stack[n][first], stack[n][first + 1] = rows[n]
    return stack


def groups_of(value):
    return [value[8 * g : 8 * g + 8, :] for g in range(value.shape[0] // 8)]


def node_orders(layout):
    tile = lax.axis_index("tile")
    core = tile % 2
    shape = (F, 256)
    target = lax.broadcasted_iota(jnp.int32, shape, 0)
    source = lax.broadcasted_iota(jnp.int32, shape, 1)
    inner = source % 8
    place = source // 16
    if layout != "plane":
        in_y, in_x = place // 4, place % 4
        if layout == "x first":
            in_y, in_x = in_x, in_y

        def moved(start, step):
            far = jnp.where(step == 3, 2, 0)
            return (start + jnp.where(step == 1, 3, jnp.where(step == 2, 1, far))) % 4

        place = moved((tile // 8) % 4, in_y) * 4 + moved((tile // 2) % 4, in_x)
    half = (source // 8) % 2
    half = jnp.where(tile >= 32, 1 - half, half)
    orders = []
    for held_core in (core, 1 - core):
        node = NODES * ((half * 16 + place) * 2 + held_core) + inner
        hit = (node == target) & (inner < NODES)
        orders.append(jnp.where(hit, 1.0, 0.0).astype(jnp.bfloat16))
    return orders


def in_node_order(orders, pieces):
    total = None
    for order, piece in zip(orders, pieces):
        for _ in range(3):
            part = piece.astype(jnp.bfloat16)
            piece = piece - part.astype(jnp.float32)
            term = jnp.dot(order, part, preferred_element_type=jnp.float32)
            total = term if total is None else total + term
    return total


def pair_kernel(own_ref, other_ref, inverse_ref, work, panel):
    orders = node_orders("plane")
    for n in range(2):
        pieces = [ref[:, :, n].reshape(256, 512) for ref in (own_ref, other_ref)]
        work[n, :F, :] = in_node_order(orders, pieces)
        work[n, F:, :] = jnp.zeros((512 - F, 512), jnp.float32)

    def eliminate(block, height):
        at = pl.ds(pl.multiple_of(block * LANES, LANES), LANES)
        squares = [groups_of(work[n, at, at])[: height // 8] for n in range(2)]
        inverses = invert(squares)
        for n in range(2):
            square = jnp.concatenate(inverses[n], 0)
            if height < LANES:
                square = jnp.concatenate(
                    [square, jnp.zeros((LANES - height, LANES), jnp.float32)], 0
                )
            left = left_parts(work[n, :, at])
            scaled = split_matmul(left_parts(square), right_parts(work[n, at, :]))
            work[n, :, at] = jnp.zeros((512, LANES), jnp.float32)
            panel[n] = scaled
            panel[n, :, at] = square
            scaled = panel[n]
            work[n] = work[n] - split_matmul(left, right_parts(scaled))
            work[n, at, :] = scaled

    def step(block, carry):
        eliminate(block, LANES)
        return carry

    lax.fori_loop(0, 3, step, 0)
    eliminate(jnp.int32(3), F - 3 * LANES)
    inverse_ref[...] = work[:, :F, :]


def merge_kernel(
    own_ref,
    other_ref,
    inverse_ref,
    rows_ref,
    first_ref,
    second_ref,
    coupling,
    weighted,
    system,
    panel,
):
    tile = lax.axis_index("tile")
    box = lax.axis_index("box")
    source_box = tile // 16
    pair_slot = jnp.where(source_box // 2 == box // 2, 0, 1)
    side_slot = jnp.where(source_box % 2 == box % 2, 0, 1)
    orders = node_orders("y first")

    def ordered(index):
        pieces = [ref[:, :, index].reshape(256, 512) for ref in (own_ref, other_ref)]
        return in_node_order(orders, pieces)

    for pair in range(2):
        square = right_parts(
            jnp.concatenate([inverse_ref[pair], jnp.zeros((512 - F, 512), jnp.float32)], 0)
        )
        for side in range(2):
            at = pl.ds(side * F, F)
            left = left_parts(ordered(2 * pair + side))
            coupling[pair, at, :] = left
            weighted[pair, at, :] = right_parts(split_matmul(left, square), 1)

    for half in range(2):
        at = pl.ds(half * F, F)
        total = split_matmul_nt(coupling[0, at, :], weighted[0])
        system[at, :] = -total - split_matmul_nt(coupling[1, at, :], weighted[1])
    system[:F, :512] = system[:F, :512] + ordered(4)
    system[F : 2 * F, 384:] = system[F : 2 * F, 384:] + ordered(5)
    coupled = jnp.concatenate(
        [rows_ref[:, :, :F].reshape(LANES, F), jnp.zeros((LANES, 512 - F), jnp.float32)], 1
    )
    coupled_parts = left_parts(coupled)
    system[2 * F :, :] = -split_matmul_nt(coupled_parts, weighted[pair_slot])
    direct = rows_ref[:, :, F : 2 * F].reshape(LANES, F)
    gap = jnp.zeros((LANES, 512 - F), jnp.float32)

    @pl.when(side_slot == 0)
    def _():
        system[2 * F :, :512] = system[2 * F :, :512] + jnp.concatenate([direct, gap], 1)

    @pl.when(side_slot == 1)
    def _():
        system[2 * F :, 384:] = system[2 * F :, 384:] + jnp.concatenate([gap, direct], 1)

    def eliminate(block, carry):
        at = pl.ds(pl.multiple_of(block * LANES, LANES), LANES)
        square = jnp.concatenate(invert([groups_of(system[at, at])])[0], 0)
        scaled = split_matmul(left_parts(square), right_parts(system[at, :]))
        high, low = halves(scaled)
        panel[:LANES] = high
        panel[LANES : 2 * LANES] = low
        high, low = halves(-square)
        panel[:LANES, at] = high
        panel[LANES : 2 * LANES, at] = low
        panel[2 * LANES :] = panel[:LANES]

        def update(start, count):
            rows = pl.ds(pl.multiple_of(start * LANES, LANES), count * LANES)
            left = left_parts(system[rows, at])
            system[rows, at] = jnp.zeros((count * LANES, LANES), jnp.float32)
            system[rows, :] = system[rows, :] - split_matmul(left, panel[...])

        def pairwise(index, inner):
            update(6 - 2 * index, 2)
            return inner

        lax.fori_loop(0, (7 - block) // 2, pairwise, 0)

        @pl.when((7 - block) % 2 == 1)
        def _():
            update(block + 1, 1)

        return carry

    lax.fori_loop(0, 7, eliminate, 0)
    solved = system[2 * F :, :]
    same_pair = jnp.where(pair_slot == 0, 1.0, 0.0)
    square = right_parts(
        jnp.concatenate([inverse_ref[0], jnp.zeros((512 - F, 512), jnp.float32)], 0)
    )
    high = weighted[0, :, :512]
    low = weighted[0, :, 512:1024]
    first = same_pair * split_matmul(coupled_parts, square)
    first = first - split_matmul(left_parts(solved), jnp.concatenate([high, low, high], 0))
    first_ref[...] = first[:, :F]
    second_ref[...] = solved[:, :F]


def output_kernel(first_ref, second_ref, own_ref, other_ref, rows_ref, out_ref, spread):
    @pl.when(pl.program_id(0) == 0)
    def _():
        target = lax.broadcasted_iota(jnp.int32, (112, LANES), 0)
        source = lax.broadcasted_iota(jnp.int32, (112, LANES), 1)
        hit = (NODES * (source // 8) + source % 8 == target) & (source % 8 < NODES)
        compact = jnp.where(hit, 1.0, 0.0)
        orders = node_orders("x first")
        for index, ref in enumerate((first_ref, second_ref)):
            high, low = halves(matmul(compact, ref[...]))
            for place, order in enumerate(orders):
                for part, value in enumerate((high, high, low)):
                    moved = jnp.dot(value, order, preferred_element_type=jnp.float32)
                    spread[index, place, part] = moved.astype(jnp.bfloat16)

    target = lax.broadcasted_iota(jnp.int32, (112, LANES), 0)
    source = lax.broadcasted_iota(jnp.int32, (112, LANES), 1)
    hit = (NODES * (source // 8) + source % 8 == target) & (source % 8 < NODES)
    compact = jnp.where(hit, 1.0, 0.0)
    total = matmul(compact, rows_ref[...].reshape(LANES, -1))
    lefts = []
    rights = []
    for index in range(2):
        for place, ref in enumerate((own_ref, other_ref)):
            lefts += [spread[index, place, part] for part in range(3)]
            rights.append(right_parts(ref[:, :, index].reshape(256, -1)))
    total = total - split_matmul(jnp.concatenate(lefts, 1), jnp.concatenate(rights, 0))
    out_ref[...] = total


def select_kernel(slots_ref, stored_ref, mine_ref, shared_ref, goals_ref):
    box = lax.axis_index("box")
    along_x = box % 2
    along_y = box // 2
    x_shared = slots_ref[box, 1 - along_x]
    y_shared = slots_ref[box, 3 - along_y]
    finals = [
        slots_ref[box, along_x],
        slots_ref[box, 2 + along_y],
        slots_ref[box, 4],
        slots_ref[box, 5],
    ]
    lane = lax.broadcasted_iota(jnp.int32, (8, 512), 1)

    def block(row_slot, col_slot):
        start = pl.multiple_of(((col_slot * 7) // 2) * LANES, LANES)
        value = stored_ref[row_slot, :, pl.ds(start, 512)]
        value = jnp.concatenate([value, jnp.zeros((1, 512), jnp.float32)], 0)
        value = jnp.where(col_slot % 2 == 1, pltpu.roll(value, F, 1), value)
        return jnp.where(lane < F, value, 0.0)

    mine_ref[0] = block(x_shared, x_shared)
    mine_ref[1] = block(y_shared, x_shared)
    mine_ref[2] = block(y_shared, y_shared)
    for index, row_slot in enumerate((x_shared, y_shared)):
        for place, col_slot in enumerate(finals):
            shared_ref[index, :, place * F : place * F + F] = block(row_slot, col_slot)[:, :F]
    for index, row_slot in enumerate(finals):
        for place, col_slot in enumerate((x_shared, y_shared, *finals)):
            value = block(row_slot, col_slot)[:, :F]
            for goal in range(4):
                goals_ref[4 * index + goal, :, place * F : place * F + F] = value


def combine_kernel(*refs):
    squares_ref, links_ref = refs[-2:]
    for half in range(2):
        mine, beside, other, across = refs[4 * half : 4 * half + 4]
        first = mine[0] + beside[0]
        second = other[0] + across[0]
        for copy in range(16):
            squares_ref[copy, half, 0] = first
            squares_ref[copy, half, 1] = second
        for index, ref in enumerate((mine, beside, other, across)):
            links_ref[half, index] = ref[1]
        links_ref[half, 4] = mine[2] + other[2]
        links_ref[half, 5] = pltpu.roll(beside[2] + across[2], 512 - F, 1)


def other_half(value, axis_part):
    flip = 32 if axis_part == "z" else 1
    return lax.ppermute(value, "tile", [(tile, tile ^ flip) for tile in range(64)])


def to_plane(copies):
    return lax.all_to_all(
        copies, "tile", split_axis=0, concat_axis=0, tiled=True, axis_index_groups=PLANES
    )


def ring_shift(value, axis_part, step):
    unit, length = {"x": (2, 4), "y": (8, 4)}[axis_part]
    pairs = []
    for tile in range(64):
        place = (tile // unit) % length
        pairs.append((tile, tile + ((place + step) % length - place) * unit))
    return lax.ppermute(value, "tile", pairs)


def ring_near(value, axis_part):
    return ring_shift(value, axis_part, 1), ring_shift(value, axis_part, -1)


def ring_far(before, after, axis_part, dim):
    return (
        ring_shift(lax.slice_in_dim(before, 0, 1, axis=dim), axis_part, 1),
        ring_shift(lax.slice_in_dim(after, 1, 2, axis=dim), axis_part, -1),
    )


def ring_stack(own, near, far, dim):
    return jnp.stack([own, *near, jnp.concatenate(far, dim)])


def kernel_call(body, out_shapes, name, micros, **options):
    return pl.pallas_call(
        body,
        out_shape=[jax.ShapeDtypeStruct(shape, jnp.float32) for shape in out_shapes],
        compiler_params=pltpu.CompilerParams(vmem_limit_bytes=VMEM_BYTES),
        cost_estimate=pl.CostEstimate(
            flops=micros * 10**9, bytes_accessed=10**6, transcendentals=0
        ),
        name=name,
        **options,
    )


def per_device(box_maps, face_slots):
    smem = pl.BlockSpec(memory_space=pltpu.SMEM)
    vmem = pl.BlockSpec(memory_space=pltpu.VMEM)
    mine, shared_rows, goals = kernel_call(
        select_kernel,
        [(3, 8, 512), (2, 8, 4 * F), (16, 8, 6 * F)],
        "select_rows",
        2,
        in_specs=[smem, vmem],
        out_specs=[vmem] * 3,
    )(face_slots, box_maps[0])
    spread = [
        (64 * box + 16 * quarter + 4 * face + goal, 64 * goal + 16 * box + 4 * face + quarter)
        for box in range(4)
        for quarter in range(4)
        for face in range(4)
        for goal in range(4)
    ]

    parts = [mine] + [
        lax.ppermute(
            mine,
            ("box", "tile"),
            [
                (64 * box + tile, 64 * (box ^ mask) + (tile ^ flip))
                for box in range(4)
                for tile in range(64)
            ],
        )
        for flip in (0, 32)
        for mask in range(4)
        if flip or mask
    ]
    shared_far = other_half(shared_rows, "z")
    row_goals = lax.all_to_all(
        goals, "tile", split_axis=0, concat_axis=0, tiled=True, axis_index_groups=QUARTERS
    )
    parts, shared_far, row_goals = lax.optimization_barrier((parts, shared_far, row_goals))

    squares, links = kernel_call(
        combine_kernel,
        [(16, 2, 2, 8, 512), (2, 6, 8, 512)],
        "combine_boxes",
        1,
        in_specs=[vmem] * 8,
        out_specs=[vmem] * 2,
    )(*parts)
    columns = jnp.stack([shared_rows, shared_far])
    columns_near = ring_near(columns, "y")
    links_near = ring_near(links, "x")
    squares_own = to_plane(squares)
    row_parts = lax.ppermute(row_goals[:, :, : 2 * F], ("box", "tile"), spread)
    squares_own, columns_near, links_near, row_parts = lax.optimization_barrier(
        (squares_own, columns_near, links_near, row_parts)
    )

    squares_other = other_half(squares_own, "core")
    columns_far = ring_far(*columns_near, "y", 0)
    links_far = ring_far(*links_near, "x", 0)
    squares_other, columns_far, links_far = lax.optimization_barrier(
        (squares_other, columns_far, links_far)
    )

    columns = ring_stack(columns, columns_near, columns_far, 0)
    links = ring_stack(links, links_near, links_far, 0)
    columns_near = ring_near(columns, "x")
    links_near = ring_near(links, "y")
    (inverse,) = kernel_call(
        pair_kernel,
        [(2, F, 512)],
        "invert_pairs",
        20,
        in_specs=[vmem] * 2,
        out_specs=[vmem],
        scratch_shapes=[
            pltpu.VMEM((2, 512, 512), jnp.float32),
            pltpu.VMEM((2, LANES, 512), jnp.float32),
        ],
    )(squares_own, squares_other)
    inverse, columns_near, links_near, row_goals = lax.optimization_barrier(
        (inverse, columns_near, links_near, row_goals)
    )
    links_far = ring_far(*links_near, "y", 1)
    columns_far = ring_far(*columns_near, "x", 1)
    links_far, columns_far = lax.optimization_barrier((links_far, columns_far))
    links_own = ring_stack(links, links_near, links_far, 1).reshape(16, 2, 6, 8, 512)
    links_other = other_half(links_own, "core")
    columns_own = ring_stack(columns, columns_near, columns_far, 1).reshape(16, 2, 2, 8, 4 * F)
    columns_other = other_half(columns_own, "core")
    own_rows = lax.ppermute(
        row_goals[:, :, 2 * F :],
        ("box", "tile"),
        [pair for pair in spread if pair[0] // 64 == pair[1] // 64],
    )
    first, second = kernel_call(
        merge_kernel,
        [(LANES, F)] * 2,
        "merge_pairs",
        45,
        in_specs=[vmem] * 4,
        out_specs=[vmem] * 2,
        scratch_shapes=[
            pltpu.VMEM((2, 2 * F, 3 * 512), jnp.bfloat16),
            pltpu.VMEM((2, 2 * F, 3 * 512), jnp.bfloat16),
            pltpu.VMEM((2 * F + LANES, 2 * F), jnp.float32),
            pltpu.VMEM((3 * LANES, 2 * F), jnp.bfloat16),
        ],
    )(links_own, links_other, inverse, row_parts)
    (out,) = kernel_call(
        output_kernel,
        [(112, 4 * F)],
        "final_map",
        6,
        grid=(7,),
        in_specs=[
            pl.BlockSpec((LANES, F), lambda i: (0, 0)),
            pl.BlockSpec((LANES, F), lambda i: (0, 0)),
            pl.BlockSpec((16, 2, 2, 8, 256), lambda i: (0, 0, 0, 0, i)),
            pl.BlockSpec((16, 2, 2, 8, 256), lambda i: (0, 0, 0, 0, i)),
            pl.BlockSpec((16, 8, 256), lambda i: (0, 0, i)),
        ],
        out_specs=[pl.BlockSpec((112, 256), lambda i: (0, i))],
        scratch_shapes=[pltpu.VMEM((2, 2, 3, 112, 256), jnp.bfloat16)],
    )(first, second, columns_own, columns_other, own_rows)
    return out


def solution(mesh):
    return jax.shard_map(
        per_device,
        mesh=mesh,
        in_specs=(P("box", None, "tile", None), P()),
        out_specs=P("tile", "box"),
        check_vma=False,
    )
```

```python
import functools

import jax
import jax.numpy as jnp
from jax import lax
from jax.experimental import pallas as pl
from jax.experimental.pallas import tpu as pltpu
from jax.sharding import PartitionSpec as P

F = 448
NODES = 7
LANES = 128
MICRO = 16
VMEM_BYTES = 56 * 1024 * 1024


def tile_of(z, y, x, core):
    return ((z * 4 + y) * 4 + x) * 2 + core


PLANES = [
    [tile_of(z, y, x, core) for y in range(4) for x in range(4)]
    for z in range(2)
    for core in range(2)
]
LINES = [
    [64 * box + 32 * half + tile for half in range(2) for box in range(4)] for tile in range(32)
]
QUARTERS = [[16 * quarter + own for own in range(16)] for quarter in range(4)]


def matmul(left, right):
    return jnp.dot(left, right, precision=lax.Precision.HIGHEST, preferred_element_type=jnp.float32)


def halves(value):
    high = value.astype(jnp.bfloat16)
    return high, (value - high.astype(jnp.float32)).astype(jnp.bfloat16)


def left_parts(value):
    high, low = halves(value)
    return jnp.concatenate([high, high, low], 1)


def right_parts(value, dim=0):
    high, low = halves(value)
    return jnp.concatenate([high, low, high], dim)


def split_matmul(left, right):
    return jnp.dot(left, right, preferred_element_type=jnp.float32)


def split_matmul_nt(left, right):
    return lax.dot_general(
        left, right, (((1,), (1,)), ((), ())), preferred_element_type=jnp.float32
    )


def invert(stack):
    full = (8, LANES)
    lane = lax.broadcasted_iota(jnp.int32, full, 1)
    sub = lax.broadcasted_iota(jnp.int32, full, 0)

    def along_rows(value, row):
        return jnp.broadcast_to(value[row : row + 1, :], full)

    def along_lanes(value, column):
        return jnp.broadcast_to(value[:, column : column + 1], full)

    stack = [list(rows) for rows in stack]
    count = len(stack[0])
    which = range(len(stack))
    for start in range(0, 8 * count, MICRO):
        first = start // 8
        inside = (lane >= start) & (lane < start + MICRO)
        following = [group for group in (first + 2, first + 3) if group < count]
        rest = [g for g in range(count) if g not in (first, first + 1, *following)]
        pivots = [
            [[along_lanes(stack[n][first + h], start + k) for h in range(2)] for k in range(MICRO)]
            for n in which
        ]
        rows = [
            [
                jnp.where(
                    inside,
                    jnp.where(lane == start + 8 * h + sub, 1.0, 0.0),
                    stack[n][first + h],
                )
                for h in range(2)
            ]
            for n in which
        ]
        ahead = [
            [[along_lanes(stack[n][group], start + k) for k in range(MICRO)] for group in following]
            for n in which
        ]
        for j in range(MICRO):
            half, row = divmod(j, 8)
            chosen = sub == row
            for n in which:
                scale = 1.0 / along_rows(pivots[n][j][half], row)
                pivot_row = along_rows(rows[n][half], row) * scale
                for k in range(j + 1, MICRO):
                    scaled = along_rows(pivots[n][k][half], row) * scale
                    for h in range(2):
                        value = pivots[n][k][h] - pivots[n][j][h] * scaled
                        pivots[n][k][h] = jnp.where(chosen, scaled, value) if h == half else value
                for h in range(2):
                    value = rows[n][h] - pivots[n][j][h] * pivot_row
                    rows[n][h] = jnp.where(chosen, pivot_row, value) if h == half else value
        for n in which:
            spread = [along_rows(rows[n][k // 8], k % 8) for k in range(MICRO)]
            for position, group in enumerate(following):
                terms = [ahead[n][position][k] * spread[k] for k in range(MICRO)]
                while len(terms) > 1:
                    terms = [terms[i] + terms[i + 1] for i in range(0, len(terms), 2)]
                stack[n][group] = jnp.where(inside, 0.0, stack[n][group]) - terms[0]
            if rest:
                zero = jnp.zeros(full, jnp.float32)
                held = jnp.concatenate([stack[n][group] for group in rest], 0)
                panel = jnp.concatenate(
                    [zero] * first + rows[n] + [zero] * (LANES // 8 - first - 2), 0
                )
                update = matmul(held, panel)
                for i, group in enumerate(rest):
                    stack[n][group] = (
                        jnp.where(inside, 0.0, stack[n][group]) - update[8 * i : 8 * i + 8]
                    )
            stack[n][first], stack[n][first + 1] = rows[n]
    return stack


def groups_of(value):
    return [value[8 * g : 8 * g + 8, :] for g in range(value.shape[0] // 8)]


def node_orders(layout):
    tile = lax.axis_index("tile")
    core = tile % 2
    shape = (F, 256)
    target = lax.broadcasted_iota(jnp.int32, shape, 0)
    source = lax.broadcasted_iota(jnp.int32, shape, 1)
    inner = source % 8
    place = source // 16
    if layout != "plane":
        in_y, in_x = place // 4, place % 4
        if layout == "x first":
            in_y, in_x = in_x, in_y

        def moved(start, step):
            far = jnp.where(step == 3, 2, 0)
            return (start + jnp.where(step == 1, 3, jnp.where(step == 2, 1, far))) % 4

        place = moved((tile // 8) % 4, in_y) * 4 + moved((tile // 2) % 4, in_x)
    half = (source // 8) % 2
    half = jnp.where(tile >= 32, 1 - half, half)
    orders = []
    for held_core in (core, 1 - core):
        node = NODES * ((half * 16 + place) * 2 + held_core) + inner
        hit = (node == target) & (inner < NODES)
        orders.append(jnp.where(hit, 1.0, 0.0).astype(jnp.bfloat16))
    return orders


def in_node_order(orders, pieces):
    total = None
    for order, piece in zip(orders, pieces):
        for _ in range(3):
            part = piece.astype(jnp.bfloat16)
            piece = piece - part.astype(jnp.float32)
            term = jnp.dot(order, part, preferred_element_type=jnp.float32)
            total = term if total is None else total + term
    return total


def pair_kernel(own_ref, other_ref, inverse_ref, work, panel):
    orders = node_orders("plane")
    for n in range(2):
        pieces = [ref[:, :, n].reshape(256, 512) for ref in (own_ref, other_ref)]
        work[n, :F, :] = in_node_order(orders, pieces)
        work[n, F:, :] = jnp.zeros((512 - F, 512), jnp.float32)

    def eliminate(block, height):
        at = pl.ds(pl.multiple_of(block * LANES, LANES), LANES)
        squares = [groups_of(work[n, at, at])[: height // 8] for n in range(2)]
        inverses = invert(squares)
        for n in range(2):
            square = jnp.concatenate(inverses[n], 0)
            if height < LANES:
                square = jnp.concatenate(
                    [square, jnp.zeros((LANES - height, LANES), jnp.float32)], 0
                )
            left = left_parts(work[n, :, at])
            scaled = split_matmul(left_parts(square), right_parts(work[n, at, :]))
            work[n, :, at] = jnp.zeros((512, LANES), jnp.float32)
            panel[n] = scaled
            panel[n, :, at] = square
            scaled = panel[n]
            work[n] = work[n] - split_matmul(left, right_parts(scaled))
            work[n, at, :] = scaled

    def step(block, carry):
        eliminate(block, LANES)
        return carry

    lax.fori_loop(0, 3, step, 0)
    eliminate(jnp.int32(3), F - 3 * LANES)
    inverse_ref[...] = work[:, :F, :]


def merge_kernel(
    own_ref,
    other_ref,
    inverse_ref,
    rows_ref,
    first_ref,
    second_ref,
    coupling,
    weighted,
    system,
    panel,
):
    tile = lax.axis_index("tile")
    box = lax.axis_index("box")
    source_box = tile // 16
    pair_slot = jnp.where(source_box // 2 == box // 2, 0, 1)
    side_slot = jnp.where(source_box % 2 == box % 2, 0, 1)
    orders = node_orders("y first")

    def ordered(index):
        pieces = [ref[:, :, index].reshape(256, 512) for ref in (own_ref, other_ref)]
        return in_node_order(orders, pieces)

    for pair in range(2):
        square = right_parts(
            jnp.concatenate([inverse_ref[pair], jnp.zeros((512 - F, 512), jnp.float32)], 0)
        )
        for side in range(2):
            at = pl.ds(side * F, F)
            left = left_parts(ordered(2 * pair + side))
            coupling[pair, at, :] = left
            weighted[pair, at, :] = right_parts(split_matmul(left, square), 1)

    for half in range(2):
        at = pl.ds(half * F, F)
        total = split_matmul_nt(coupling[0, at, :], weighted[0])
        system[at, :] = -total - split_matmul_nt(coupling[1, at, :], weighted[1])
    system[:F, :512] = system[:F, :512] + ordered(4)
    system[F : 2 * F, 384:] = system[F : 2 * F, 384:] + ordered(5)
    coupled = jnp.concatenate(
        [rows_ref[:, :, :F].reshape(LANES, F), jnp.zeros((LANES, 512 - F), jnp.float32)], 1
    )
    coupled_parts = left_parts(coupled)
    system[2 * F :, :] = -split_matmul_nt(coupled_parts, weighted[pair_slot])
    direct = rows_ref[:, :, F : 2 * F].reshape(LANES, F)
    gap = jnp.zeros((LANES, 512 - F), jnp.float32)

    @pl.when(side_slot == 0)
    def _():
        system[2 * F :, :512] = system[2 * F :, :512] + jnp.concatenate([direct, gap], 1)

    @pl.when(side_slot == 1)
    def _():
        system[2 * F :, 384:] = system[2 * F :, 384:] + jnp.concatenate([gap, direct], 1)

    def eliminate(block, carry):
        at = pl.ds(pl.multiple_of(block * LANES, LANES), LANES)
        square = jnp.concatenate(invert([groups_of(system[at, at])])[0], 0)
        scaled = split_matmul(left_parts(square), right_parts(system[at, :]))
        high, low = halves(scaled)
        panel[:LANES] = high
        panel[LANES : 2 * LANES] = low
        high, low = halves(-square)
        panel[:LANES, at] = high
        panel[LANES : 2 * LANES, at] = low
        panel[2 * LANES :] = panel[:LANES]

        def update(start, count):
            rows = pl.ds(pl.multiple_of(start * LANES, LANES), count * LANES)
            left = left_parts(system[rows, at])
            system[rows, at] = jnp.zeros((count * LANES, LANES), jnp.float32)
            system[rows, :] = system[rows, :] - split_matmul(left, panel[...])

        def pairwise(index, inner):
            update(6 - 2 * index, 2)
            return inner

        lax.fori_loop(0, (7 - block) // 2, pairwise, 0)

        @pl.when((7 - block) % 2 == 1)
        def _():
            update(block + 1, 1)

        return carry

    lax.fori_loop(0, 7, eliminate, 0)
    solved = system[2 * F :, :]
    same_pair = jnp.where(pair_slot == 0, 1.0, 0.0)
    square = right_parts(
        jnp.concatenate([inverse_ref[0], jnp.zeros((512 - F, 512), jnp.float32)], 0)
    )
    high = weighted[0, :, :512]
    low = weighted[0, :, 512:1024]
    first = same_pair * split_matmul(coupled_parts, square)
    first = first - split_matmul(left_parts(solved), jnp.concatenate([high, low, high], 0))
    first_ref[...] = first[:, :F]
    second_ref[...] = solved[:, :F]


def output_kernel(first_ref, second_ref, own_ref, other_ref, rows_ref, out_ref, spread):
    @pl.when(pl.program_id(0) == 0)
    def _():
        target = lax.broadcasted_iota(jnp.int32, (112, LANES), 0)
        source = lax.broadcasted_iota(jnp.int32, (112, LANES), 1)
        hit = (NODES * (source // 8) + source % 8 == target) & (source % 8 < NODES)
        compact = jnp.where(hit, 1.0, 0.0)
        orders = node_orders("x first")
        for index, ref in enumerate((first_ref, second_ref)):
            high, low = halves(matmul(compact, ref[...]))
            for place, order in enumerate(orders):
                for part, value in enumerate((high, high, low)):
                    moved = jnp.dot(value, order, preferred_element_type=jnp.float32)
                    spread[index, place, part] = moved.astype(jnp.bfloat16)

    target = lax.broadcasted_iota(jnp.int32, (112, LANES), 0)
    source = lax.broadcasted_iota(jnp.int32, (112, LANES), 1)
    hit = (NODES * (source // 8) + source % 8 == target) & (source % 8 < NODES)
    compact = jnp.where(hit, 1.0, 0.0)
    total = matmul(compact, rows_ref[...].reshape(LANES, -1))
    lefts = []
    rights = []
    for index in range(2):
        for place, ref in enumerate((own_ref, other_ref)):
            lefts += [spread[index, place, part] for part in range(3)]
            rights.append(right_parts(ref[:, :, index].reshape(256, -1)))
    total = total - split_matmul(jnp.concatenate(lefts, 1), jnp.concatenate(rights, 0))
    out_ref[...] = total


def select_kernel(slots_ref, stored_ref, mine_ref, shared_ref, goals_ref):
    box = lax.axis_index("box")
    along_x = box % 2
    along_y = box // 2
    x_shared = slots_ref[box, 1 - along_x]
    y_shared = slots_ref[box, 3 - along_y]
    finals = [
        slots_ref[box, along_x],
        slots_ref[box, 2 + along_y],
        slots_ref[box, 4],
        slots_ref[box, 5],
    ]
    lane = lax.broadcasted_iota(jnp.int32, (8, 512), 1)

    def block(row_slot, col_slot):
        start = pl.multiple_of(((col_slot * 7) // 2) * LANES, LANES)
        value = stored_ref[row_slot, :, pl.ds(start, 512)]
        value = jnp.concatenate([value, jnp.zeros((1, 512), jnp.float32)], 0)
        value = jnp.where(col_slot % 2 == 1, pltpu.roll(value, F, 1), value)
        return jnp.where(lane < F, value, 0.0)

    pieces = [(x_shared, x_shared), (y_shared, x_shared), (y_shared, y_shared)]
    for index, slots in enumerate(pieces):
        value = block(*slots)
        for copy in range(8):
            mine_ref[copy, index] = value
    for index, row_slot in enumerate((x_shared, y_shared)):
        for place, col_slot in enumerate(finals):
            shared_ref[index, :, place * F : place * F + F] = block(row_slot, col_slot)[:, :F]
    for index, row_slot in enumerate(finals):
        for place, col_slot in enumerate((x_shared, y_shared, *finals)):
            value = block(row_slot, col_slot)[:, :F]
            for goal in range(4):
                goals_ref[4 * index + goal, :, place * F : place * F + F] = value


def combine_kernel(line_ref, squares_ref, links_ref):
    box = lax.axis_index("box")
    z_half = lax.axis_index("tile") // 32
    along_x = box % 2
    pair = box - along_x
    for half in range(2):
        base = 4 * (z_half if half == 0 else 1 - z_half)
        mine, beside, other, across = (
            line_ref.at[base + place]
            for place in (
                box,
                pair + 1 - along_x,
                2 - pair + along_x,
                2 - pair + 1 - along_x,
            )
        )
        first = mine[0] + beside[0]
        second = other[0] + across[0]
        for copy in range(16):
            squares_ref[copy, half, 0] = first
            squares_ref[copy, half, 1] = second
        for index, ref in enumerate((mine, beside, other, across)):
            links_ref[half, index] = ref[1]
        links_ref[half, 4] = mine[2] + other[2]
        links_ref[half, 5] = pltpu.roll(beside[2] + across[2], 512 - F, 1)


def other_half(value, axis_part):
    flip = 32 if axis_part == "z" else 1
    return lax.ppermute(value, "tile", [(tile, tile ^ flip) for tile in range(64)])


def to_plane(copies):
    return lax.all_to_all(
        copies, "tile", split_axis=0, concat_axis=0, tiled=True, axis_index_groups=PLANES
    )


def ring_shift(value, axis_part, step):
    unit, length = {"x": (2, 4), "y": (8, 4)}[axis_part]
    pairs = []
    for tile in range(64):
        place = (tile // unit) % length
        pairs.append((tile, tile + ((place + step) % length - place) * unit))
    return lax.ppermute(value, "tile", pairs)


def ring_near(value, axis_part):
    return ring_shift(value, axis_part, 1), ring_shift(value, axis_part, -1)


def ring_far(before, after, axis_part, dim):
    return (
        ring_shift(lax.slice_in_dim(before, 0, 1, axis=dim), axis_part, 1),
        ring_shift(lax.slice_in_dim(after, 1, 2, axis=dim), axis_part, -1),
    )


def ring_stack(own, near, far, dim):
    return jnp.stack([own, *near, jnp.concatenate(far, dim)])


def kernel_call(body, out_shapes, name, micros, **options):
    return pl.pallas_call(
        body,
        out_shape=[jax.ShapeDtypeStruct(shape, jnp.float32) for shape in out_shapes],
        compiler_params=pltpu.CompilerParams(vmem_limit_bytes=VMEM_BYTES),
        cost_estimate=pl.CostEstimate(
            flops=micros * 10**9, bytes_accessed=10**6, transcendentals=0
        ),
        name=name,
        **options,
    )


def per_device(box_maps, face_slots):
    smem = pl.BlockSpec(memory_space=pltpu.SMEM)
    vmem = pl.BlockSpec(memory_space=pltpu.VMEM)
    mine, shared_rows, goals = kernel_call(
        select_kernel,
        [(8, 3, 8, 512), (2, 8, 4 * F), (16, 8, 6 * F)],
        "select_rows",
        2,
        in_specs=[smem, vmem],
        out_specs=[vmem] * 3,
    )(face_slots, box_maps[0])
    spread = [
        (64 * box + 16 * quarter + 4 * face + goal, 64 * goal + 16 * box + 4 * face + quarter)
        for box in range(4)
        for quarter in range(4)
        for face in range(4)
        for goal in range(4)
    ]

    line = lax.all_to_all(
        mine, ("box", "tile"), split_axis=0, concat_axis=0, tiled=True, axis_index_groups=LINES
    )
    shared_far = other_half(shared_rows, "z")
    line, shared_far = lax.optimization_barrier((line, shared_far))

    squares, links = kernel_call(
        combine_kernel,
        [(16, 2, 2, 8, 512), (2, 6, 8, 512)],
        "combine_boxes",
        1,
        in_specs=[vmem],
        out_specs=[vmem] * 2,
    )(line)
    columns = jnp.stack([shared_rows, shared_far])
    columns_near = ring_near(columns, "y")
    links_near = ring_near(links, "x")
    squares_own = to_plane(squares)
    squares_own, columns_near, links_near, goals = lax.optimization_barrier(
        (squares_own, columns_near, links_near, goals)
    )
    row_goals = lax.all_to_all(
        goals, "tile", split_axis=0, concat_axis=0, tiled=True, axis_index_groups=QUARTERS
    )

    squares_other = other_half(squares_own, "core")
    columns_far = ring_far(*columns_near, "y", 0)
    links_far = ring_far(*links_near, "x", 0)
    squares_other, columns_far, links_far = lax.optimization_barrier(
        (squares_other, columns_far, links_far)
    )

    columns = ring_stack(columns, columns_near, columns_far, 0)
    links = ring_stack(links, links_near, links_far, 0)
    columns_near = ring_near(columns, "x")
    links_near = ring_near(links, "y")
    (inverse,) = kernel_call(
        pair_kernel,
        [(2, F, 512)],
        "invert_pairs",
        20,
        in_specs=[vmem] * 2,
        out_specs=[vmem],
        scratch_shapes=[
            pltpu.VMEM((2, 512, 512), jnp.float32),
            pltpu.VMEM((2, LANES, 512), jnp.float32),
        ],
    )(squares_own, squares_other)
    inverse, columns_near, links_near, row_goals = lax.optimization_barrier(
        (inverse, columns_near, links_near, row_goals)
    )
    row_parts = lax.ppermute(row_goals[:, :, : 2 * F], ("box", "tile"), spread)
    links_far = ring_far(*links_near, "y", 1)
    links_far, columns_near = lax.optimization_barrier((links_far, columns_near))
    columns_far = ring_far(*columns_near, "x", 1)
    links_own = ring_stack(links, links_near, links_far, 1).reshape(16, 2, 6, 8, 512)
    links_other = other_half(links_own, "core")
    links_other, columns_far = lax.optimization_barrier((links_other, columns_far))
    columns_own = ring_stack(columns, columns_near, columns_far, 1).reshape(16, 2, 2, 8, 4 * F)
    columns_other = other_half(columns_own, "core")
    own_rows = lax.ppermute(
        row_goals[:, :, 2 * F :],
        ("box", "tile"),
        [pair for pair in spread if pair[0] // 64 == pair[1] // 64],
    )
    first, second = kernel_call(
        merge_kernel,
        [(LANES, F)] * 2,
        "merge_pairs",
        45,
        in_specs=[vmem] * 4,
        out_specs=[vmem] * 2,
        scratch_shapes=[
            pltpu.VMEM((2, 2 * F, 3 * 512), jnp.bfloat16),
            pltpu.VMEM((2, 2 * F, 3 * 512), jnp.bfloat16),
            pltpu.VMEM((2 * F + LANES, 2 * F), jnp.float32),
            pltpu.VMEM((3 * LANES, 2 * F), jnp.bfloat16),
        ],
    )(links_own, links_other, inverse, row_parts)
    (out,) = kernel_call(
        output_kernel,
        [(112, 4 * F)],
        "final_map",
        6,
        grid=(7,),
        in_specs=[
            pl.BlockSpec((LANES, F), lambda i: (0, 0)),
            pl.BlockSpec((LANES, F), lambda i: (0, 0)),
            pl.BlockSpec((16, 2, 2, 8, 256), lambda i: (0, 0, 0, 0, i)),
            pl.BlockSpec((16, 2, 2, 8, 256), lambda i: (0, 0, 0, 0, i)),
            pl.BlockSpec((16, 8, 256), lambda i: (0, 0, i)),
        ],
        out_specs=[pl.BlockSpec((112, 256), lambda i: (0, i))],
        scratch_shapes=[pltpu.VMEM((2, 2, 3, 112, 256), jnp.bfloat16)],
    )(first, second, columns_own, columns_other, own_rows)
    return out


def solution(mesh):
    return jax.shard_map(
        per_device,
        mesh=mesh,
        in_specs=(P("box", None, "tile", None), P()),
        out_specs=P("tile", "box"),
        check_vma=False,
    )
```

```python
import functools

import jax
import jax.numpy as jnp
from jax import lax
from jax.experimental import pallas as pl
from jax.experimental.pallas import tpu as pltpu
from jax.sharding import PartitionSpec as P

F = 448
NODES = 7
LANES = 128
MICRO = 16
VMEM_BYTES = 56 * 1024 * 1024


def tile_of(z, y, x, core):
    return ((z * 4 + y) * 4 + x) * 2 + core


PLANES = [
    [tile_of(z, y, x, core) for y in range(4) for x in range(4)]
    for z in range(2)
    for core in range(2)
]
LINES = [
    [64 * box + 32 * half + tile for half in range(2) for box in range(4)] for tile in range(32)
]
QUARTERS = [[16 * quarter + own for own in range(16)] for quarter in range(4)]


def matmul(left, right):
    return jnp.dot(left, right, precision=lax.Precision.HIGHEST, preferred_element_type=jnp.float32)


def halves(value):
    high = value.astype(jnp.bfloat16)
    return high, (value - high.astype(jnp.float32)).astype(jnp.bfloat16)


def left_parts(value):
    high, low = halves(value)
    return jnp.concatenate([high, high, low], 1)


def right_parts(value, dim=0):
    high, low = halves(value)
    return jnp.concatenate([high, low, high], dim)


def split_matmul(left, right):
    return jnp.dot(left, right, preferred_element_type=jnp.float32)


def split_matmul_nt(left, right):
    return lax.dot_general(
        left, right, (((1,), (1,)), ((), ())), preferred_element_type=jnp.float32
    )


def invert(stack):
    full = (8, LANES)
    lane = lax.broadcasted_iota(jnp.int32, full, 1)
    sub = lax.broadcasted_iota(jnp.int32, full, 0)

    def along_rows(value, row):
        return jnp.broadcast_to(value[row : row + 1, :], full)

    def along_lanes(value, column):
        return jnp.broadcast_to(value[:, column : column + 1], full)

    stack = [list(rows) for rows in stack]
    count = len(stack[0])
    which = range(len(stack))
    for start in range(0, 8 * count, MICRO):
        first = start // 8
        inside = (lane >= start) & (lane < start + MICRO)
        following = [group for group in (first + 2, first + 3) if group < count]
        rest = [g for g in range(count) if g not in (first, first + 1, *following)]
        pivots = [
            [[along_lanes(stack[n][first + h], start + k) for h in range(2)] for k in range(MICRO)]
            for n in which
        ]
        rows = [
            [
                jnp.where(
                    inside,
                    jnp.where(lane == start + 8 * h + sub, 1.0, 0.0),
                    stack[n][first + h],
                )
                for h in range(2)
            ]
            for n in which
        ]
        ahead = [
            [[along_lanes(stack[n][group], start + k) for k in range(MICRO)] for group in following]
            for n in which
        ]
        for j in range(MICRO):
            half, row = divmod(j, 8)
            chosen = sub == row
            for n in which:
                scale = 1.0 / along_rows(pivots[n][j][half], row)
                pivot_row = along_rows(rows[n][half], row) * scale
                for k in range(j + 1, MICRO):
                    scaled = along_rows(pivots[n][k][half], row) * scale
                    for h in range(2):
                        value = pivots[n][k][h] - pivots[n][j][h] * scaled
                        pivots[n][k][h] = jnp.where(chosen, scaled, value) if h == half else value
                for h in range(2):
                    value = rows[n][h] - pivots[n][j][h] * pivot_row
                    rows[n][h] = jnp.where(chosen, pivot_row, value) if h == half else value
        for n in which:
            spread = [along_rows(rows[n][k // 8], k % 8) for k in range(MICRO)]
            for position, group in enumerate(following):
                terms = [ahead[n][position][k] * spread[k] for k in range(MICRO)]
                while len(terms) > 1:
                    terms = [terms[i] + terms[i + 1] for i in range(0, len(terms), 2)]
                stack[n][group] = jnp.where(inside, 0.0, stack[n][group]) - terms[0]
            if rest:
                zero = jnp.zeros(full, jnp.float32)
                held = jnp.concatenate([stack[n][group] for group in rest], 0)
                panel = jnp.concatenate(
                    [zero] * first + rows[n] + [zero] * (LANES // 8 - first - 2), 0
                )
                update = matmul(held, panel)
                for i, group in enumerate(rest):
                    stack[n][group] = (
                        jnp.where(inside, 0.0, stack[n][group]) - update[8 * i : 8 * i + 8]
                    )
            stack[n][first], stack[n][first + 1] = rows[n]
    return stack


def groups_of(value):
    return [value[8 * g : 8 * g + 8, :] for g in range(value.shape[0] // 8)]


def node_orders(layout):
    tile = lax.axis_index("tile")
    core = tile % 2
    shape = (F, 256)
    target = lax.broadcasted_iota(jnp.int32, shape, 0)
    source = lax.broadcasted_iota(jnp.int32, shape, 1)
    inner = source % 8
    place = source // 16
    if layout != "plane":
        in_y, in_x = place // 4, place % 4
        if layout == "x first":
            in_y, in_x = in_x, in_y

        def moved(start, step):
            far = jnp.where(step == 3, 2, 0)
            return (start + jnp.where(step == 1, 3, jnp.where(step == 2, 1, far))) % 4

        place = moved((tile // 8) % 4, in_y) * 4 + moved((tile // 2) % 4, in_x)
    half = (source // 8) % 2
    half = jnp.where(tile >= 32, 1 - half, half)
    orders = []
    for held_core in (core, 1 - core):
        node = NODES * ((half * 16 + place) * 2 + held_core) + inner
        hit = (node == target) & (inner < NODES)
        orders.append(jnp.where(hit, 1.0, 0.0).astype(jnp.bfloat16))
    return orders


def in_node_order(orders, pieces):
    total = None
    for order, piece in zip(orders, pieces):
        for _ in range(3):
            part = piece.astype(jnp.bfloat16)
            piece = piece - part.astype(jnp.float32)
            term = jnp.dot(order, part, preferred_element_type=jnp.float32)
            total = term if total is None else total + term
    return total


def pair_kernel(own_ref, other_ref, inverse_ref, work, panel):
    orders = node_orders("plane")
    for n in range(2):
        pieces = [ref[:, :, n].reshape(256, 512) for ref in (own_ref, other_ref)]
        work[n, :F, :] = in_node_order(orders, pieces)
        work[n, F:, :] = jnp.zeros((512 - F, 512), jnp.float32)

    def eliminate(block, height):
        at = pl.ds(pl.multiple_of(block * LANES, LANES), LANES)
        squares = [groups_of(work[n, at, at])[: height // 8] for n in range(2)]
        inverses = invert(squares)
        for n in range(2):
            square = jnp.concatenate(inverses[n], 0)
            if height < LANES:
                square = jnp.concatenate(
                    [square, jnp.zeros((LANES - height, LANES), jnp.float32)], 0
                )
            left = left_parts(work[n, :, at])
            scaled = split_matmul(left_parts(square), right_parts(work[n, at, :]))
            work[n, :, at] = jnp.zeros((512, LANES), jnp.float32)
            panel[n] = scaled
            panel[n, :, at] = square
            scaled = panel[n]
            work[n] = work[n] - split_matmul(left, right_parts(scaled))
            work[n, at, :] = scaled

    def step(block, carry):
        eliminate(block, LANES)
        return carry

    lax.fori_loop(0, 3, step, 0)
    eliminate(jnp.int32(3), F - 3 * LANES)
    inverse_ref[...] = work[:, :F, :]


def merge_kernel(
    own_ref,
    other_ref,
    inverse_ref,
    rows_ref,
    first_ref,
    second_ref,
    coupling,
    weighted,
    system,
    panel,
):
    tile = lax.axis_index("tile")
    box = lax.axis_index("box")
    source_box = tile // 16
    pair_slot = jnp.where(source_box // 2 == box // 2, 0, 1)
    side_slot = jnp.where(source_box % 2 == box % 2, 0, 1)
    orders = node_orders("y first")

    def ordered(index):
        pieces = [ref[:, :, index].reshape(256, 512) for ref in (own_ref, other_ref)]
        return in_node_order(orders, pieces)

    for pair in range(2):
        square = right_parts(
            jnp.concatenate([inverse_ref[pair], jnp.zeros((512 - F, 512), jnp.float32)], 0)
        )
        for side in range(2):
            at = pl.ds(side * F, F)
            left = left_parts(ordered(2 * pair + side))
            coupling[pair, at, :] = left
            weighted[pair, at, :] = right_parts(split_matmul(left, square), 1)

    for half in range(2):
        at = pl.ds(half * F, F)
        total = split_matmul_nt(coupling[0, at, :], weighted[0])
        system[at, :] = -total - split_matmul_nt(coupling[1, at, :], weighted[1])
    system[:F, :512] = system[:F, :512] + ordered(4)
    system[F : 2 * F, 384:] = system[F : 2 * F, 384:] + ordered(5)
    coupled = jnp.concatenate(
        [rows_ref[:, :, :F].reshape(LANES, F), jnp.zeros((LANES, 512 - F), jnp.float32)], 1
    )
    coupled_parts = left_parts(coupled)
    system[2 * F :, :] = -split_matmul_nt(coupled_parts, weighted[pair_slot])
    direct = rows_ref[:, :, F : 2 * F].reshape(LANES, F)
    gap = jnp.zeros((LANES, 512 - F), jnp.float32)

    @pl.when(side_slot == 0)
    def _():
        system[2 * F :, :512] = system[2 * F :, :512] + jnp.concatenate([direct, gap], 1)

    @pl.when(side_slot == 1)
    def _():
        system[2 * F :, 384:] = system[2 * F :, 384:] + jnp.concatenate([gap, direct], 1)

    def eliminate(block, carry):
        at = pl.ds(pl.multiple_of(block * LANES, LANES), LANES)
        square = jnp.concatenate(invert([groups_of(system[at, at])])[0], 0)
        scaled = split_matmul(left_parts(square), right_parts(system[at, :]))
        high, low = halves(scaled)
        panel[:LANES] = high
        panel[LANES : 2 * LANES] = low
        high, low = halves(-square)
        panel[:LANES, at] = high
        panel[LANES : 2 * LANES, at] = low
        panel[2 * LANES :] = panel[:LANES]

        def update(start, count):
            rows = pl.ds(pl.multiple_of(start * LANES, LANES), count * LANES)
            left = left_parts(system[rows, at])
            system[rows, at] = jnp.zeros((count * LANES, LANES), jnp.float32)
            system[rows, :] = system[rows, :] - split_matmul(left, panel[...])

        def pairwise(index, inner):
            update(6 - 2 * index, 2)
            return inner

        lax.fori_loop(0, (7 - block) // 2, pairwise, 0)

        @pl.when((7 - block) % 2 == 1)
        def _():
            update(block + 1, 1)

        return carry

    lax.fori_loop(0, 7, eliminate, 0)
    solved = system[2 * F :, :]
    same_pair = jnp.where(pair_slot == 0, 1.0, 0.0)
    square = right_parts(
        jnp.concatenate([inverse_ref[0], jnp.zeros((512 - F, 512), jnp.float32)], 0)
    )
    high = weighted[0, :, :512]
    low = weighted[0, :, 512:1024]
    first = same_pair * split_matmul(coupled_parts, square)
    first = first - split_matmul(left_parts(solved), jnp.concatenate([high, low, high], 0))
    first_ref[...] = first[:, :F]
    second_ref[...] = solved[:, :F]


def output_kernel(first_ref, second_ref, own_ref, other_ref, rows_ref, out_ref, spread):
    @pl.when(pl.program_id(0) == 0)
    def _():
        target = lax.broadcasted_iota(jnp.int32, (112, LANES), 0)
        source = lax.broadcasted_iota(jnp.int32, (112, LANES), 1)
        hit = (NODES * (source // 8) + source % 8 == target) & (source % 8 < NODES)
        compact = jnp.where(hit, 1.0, 0.0)
        orders = node_orders("x first")
        for index, ref in enumerate((first_ref, second_ref)):
            high, low = halves(matmul(compact, ref[...]))
            for place, order in enumerate(orders):
                for part, value in enumerate((high, high, low)):
                    moved = jnp.dot(value, order, preferred_element_type=jnp.float32)
                    spread[index, place, part] = moved.astype(jnp.bfloat16)

    target = lax.broadcasted_iota(jnp.int32, (112, LANES), 0)
    source = lax.broadcasted_iota(jnp.int32, (112, LANES), 1)
    hit = (NODES * (source // 8) + source % 8 == target) & (source % 8 < NODES)
    compact = jnp.where(hit, 1.0, 0.0)
    total = matmul(compact, rows_ref[...].reshape(LANES, -1))
    lefts = []
    rights = []
    for index in range(2):
        for place, ref in enumerate((own_ref, other_ref)):
            lefts += [spread[index, place, part] for part in range(3)]
            rights.append(right_parts(ref[:, :, index].reshape(256, -1)))
    total = total - split_matmul(jnp.concatenate(lefts, 1), jnp.concatenate(rights, 0))
    out_ref[...] = total


def select_kernel(slots_ref, stored_ref, mine_ref, shared_ref, goals_ref):
    box = lax.axis_index("box")
    along_x = box % 2
    along_y = box // 2
    x_shared = slots_ref[box, 1 - along_x]
    y_shared = slots_ref[box, 3 - along_y]
    finals = [
        slots_ref[box, along_x],
        slots_ref[box, 2 + along_y],
        slots_ref[box, 4],
        slots_ref[box, 5],
    ]
    lane = lax.broadcasted_iota(jnp.int32, (8, 512), 1)

    def block(row_slot, col_slot):
        start = pl.multiple_of(((col_slot * 7) // 2) * LANES, LANES)
        value = stored_ref[row_slot, :, pl.ds(start, 512)]
        value = jnp.concatenate([value, jnp.zeros((1, 512), jnp.float32)], 0)
        value = jnp.where(col_slot % 2 == 1, pltpu.roll(value, F, 1), value)
        return jnp.where(lane < F, value, 0.0)

    pieces = [(x_shared, x_shared), (y_shared, x_shared), (y_shared, y_shared)]
    for index, slots in enumerate(pieces):
        value = block(*slots)
        for copy in range(8):
            mine_ref[copy, index] = value
    for index, row_slot in enumerate((x_shared, y_shared)):
        for place, col_slot in enumerate(finals):
            shared_ref[index, :, place * F : place * F + F] = block(row_slot, col_slot)[:, :F]
    for index, row_slot in enumerate(finals):
        for place, col_slot in enumerate((x_shared, y_shared, *finals)):
            value = block(row_slot, col_slot)[:, :F]
            for goal in range(4):
                goals_ref[4 * index + goal, :, place * F : place * F + F] = value


def combine_kernel(line_ref, squares_ref, links_ref):
    box = lax.axis_index("box")
    z_half = lax.axis_index("tile") // 32
    along_x = box % 2
    pair = box - along_x
    for half in range(2):
        base = 4 * (z_half if half == 0 else 1 - z_half)
        mine, beside, other, across = (
            line_ref.at[base + place]
            for place in (
                box,
                pair + 1 - along_x,
                2 - pair + along_x,
                2 - pair + 1 - along_x,
            )
        )
        first = mine[0] + beside[0]
        second = other[0] + across[0]
        for copy in range(16):
            squares_ref[copy, half, 0] = first
            squares_ref[copy, half, 1] = second
        for index, ref in enumerate((mine, beside, other, across)):
            links_ref[half, index] = ref[1]
        links_ref[half, 4] = mine[2] + other[2]
        links_ref[half, 5] = pltpu.roll(beside[2] + across[2], 512 - F, 1)


def other_half(value, axis_part):
    flip = 32 if axis_part == "z" else 1
    return lax.ppermute(value, "tile", [(tile, tile ^ flip) for tile in range(64)])


def to_plane(copies):
    return lax.all_to_all(
        copies, "tile", split_axis=0, concat_axis=0, tiled=True, axis_index_groups=PLANES
    )


def ring_shift(value, axis_part, step):
    unit, length = {"x": (2, 4), "y": (8, 4)}[axis_part]
    pairs = []
    for tile in range(64):
        place = (tile // unit) % length
        pairs.append((tile, tile + ((place + step) % length - place) * unit))
    return lax.ppermute(value, "tile", pairs)


def ring_near(value, axis_part):
    return ring_shift(value, axis_part, 1), ring_shift(value, axis_part, -1)


def ring_far(before, after, axis_part, dim):
    return (
        ring_shift(lax.slice_in_dim(before, 0, 1, axis=dim), axis_part, 1),
        ring_shift(lax.slice_in_dim(after, 1, 2, axis=dim), axis_part, -1),
    )


def ring_stack(own, near, far, dim):
    return jnp.stack([own, *near, jnp.concatenate(far, dim)])


def kernel_call(body, out_shapes, name, micros, **options):
    return pl.pallas_call(
        body,
        out_shape=[jax.ShapeDtypeStruct(shape, jnp.float32) for shape in out_shapes],
        compiler_params=pltpu.CompilerParams(vmem_limit_bytes=VMEM_BYTES),
        cost_estimate=pl.CostEstimate(
            flops=micros * 10**9, bytes_accessed=10**6, transcendentals=0
        ),
        name=name,
        **options,
    )


def per_device(box_maps, face_slots):
    smem = pl.BlockSpec(memory_space=pltpu.SMEM)
    vmem = pl.BlockSpec(memory_space=pltpu.VMEM)
    mine, shared_rows, goals = kernel_call(
        select_kernel,
        [(8, 3, 8, 512), (2, 8, 4 * F), (16, 8, 6 * F)],
        "select_rows",
        2,
        in_specs=[smem, vmem],
        out_specs=[vmem] * 3,
    )(face_slots, box_maps[0])
    spread = [
        (64 * box + 16 * quarter + 4 * face + goal, 64 * goal + 16 * box + 4 * face + quarter)
        for box in range(4)
        for quarter in range(4)
        for face in range(4)
        for goal in range(4)
    ]

    line = lax.all_to_all(
        mine, ("box", "tile"), split_axis=0, concat_axis=0, tiled=True, axis_index_groups=LINES
    )
    shared_far = other_half(shared_rows, "z")

    squares, links = kernel_call(
        combine_kernel,
        [(16, 2, 2, 8, 512), (2, 6, 8, 512)],
        "combine_boxes",
        1,
        in_specs=[vmem],
        out_specs=[vmem] * 2,
    )(line)
    columns = jnp.stack([shared_rows, shared_far])
    columns_near = ring_near(columns, "y")
    links_near = ring_near(links, "x")
    squares_own = to_plane(squares)
    squares_own, columns_near, links_near, goals = lax.optimization_barrier(
        (squares_own, columns_near, links_near, goals)
    )
    row_goals = lax.all_to_all(
        goals, "tile", split_axis=0, concat_axis=0, tiled=True, axis_index_groups=QUARTERS
    )

    squares_other = other_half(squares_own, "core")
    columns_far = ring_far(*columns_near, "y", 0)
    links_far = ring_far(*links_near, "x", 0)
    squares_other, columns_far, links_far = lax.optimization_barrier(
        (squares_other, columns_far, links_far)
    )

    columns = ring_stack(columns, columns_near, columns_far, 0)
    links = ring_stack(links, links_near, links_far, 0)
    columns_near = ring_near(columns, "x")
    links_near = ring_near(links, "y")
    (inverse,) = kernel_call(
        pair_kernel,
        [(2, F, 512)],
        "invert_pairs",
        20,
        in_specs=[vmem] * 2,
        out_specs=[vmem],
        scratch_shapes=[
            pltpu.VMEM((2, 512, 512), jnp.float32),
            pltpu.VMEM((2, LANES, 512), jnp.float32),
        ],
    )(squares_own, squares_other)
    inverse, columns_near, links_near, row_goals = lax.optimization_barrier(
        (inverse, columns_near, links_near, row_goals)
    )
    row_parts = lax.ppermute(row_goals[:, :, : 2 * F], ("box", "tile"), spread)
    links_far = ring_far(*links_near, "y", 1)
    columns_far = ring_far(*columns_near, "x", 1)
    links_far, columns_far, row_parts = lax.optimization_barrier(
        (links_far, columns_far, row_parts)
    )
    links_own = ring_stack(links, links_near, links_far, 1).reshape(16, 2, 6, 8, 512)
    links_other = other_half(links_own, "core")
    links_other, row_goals = lax.optimization_barrier((links_other, row_goals))
    columns_own = ring_stack(columns, columns_near, columns_far, 1).reshape(16, 2, 2, 8, 4 * F)
    columns_other = other_half(columns_own, "core")
    own_rows = lax.ppermute(
        row_goals[:, :, 2 * F :],
        ("box", "tile"),
        [pair for pair in spread if pair[0] // 64 == pair[1] // 64],
    )
    first, second = kernel_call(
        merge_kernel,
        [(LANES, F)] * 2,
        "merge_pairs",
        45,
        in_specs=[vmem] * 4,
        out_specs=[vmem] * 2,
        scratch_shapes=[
            pltpu.VMEM((2, 2 * F, 3 * 512), jnp.bfloat16),
            pltpu.VMEM((2, 2 * F, 3 * 512), jnp.bfloat16),
            pltpu.VMEM((2 * F + LANES, 2 * F), jnp.float32),
            pltpu.VMEM((3 * LANES, 2 * F), jnp.bfloat16),
        ],
    )(links_own, links_other, inverse, row_parts)
    (out,) = kernel_call(
        output_kernel,
        [(112, 4 * F)],
        "final_map",
        6,
        grid=(7,),
        in_specs=[
            pl.BlockSpec((LANES, F), lambda i: (0, 0)),
            pl.BlockSpec((LANES, F), lambda i: (0, 0)),
            pl.BlockSpec((16, 2, 2, 8, 256), lambda i: (0, 0, 0, 0, i)),
            pl.BlockSpec((16, 2, 2, 8, 256), lambda i: (0, 0, 0, 0, i)),
            pl.BlockSpec((16, 8, 256), lambda i: (0, 0, i)),
        ],
        out_specs=[pl.BlockSpec((112, 256), lambda i: (0, i))],
        scratch_shapes=[pltpu.VMEM((2, 2, 3, 112, 256), jnp.bfloat16)],
    )(first, second, columns_own, columns_other, own_rows)
    return out


def solution(mesh):
    return jax.shard_map(
        per_device,
        mesh=mesh,
        in_specs=(P("box", None, "tile", None), P()),
        out_specs=P("tile", "box"),
        check_vma=False,
    )
```

```python
import functools

import jax
import jax.numpy as jnp
from jax import lax
from jax.experimental import pallas as pl
from jax.experimental.pallas import tpu as pltpu
from jax.sharding import PartitionSpec as P

F = 448
NODES = 7
LANES = 128
MICRO = 16
VMEM_BYTES = 32 * 1024 * 1024


def tile_of(z, y, x, core):
    return ((z * 4 + y) * 4 + x) * 2 + core


PLANES = [
    [tile_of(z, y, x, core) for y in range(4) for x in range(4)]
    for z in range(2)
    for core in range(2)
]
LINES = [
    [64 * box + 32 * half + tile for half in range(2) for box in range(4)] for tile in range(32)
]
QUARTERS = [[16 * quarter + own for own in range(16)] for quarter in range(4)]


def matmul(left, right):
    return jnp.dot(left, right, precision=lax.Precision.HIGHEST, preferred_element_type=jnp.float32)


def halves(value):
    high = value.astype(jnp.bfloat16)
    return high, (value - high.astype(jnp.float32)).astype(jnp.bfloat16)


def left_parts(value):
    high, low = halves(value)
    return jnp.concatenate([high, high, low], 1)


def right_parts(value, dim=0):
    high, low = halves(value)
    return jnp.concatenate([high, low, high], dim)


def split_matmul(left, right):
    return jnp.dot(left, right, preferred_element_type=jnp.float32)


def split_matmul_nt(left, right):
    return lax.dot_general(
        left, right, (((1,), (1,)), ((), ())), preferred_element_type=jnp.float32
    )


def invert(stack):
    full = (8, LANES)
    lane = lax.broadcasted_iota(jnp.int32, full, 1)
    sub = lax.broadcasted_iota(jnp.int32, full, 0)

    def along_rows(value, row):
        return jnp.broadcast_to(value[row : row + 1, :], full)

    def along_lanes(value, column):
        return jnp.broadcast_to(value[:, column : column + 1], full)

    stack = [list(rows) for rows in stack]
    count = len(stack[0])
    which = range(len(stack))
    for start in range(0, 8 * count, MICRO):
        first = start // 8
        inside = (lane >= start) & (lane < start + MICRO)
        following = [group for group in (first + 2, first + 3) if group < count]
        rest = [g for g in range(count) if g not in (first, first + 1, *following)]
        pivots = [
            [[along_lanes(stack[n][first + h], start + k) for h in range(2)] for k in range(MICRO)]
            for n in which
        ]
        rows = [
            [
                jnp.where(
                    inside,
                    jnp.where(lane == start + 8 * h + sub, 1.0, 0.0),
                    stack[n][first + h],
                )
                for h in range(2)
            ]
            for n in which
        ]
        ahead = [
            [[along_lanes(stack[n][group], start + k) for k in range(MICRO)] for group in following]
            for n in which
        ]
        for j in range(MICRO):
            half, row = divmod(j, 8)
            chosen = sub == row
            for n in which:
                scale = 1.0 / along_rows(pivots[n][j][half], row)
                pivot_row = along_rows(rows[n][half], row) * scale
                for k in range(j + 1, MICRO):
                    scaled = along_rows(pivots[n][k][half], row) * scale
                    for h in range(2):
                        value = pivots[n][k][h] - pivots[n][j][h] * scaled
                        pivots[n][k][h] = jnp.where(chosen, scaled, value) if h == half else value
                for h in range(2):
                    value = rows[n][h] - pivots[n][j][h] * pivot_row
                    rows[n][h] = jnp.where(chosen, pivot_row, value) if h == half else value
        for n in which:
            spread = [along_rows(rows[n][k // 8], k % 8) for k in range(MICRO)]
            for position, group in enumerate(following):
                terms = [ahead[n][position][k] * spread[k] for k in range(MICRO)]
                while len(terms) > 1:
                    terms = [terms[i] + terms[i + 1] for i in range(0, len(terms), 2)]
                stack[n][group] = jnp.where(inside, 0.0, stack[n][group]) - terms[0]
            if rest:
                zero = jnp.zeros(full, jnp.float32)
                held = jnp.concatenate([stack[n][group] for group in rest], 0)
                panel = jnp.concatenate(
                    [zero] * first + rows[n] + [zero] * (LANES // 8 - first - 2), 0
                )
                update = matmul(held, panel)
                for i, group in enumerate(rest):
                    stack[n][group] = (
                        jnp.where(inside, 0.0, stack[n][group]) - update[8 * i : 8 * i + 8]
                    )
            stack[n][first], stack[n][first + 1] = rows[n]
    return stack


def groups_of(value):
    return [value[8 * g : 8 * g + 8, :] for g in range(value.shape[0] // 8)]


def node_orders(layout):
    tile = lax.axis_index("tile")
    core = tile % 2
    shape = (F, 256)
    target = lax.broadcasted_iota(jnp.int32, shape, 0)
    source = lax.broadcasted_iota(jnp.int32, shape, 1)
    inner = source % 8
    place = source // 16
    if layout != "plane":
        in_y, in_x = place // 4, place % 4
        if layout == "x first":
            in_y, in_x = in_x, in_y

        def moved(start, step):
            far = jnp.where(step == 3, 2, 0)
            return (start + jnp.where(step == 1, 3, jnp.where(step == 2, 1, far))) % 4

        place = moved((tile // 8) % 4, in_y) * 4 + moved((tile // 2) % 4, in_x)
    half = (source // 8) % 2
    half = jnp.where(tile >= 32, 1 - half, half)
    orders = []
    for held_core in (core, 1 - core):
        node = NODES * ((half * 16 + place) * 2 + held_core) + inner
        hit = (node == target) & (inner < NODES)
        orders.append(jnp.where(hit, 1.0, 0.0).astype(jnp.bfloat16))
    return orders


def in_node_order(orders, pieces):
    total = None
    for order, piece in zip(orders, pieces):
        for _ in range(3):
            part = piece.astype(jnp.bfloat16)
            piece = piece - part.astype(jnp.float32)
            term = jnp.dot(order, part, preferred_element_type=jnp.float32)
            total = term if total is None else total + term
    return total


def pair_kernel(own_ref, other_ref, inverse_ref, work, panel):
    orders = node_orders("plane")
    for n in range(2):
        pieces = [ref[:, :, n].reshape(256, 512) for ref in (own_ref, other_ref)]
        work[n, :F, :] = in_node_order(orders, pieces)
        work[n, F:, :] = jnp.zeros((512 - F, 512), jnp.float32)

    def eliminate(block, height):
        at = pl.ds(pl.multiple_of(block * LANES, LANES), LANES)
        squares = [groups_of(work[n, at, at])[: height // 8] for n in range(2)]
        inverses = invert(squares)
        for n in range(2):
            square = jnp.concatenate(inverses[n], 0)
            if height < LANES:
                square = jnp.concatenate(
                    [square, jnp.zeros((LANES - height, LANES), jnp.float32)], 0
                )
            left = left_parts(work[n, :, at])
            scaled = split_matmul(left_parts(square), right_parts(work[n, at, :]))
            work[n, :, at] = jnp.zeros((512, LANES), jnp.float32)
            panel[n] = scaled
            panel[n, :, at] = square
            scaled = panel[n]
            work[n] = work[n] - split_matmul(left, right_parts(scaled))
            work[n, at, :] = scaled

    def step(block, carry):
        eliminate(block, LANES)
        return carry

    lax.fori_loop(0, 3, step, 0)
    eliminate(jnp.int32(3), F - 3 * LANES)
    inverse_ref[...] = work[:, :F, :]


def build_kernel(own_ref, other_ref, inverse_ref, system, weighted, coupling):
    orders = node_orders("y first")

    def ordered(index):
        pieces = [ref[:, :, index].reshape(256, 512) for ref in (own_ref, other_ref)]
        return in_node_order(orders, pieces)

    for pair in range(2):
        square = right_parts(
            jnp.concatenate([inverse_ref[pair], jnp.zeros((512 - F, 512), jnp.float32)], 0)
        )
        for side in range(2):
            at = pl.ds(side * F, F)
            left = left_parts(ordered(2 * pair + side))
            coupling[pair, at, :] = left
            weighted[pair, at, :] = right_parts(split_matmul(left, square), 1)

    for half in range(2):
        at = pl.ds(half * F, F)
        total = split_matmul_nt(coupling[0, at, :], weighted[0])
        system[at, :] = -total - split_matmul_nt(coupling[1, at, :], weighted[1])
    system[:F, :512] = system[:F, :512] + ordered(4)
    system[F : 2 * F, 384:] = system[F : 2 * F, 384:] + ordered(5)


def merge_kernel(
    built_ref, weighted, inverse_ref, rows_ref, first_ref, second_ref, system, panel
):
    tile = lax.axis_index("tile")
    box = lax.axis_index("box")
    source_box = tile // 16
    pair_slot = jnp.where(source_box // 2 == box // 2, 0, 1)
    side_slot = jnp.where(source_box % 2 == box % 2, 0, 1)
    system[: 2 * F, :] = built_ref[...]
    coupled = jnp.concatenate(
        [rows_ref[:, :, :F].reshape(LANES, F), jnp.zeros((LANES, 512 - F), jnp.float32)], 1
    )
    coupled_parts = left_parts(coupled)
    system[2 * F :, :] = -split_matmul_nt(coupled_parts, weighted[pair_slot])
    direct = rows_ref[:, :, F : 2 * F].reshape(LANES, F)
    gap = jnp.zeros((LANES, 512 - F), jnp.float32)

    @pl.when(side_slot == 0)
    def _():
        system[2 * F :, :512] = system[2 * F :, :512] + jnp.concatenate([direct, gap], 1)

    @pl.when(side_slot == 1)
    def _():
        system[2 * F :, 384:] = system[2 * F :, 384:] + jnp.concatenate([gap, direct], 1)

    def eliminate(block, carry):
        at = pl.ds(pl.multiple_of(block * LANES, LANES), LANES)
        square = jnp.concatenate(invert([groups_of(system[at, at])])[0], 0)
        scaled = split_matmul(left_parts(square), right_parts(system[at, :]))
        high, low = halves(scaled)
        panel[:LANES] = high
        panel[LANES : 2 * LANES] = low
        high, low = halves(-square)
        panel[:LANES, at] = high
        panel[LANES : 2 * LANES, at] = low
        panel[2 * LANES :] = panel[:LANES]

        def update(start, count):
            rows = pl.ds(pl.multiple_of(start * LANES, LANES), count * LANES)
            left = left_parts(system[rows, at])
            system[rows, at] = jnp.zeros((count * LANES, LANES), jnp.float32)
            system[rows, :] = system[rows, :] - split_matmul(left, panel[...])

        def pairwise(index, inner):
            update(6 - 2 * index, 2)
            return inner

        lax.fori_loop(0, (7 - block) // 2, pairwise, 0)

        @pl.when((7 - block) % 2 == 1)
        def _():
            update(block + 1, 1)

        return carry

    lax.fori_loop(0, 7, eliminate, 0)
    solved = system[2 * F :, :]
    same_pair = jnp.where(pair_slot == 0, 1.0, 0.0)
    square = right_parts(
        jnp.concatenate([inverse_ref[0], jnp.zeros((512 - F, 512), jnp.float32)], 0)
    )
    high = weighted[0, :, :512]
    low = weighted[0, :, 512:1024]
    first = same_pair * split_matmul(coupled_parts, square)
    first = first - split_matmul(left_parts(solved), jnp.concatenate([high, low, high], 0))
    first_ref[...] = first[:, :F]
    second_ref[...] = solved[:, :F]


def output_kernel(first_ref, second_ref, own_ref, other_ref, rows_ref, out_ref, spread):
    @pl.when(pl.program_id(0) == 0)
    def _():
        target = lax.broadcasted_iota(jnp.int32, (112, LANES), 0)
        source = lax.broadcasted_iota(jnp.int32, (112, LANES), 1)
        hit = (NODES * (source // 8) + source % 8 == target) & (source % 8 < NODES)
        compact = jnp.where(hit, 1.0, 0.0)
        orders = node_orders("x first")
        for index, ref in enumerate((first_ref, second_ref)):
            high, low = halves(matmul(compact, ref[...]))
            for place, order in enumerate(orders):
                for part, value in enumerate((high, high, low)):
                    moved = jnp.dot(value, order, preferred_element_type=jnp.float32)
                    spread[index, place, part] = moved.astype(jnp.bfloat16)

    target = lax.broadcasted_iota(jnp.int32, (112, LANES), 0)
    source = lax.broadcasted_iota(jnp.int32, (112, LANES), 1)
    hit = (NODES * (source // 8) + source % 8 == target) & (source % 8 < NODES)
    compact = jnp.where(hit, 1.0, 0.0)
    total = matmul(compact, rows_ref[...].reshape(LANES, -1))
    lefts = []
    rights = []
    for index in range(2):
        for place, ref in enumerate((own_ref, other_ref)):
            lefts += [spread[index, place, part] for part in range(3)]
            rights.append(right_parts(ref[:, :, index].reshape(256, -1)))
    total = total - split_matmul(jnp.concatenate(lefts, 1), jnp.concatenate(rights, 0))
    out_ref[...] = total


def select_kernel(slots_ref, stored_ref, mine_ref, shared_ref, goals_ref):
    box = lax.axis_index("box")
    along_x = box % 2
    along_y = box // 2
    x_shared = slots_ref[box, 1 - along_x]
    y_shared = slots_ref[box, 3 - along_y]
    finals = [
        slots_ref[box, along_x],
        slots_ref[box, 2 + along_y],
        slots_ref[box, 4],
        slots_ref[box, 5],
    ]
    lane = lax.broadcasted_iota(jnp.int32, (8, 512), 1)

    def block(row_slot, col_slot):
        start = pl.multiple_of(((col_slot * 7) // 2) * LANES, LANES)
        value = stored_ref[row_slot, :, pl.ds(start, 512)]
        value = jnp.concatenate([value, jnp.zeros((1, 512), jnp.float32)], 0)
        value = jnp.where(col_slot % 2 == 1, pltpu.roll(value, F, 1), value)
        return jnp.where(lane < F, value, 0.0)

    pieces = [(x_shared, x_shared), (y_shared, x_shared), (y_shared, y_shared)]
    for index, slots in enumerate(pieces):
        value = block(*slots)
        for copy in range(8):
            mine_ref[copy, index] = value
    for index, row_slot in enumerate((x_shared, y_shared)):
        for place, col_slot in enumerate(finals):
            shared_ref[index, :, place * F : place * F + F] = block(row_slot, col_slot)[:, :F]
    for index, row_slot in enumerate(finals):
        for place, col_slot in enumerate((x_shared, y_shared, *finals)):
            value = block(row_slot, col_slot)[:, :F]
            for goal in range(4):
                goals_ref[4 * index + goal, :, place * F : place * F + F] = value


def combine_kernel(line_ref, squares_ref, links_ref):
    box = lax.axis_index("box")
    z_half = lax.axis_index("tile") // 32
    along_x = box % 2
    pair = box - along_x
    for half in range(2):
        base = 4 * (z_half if half == 0 else 1 - z_half)
        mine, beside, other, across = (
            line_ref.at[base + place]
            for place in (
                box,
                pair + 1 - along_x,
                2 - pair + along_x,
                2 - pair + 1 - along_x,
            )
        )
        first = mine[0] + beside[0]
        second = other[0] + across[0]
        for copy in range(16):
            squares_ref[copy, half, 0] = first
            squares_ref[copy, half, 1] = second
        for index, ref in enumerate((mine, beside, other, across)):
            links_ref[half, index] = ref[1]
        links_ref[half, 4] = mine[2] + other[2]
        links_ref[half, 5] = pltpu.roll(beside[2] + across[2], 512 - F, 1)


def other_half(value, axis_part):
    flip = 32 if axis_part == "z" else 1
    return lax.ppermute(value, "tile", [(tile, tile ^ flip) for tile in range(64)])


def to_plane(copies):
    return lax.all_to_all(
        copies, "tile", split_axis=0, concat_axis=0, tiled=True, axis_index_groups=PLANES
    )


def ring_shift(value, axis_part, step):
    unit, length = {"x": (2, 4), "y": (8, 4)}[axis_part]
    pairs = []
    for tile in range(64):
        place = (tile // unit) % length
        pairs.append((tile, tile + ((place + step) % length - place) * unit))
    return lax.ppermute(value, "tile", pairs)


def ring_near(value, axis_part):
    return ring_shift(value, axis_part, 1), ring_shift(value, axis_part, -1)


def ring_far(before, after, axis_part, dim):
    return (
        ring_shift(lax.slice_in_dim(before, 0, 1, axis=dim), axis_part, 1),
        ring_shift(lax.slice_in_dim(after, 1, 2, axis=dim), axis_part, -1),
    )


def ring_stack(own, near, far, dim):
    return jnp.stack([own, *near, jnp.concatenate(far, dim)])


def kernel_call(body, out_shapes, name, micros, **options):
    return pl.pallas_call(
        body,
        out_shape=[
            shape if hasattr(shape, "dtype") else jax.ShapeDtypeStruct(shape, jnp.float32)
            for shape in out_shapes
        ],
        compiler_params=pltpu.CompilerParams(vmem_limit_bytes=VMEM_BYTES),
        cost_estimate=pl.CostEstimate(
            flops=micros * 10**9, bytes_accessed=10**6, transcendentals=0
        ),
        name=name,
        **options,
    )


def per_device(box_maps, face_slots):
    smem = pl.BlockSpec(memory_space=pltpu.SMEM)
    vmem = pl.BlockSpec(memory_space=pltpu.VMEM)
    mine, shared_rows, goals = kernel_call(
        select_kernel,
        [(8, 3, 8, 512), (2, 8, 4 * F), (16, 8, 6 * F)],
        "select_rows",
        2,
        in_specs=[smem, vmem],
        out_specs=[vmem] * 3,
    )(face_slots, box_maps[0])
    spread = [
        (64 * box + 16 * quarter + 4 * face + goal, 64 * goal + 16 * box + 4 * face + quarter)
        for box in range(4)
        for quarter in range(4)
        for face in range(4)
        for goal in range(4)
    ]

    line = lax.all_to_all(
        mine, ("box", "tile"), split_axis=0, concat_axis=0, tiled=True, axis_index_groups=LINES
    )
    shared_far = other_half(shared_rows, "z")

    squares, links = kernel_call(
        combine_kernel,
        [(16, 2, 2, 8, 512), (2, 6, 8, 512)],
        "combine_boxes",
        1,
        in_specs=[vmem],
        out_specs=[vmem] * 2,
    )(line)
    columns = jnp.stack([shared_rows, shared_far])
    columns_near = ring_near(columns, "y")
    links_near = ring_near(links, "x")
    squares_own = to_plane(squares)
    squares_own, columns_near, links_near, goals = lax.optimization_barrier(
        (squares_own, columns_near, links_near, goals)
    )
    row_goals = lax.all_to_all(
        goals, "tile", split_axis=0, concat_axis=0, tiled=True, axis_index_groups=QUARTERS
    )

    squares_other = other_half(squares_own, "core")
    columns_far = ring_far(*columns_near, "y", 0)
    links_far = ring_far(*links_near, "x", 0)
    squares_other, columns_far, links_far = lax.optimization_barrier(
        (squares_other, columns_far, links_far)
    )

    columns = ring_stack(columns, columns_near, columns_far, 0)
    links = ring_stack(links, links_near, links_far, 0)
    columns_near = ring_near(columns, "x")
    links_near = ring_near(links, "y")
    (inverse,) = kernel_call(
        pair_kernel,
        [(2, F, 512)],
        "invert_pairs",
        20,
        in_specs=[vmem] * 2,
        out_specs=[vmem],
        scratch_shapes=[
            pltpu.VMEM((2, 512, 512), jnp.float32),
            pltpu.VMEM((2, LANES, 512), jnp.float32),
        ],
    )(squares_own, squares_other)
    inverse, columns_near, links_near, row_goals = lax.optimization_barrier(
        (inverse, columns_near, links_near, row_goals)
    )
    row_parts = lax.ppermute(row_goals[:, :, : 2 * F], ("box", "tile"), spread)
    links_far = ring_far(*links_near, "y", 1)
    columns_far = ring_far(*columns_near, "x", 1)
    links_far, columns_far = lax.optimization_barrier((links_far, columns_far))
    links_own = ring_stack(links, links_near, links_far, 1).reshape(16, 2, 6, 8, 512)
    links_other = other_half(links_own, "core")
    links_other, row_goals = lax.optimization_barrier((links_other, row_goals))
    columns_own = ring_stack(columns, columns_near, columns_far, 1).reshape(16, 2, 2, 8, 4 * F)
    columns_other = other_half(columns_own, "core")
    own_rows = lax.ppermute(
        row_goals[:, :, 2 * F :],
        ("box", "tile"),
        [pair for pair in spread if pair[0] // 64 == pair[1] // 64],
    )
    system, weighted = kernel_call(
        build_kernel,
        [(2 * F, 2 * F), jax.ShapeDtypeStruct((2, 2 * F, 3 * 512), jnp.bfloat16)],
        "build_system",
        20,
        in_specs=[vmem] * 3,
        out_specs=[vmem] * 2,
        scratch_shapes=[pltpu.VMEM((2, 2 * F, 3 * 512), jnp.bfloat16)],
    )(links_own, links_other, inverse)
    first, second = kernel_call(
        merge_kernel,
        [(LANES, F)] * 2,
        "merge_pairs",
        30,
        in_specs=[vmem] * 4,
        out_specs=[vmem] * 2,
        scratch_shapes=[
            pltpu.VMEM((2 * F + LANES, 2 * F), jnp.float32),
            pltpu.VMEM((3 * LANES, 2 * F), jnp.bfloat16),
        ],
    )(system, weighted, inverse, row_parts)
    (out,) = kernel_call(
        output_kernel,
        [(112, 4 * F)],
        "final_map",
        6,
        grid=(7,),
        in_specs=[
            pl.BlockSpec((LANES, F), lambda i: (0, 0)),
            pl.BlockSpec((LANES, F), lambda i: (0, 0)),
            pl.BlockSpec((16, 2, 2, 8, 256), lambda i: (0, 0, 0, 0, i)),
            pl.BlockSpec((16, 2, 2, 8, 256), lambda i: (0, 0, 0, 0, i)),
            pl.BlockSpec((16, 8, 256), lambda i: (0, 0, i)),
        ],
        out_specs=[pl.BlockSpec((112, 256), lambda i: (0, i))],
        scratch_shapes=[pltpu.VMEM((2, 2, 3, 112, 256), jnp.bfloat16)],
    )(first, second, columns_own, columns_other, own_rows)
    return out


def solution(mesh):
    return jax.shard_map(
        per_device,
        mesh=mesh,
        in_specs=(P("box", None, "tile", None), P()),
        out_specs=P("tile", "box"),
        check_vma=False,
    )
```

```python
import functools

import jax
import jax.numpy as jnp
from jax import lax
from jax.experimental import pallas as pl
from jax.experimental.pallas import tpu as pltpu
from jax.sharding import PartitionSpec as P

F = 448
NODES = 7
LANES = 128
MICRO = 16
VMEM_BYTES = 32 * 1024 * 1024


def tile_of(z, y, x, core):
    return ((z * 4 + y) * 4 + x) * 2 + core


PLANES = [
    [tile_of(z, y, x, core) for y in range(4) for x in range(4)]
    for z in range(2)
    for core in range(2)
]
LINES = [
    [64 * box + 32 * half + tile for half in range(2) for box in range(4)] for tile in range(32)
]
QUARTERS = [[16 * quarter + own for own in range(16)] for quarter in range(4)]


def matmul(left, right):
    return jnp.dot(left, right, precision=lax.Precision.HIGHEST, preferred_element_type=jnp.float32)


def halves(value):
    high = value.astype(jnp.bfloat16)
    return high, (value - high.astype(jnp.float32)).astype(jnp.bfloat16)


def left_parts(value):
    high, low = halves(value)
    return jnp.concatenate([high, high, low], 1)


def right_parts(value, dim=0):
    high, low = halves(value)
    return jnp.concatenate([high, low, high], dim)


def split_matmul(left, right):
    return jnp.dot(left, right, preferred_element_type=jnp.float32)


def split_matmul_nt(left, right):
    return lax.dot_general(
        left, right, (((1,), (1,)), ((), ())), preferred_element_type=jnp.float32
    )


def invert(stack):
    full = (8, LANES)
    lane = lax.broadcasted_iota(jnp.int32, full, 1)
    sub = lax.broadcasted_iota(jnp.int32, full, 0)

    def along_rows(value, row):
        return jnp.broadcast_to(value[row : row + 1, :], full)

    def along_lanes(value, column):
        return jnp.broadcast_to(value[:, column : column + 1], full)

    stack = [list(rows) for rows in stack]
    count = len(stack[0])
    which = range(len(stack))
    for start in range(0, 8 * count, MICRO):
        first = start // 8
        inside = (lane >= start) & (lane < start + MICRO)
        following = [group for group in (first + 2, first + 3) if group < count]
        rest = [g for g in range(count) if g not in (first, first + 1, *following)]
        pivots = [
            [[along_lanes(stack[n][first + h], start + k) for h in range(2)] for k in range(MICRO)]
            for n in which
        ]
        rows = [
            [
                jnp.where(
                    inside,
                    jnp.where(lane == start + 8 * h + sub, 1.0, 0.0),
                    stack[n][first + h],
                )
                for h in range(2)
            ]
            for n in which
        ]
        ahead = [
            [[along_lanes(stack[n][group], start + k) for k in range(MICRO)] for group in following]
            for n in which
        ]
        coming = [pivots[n][0][0] for n in which]
        for j in range(MICRO):
            half, row = divmod(j, 8)
            chosen = sub == row
            for n in which:
                scale = 1.0 / along_rows(coming[n], row)
                pivot_row = along_rows(rows[n][half], row) * scale
                for k in range(j + 1, MICRO):
                    scaled = along_rows(pivots[n][k][half], row) * scale
                    for h in range(2):
                        value = pivots[n][k][h] - pivots[n][j][h] * scaled
                        if k == j + 1 and h == k // 8:
                            coming[n] = value
                        pivots[n][k][h] = jnp.where(chosen, scaled, value) if h == half else value
                for h in range(2):
                    value = rows[n][h] - pivots[n][j][h] * pivot_row
                    rows[n][h] = jnp.where(chosen, pivot_row, value) if h == half else value
        for n in which:
            spread = [along_rows(rows[n][k // 8], k % 8) for k in range(MICRO)]
            for position, group in enumerate(following):
                terms = [ahead[n][position][k] * spread[k] for k in range(MICRO)]
                while len(terms) > 1:
                    terms = [terms[i] + terms[i + 1] for i in range(0, len(terms), 2)]
                stack[n][group] = jnp.where(inside, 0.0, stack[n][group]) - terms[0]
            if rest:
                zero = jnp.zeros(full, jnp.float32)
                held = jnp.concatenate([stack[n][group] for group in rest], 0)
                panel = jnp.concatenate(
                    [zero] * first + rows[n] + [zero] * (LANES // 8 - first - 2), 0
                )
                update = matmul(held, panel)
                for i, group in enumerate(rest):
                    stack[n][group] = (
                        jnp.where(inside, 0.0, stack[n][group]) - update[8 * i : 8 * i + 8]
                    )
            stack[n][first], stack[n][first + 1] = rows[n]
    return stack


def groups_of(value):
    return [value[8 * g : 8 * g + 8, :] for g in range(value.shape[0] // 8)]


def node_orders(layout):
    tile = lax.axis_index("tile")
    core = tile % 2
    shape = (F, 256)
    target = lax.broadcasted_iota(jnp.int32, shape, 0)
    source = lax.broadcasted_iota(jnp.int32, shape, 1)
    inner = source % 8
    place = source // 16
    if layout != "plane":
        in_y, in_x = place // 4, place % 4
        if layout == "x first":
            in_y, in_x = in_x, in_y

        def moved(start, step):
            far = jnp.where(step == 3, 2, 0)
            return (start + jnp.where(step == 1, 3, jnp.where(step == 2, 1, far))) % 4

        place = moved((tile // 8) % 4, in_y) * 4 + moved((tile // 2) % 4, in_x)
    half = (source // 8) % 2
    half = jnp.where(tile >= 32, 1 - half, half)
    orders = []
    for held_core in (core, 1 - core):
        node = NODES * ((half * 16 + place) * 2 + held_core) + inner
        hit = (node == target) & (inner < NODES)
        orders.append(jnp.where(hit, 1.0, 0.0).astype(jnp.bfloat16))
    return orders


def in_node_order(orders, pieces):
    total = None
    for order, piece in zip(orders, pieces):
        for _ in range(3):
            part = piece.astype(jnp.bfloat16)
            piece = piece - part.astype(jnp.float32)
            term = jnp.dot(order, part, preferred_element_type=jnp.float32)
            total = term if total is None else total + term
    return total


def pair_kernel(own_ref, other_ref, inverse_ref, work, panel):
    orders = node_orders("plane")
    for n in range(2):
        pieces = [ref[:, :, n].reshape(256, 512) for ref in (own_ref, other_ref)]
        work[n, :F, :] = in_node_order(orders, pieces)
        work[n, F:, :] = jnp.zeros((512 - F, 512), jnp.float32)

    def eliminate(block, height):
        at = pl.ds(pl.multiple_of(block * LANES, LANES), LANES)
        squares = [groups_of(work[n, at, at])[: height // 8] for n in range(2)]
        inverses = invert(squares)
        for n in range(2):
            square = jnp.concatenate(inverses[n], 0)
            if height < LANES:
                square = jnp.concatenate(
                    [square, jnp.zeros((LANES - height, LANES), jnp.float32)], 0
                )
            left = left_parts(work[n, :, at])
            scaled = split_matmul(left_parts(square), right_parts(work[n, at, :]))
            work[n, :, at] = jnp.zeros((512, LANES), jnp.float32)
            panel[n] = scaled
            panel[n, :, at] = square
            scaled = panel[n]
            work[n] = work[n] - split_matmul(left, right_parts(scaled))
            work[n, at, :] = scaled

    def step(block, carry):
        eliminate(block, LANES)
        return carry

    lax.fori_loop(0, 3, step, 0)
    eliminate(jnp.int32(3), F - 3 * LANES)
    inverse_ref[...] = work[:, :F, :]


def build_kernel(own_ref, other_ref, inverse_ref, system, weighted, coupling):
    orders = node_orders("y first")

    def ordered(index):
        pieces = [ref[:, :, index].reshape(256, 512) for ref in (own_ref, other_ref)]
        return in_node_order(orders, pieces)

    for pair in range(2):
        square = right_parts(
            jnp.concatenate([inverse_ref[pair], jnp.zeros((512 - F, 512), jnp.float32)], 0)
        )
        for side in range(2):
            at = pl.ds(side * F, F)
            left = left_parts(ordered(2 * pair + side))
            coupling[pair, at, :] = left
            weighted[pair, at, :] = right_parts(split_matmul(left, square), 1)

    for half in range(2):
        at = pl.ds(half * F, F)
        total = split_matmul_nt(coupling[0, at, :], weighted[0])
        system[at, :] = -total - split_matmul_nt(coupling[1, at, :], weighted[1])
    system[:F, :512] = system[:F, :512] + ordered(4)
    system[F : 2 * F, 384:] = system[F : 2 * F, 384:] + ordered(5)


def merge_kernel(
    built_ref, weighted, inverse_ref, rows_ref, first_ref, second_ref, system, panel
):
    tile = lax.axis_index("tile")
    box = lax.axis_index("box")
    source_box = tile // 16
    pair_slot = jnp.where(source_box // 2 == box // 2, 0, 1)
    side_slot = jnp.where(source_box % 2 == box % 2, 0, 1)
    system[: 2 * F, :] = built_ref[...]
    coupled = jnp.concatenate(
        [rows_ref[:, :, :F].reshape(LANES, F), jnp.zeros((LANES, 512 - F), jnp.float32)], 1
    )
    coupled_parts = left_parts(coupled)
    system[2 * F :, :] = -split_matmul_nt(coupled_parts, weighted[pair_slot])
    direct = rows_ref[:, :, F : 2 * F].reshape(LANES, F)
    gap = jnp.zeros((LANES, 512 - F), jnp.float32)

    @pl.when(side_slot == 0)
    def _():
        system[2 * F :, :512] = system[2 * F :, :512] + jnp.concatenate([direct, gap], 1)

    @pl.when(side_slot == 1)
    def _():
        system[2 * F :, 384:] = system[2 * F :, 384:] + jnp.concatenate([gap, direct], 1)

    def eliminate(block, carry):
        at = pl.ds(pl.multiple_of(block * LANES, LANES), LANES)
        square = jnp.concatenate(invert([groups_of(system[at, at])])[0], 0)
        scaled = split_matmul(left_parts(square), right_parts(system[at, :]))
        high, low = halves(scaled)
        panel[:LANES] = high
        panel[LANES : 2 * LANES] = low
        high, low = halves(-square)
        panel[:LANES, at] = high
        panel[LANES : 2 * LANES, at] = low
        panel[2 * LANES :] = panel[:LANES]

        def update(start, count):
            rows = pl.ds(pl.multiple_of(start * LANES, LANES), count * LANES)
            left = left_parts(system[rows, at])
            system[rows, at] = jnp.zeros((count * LANES, LANES), jnp.float32)
            system[rows, :] = system[rows, :] - split_matmul(left, panel[...])

        def pairwise(index, inner):
            update(6 - 2 * index, 2)
            return inner

        lax.fori_loop(0, (7 - block) // 2, pairwise, 0)

        @pl.when((7 - block) % 2 == 1)
        def _():
            update(block + 1, 1)

        return carry

    lax.fori_loop(0, 7, eliminate, 0)
    solved = system[2 * F :, :]
    same_pair = jnp.where(pair_slot == 0, 1.0, 0.0)
    square = right_parts(
        jnp.concatenate([inverse_ref[0], jnp.zeros((512 - F, 512), jnp.float32)], 0)
    )
    high = weighted[0, :, :512]
    low = weighted[0, :, 512:1024]
    first = same_pair * split_matmul(coupled_parts, square)
    first = first - split_matmul(left_parts(solved), jnp.concatenate([high, low, high], 0))
    first_ref[...] = first[:, :F]
    second_ref[...] = solved[:, :F]


def output_kernel(first_ref, second_ref, own_ref, other_ref, rows_ref, out_ref, spread):
    @pl.when(pl.program_id(0) == 0)
    def _():
        target = lax.broadcasted_iota(jnp.int32, (112, LANES), 0)
        source = lax.broadcasted_iota(jnp.int32, (112, LANES), 1)
        hit = (NODES * (source // 8) + source % 8 == target) & (source % 8 < NODES)
        compact = jnp.where(hit, 1.0, 0.0)
        orders = node_orders("x first")
        for index, ref in enumerate((first_ref, second_ref)):
            high, low = halves(matmul(compact, ref[...]))
            for place, order in enumerate(orders):
                for part, value in enumerate((high, high, low)):
                    moved = jnp.dot(value, order, preferred_element_type=jnp.float32)
                    spread[index, place, part] = moved.astype(jnp.bfloat16)

    target = lax.broadcasted_iota(jnp.int32, (112, LANES), 0)
    source = lax.broadcasted_iota(jnp.int32, (112, LANES), 1)
    hit = (NODES * (source // 8) + source % 8 == target) & (source % 8 < NODES)
    compact = jnp.where(hit, 1.0, 0.0)
    total = matmul(compact, rows_ref[...].reshape(LANES, -1))
    lefts = []
    rights = []
    for index in range(2):
        for place, ref in enumerate((own_ref, other_ref)):
            lefts += [spread[index, place, part] for part in range(3)]
            rights.append(right_parts(ref[:, :, index].reshape(256, -1)))
    total = total - split_matmul(jnp.concatenate(lefts, 1), jnp.concatenate(rights, 0))
    out_ref[...] = total


def select_kernel(slots_ref, stored_ref, mine_ref, shared_ref, goals_ref):
    box = lax.axis_index("box")
    along_x = box % 2
    along_y = box // 2
    x_shared = slots_ref[box, 1 - along_x]
    y_shared = slots_ref[box, 3 - along_y]
    finals = [
        slots_ref[box, along_x],
        slots_ref[box, 2 + along_y],
        slots_ref[box, 4],
        slots_ref[box, 5],
    ]
    lane = lax.broadcasted_iota(jnp.int32, (8, 512), 1)

    def block(row_slot, col_slot):
        start = pl.multiple_of(((col_slot * 7) // 2) * LANES, LANES)
        value = stored_ref[row_slot, :, pl.ds(start, 512)]
        value = jnp.concatenate([value, jnp.zeros((1, 512), jnp.float32)], 0)
        value = jnp.where(col_slot % 2 == 1, pltpu.roll(value, F, 1), value)
        return jnp.where(lane < F, value, 0.0)

    pieces = [(x_shared, x_shared), (y_shared, x_shared), (y_shared, y_shared)]
    for index, slots in enumerate(pieces):
        value = block(*slots)
        for copy in range(8):
            mine_ref[copy, index] = value
    for index, row_slot in enumerate((x_shared, y_shared)):
        for place, col_slot in enumerate(finals):
            shared_ref[index, :, place * F : place * F + F] = block(row_slot, col_slot)[:, :F]
    for index, row_slot in enumerate(finals):
        for place, col_slot in enumerate((x_shared, y_shared, *finals)):
            value = block(row_slot, col_slot)[:, :F]
            for goal in range(4):
                goals_ref[4 * index + goal, :, place * F : place * F + F] = value


def combine_kernel(line_ref, squares_ref, links_ref):
    box = lax.axis_index("box")
    z_half = lax.axis_index("tile") // 32
    along_x = box % 2
    pair = box - along_x
    for half in range(2):
        base = 4 * (z_half if half == 0 else 1 - z_half)
        mine, beside, other, across = (
            line_ref.at[base + place]
            for place in (
                box,
                pair + 1 - along_x,
                2 - pair + along_x,
                2 - pair + 1 - along_x,
            )
        )
        first = mine[0] + beside[0]
        second = other[0] + across[0]
        for copy in range(16):
            squares_ref[copy, half, 0] = first
            squares_ref[copy, half, 1] = second
        for index, ref in enumerate((mine, beside, other, across)):
            links_ref[half, index] = ref[1]
        links_ref[half, 4] = mine[2] + other[2]
        links_ref[half, 5] = pltpu.roll(beside[2] + across[2], 512 - F, 1)


def other_half(value, axis_part):
    flip = 32 if axis_part == "z" else 1
    return lax.ppermute(value, "tile", [(tile, tile ^ flip) for tile in range(64)])


def to_plane(copies):
    return lax.all_to_all(
        copies, "tile", split_axis=0, concat_axis=0, tiled=True, axis_index_groups=PLANES
    )


def ring_shift(value, axis_part, step):
    unit, length = {"x": (2, 4), "y": (8, 4)}[axis_part]
    pairs = []
    for tile in range(64):
        place = (tile // unit) % length
        pairs.append((tile, tile + ((place + step) % length - place) * unit))
    return lax.ppermute(value, "tile", pairs)


def ring_near(value, axis_part):
    return ring_shift(value, axis_part, 1), ring_shift(value, axis_part, -1)


def ring_far(before, after, axis_part, dim):
    return (
        ring_shift(lax.slice_in_dim(before, 0, 1, axis=dim), axis_part, 1),
        ring_shift(lax.slice_in_dim(after, 1, 2, axis=dim), axis_part, -1),
    )


def ring_stack(own, near, far, dim):
    return jnp.stack([own, *near, jnp.concatenate(far, dim)])


def kernel_call(body, out_shapes, name, micros, **options):
    return pl.pallas_call(
        body,
        out_shape=[
            shape if hasattr(shape, "dtype") else jax.ShapeDtypeStruct(shape, jnp.float32)
            for shape in out_shapes
        ],
        compiler_params=pltpu.CompilerParams(vmem_limit_bytes=VMEM_BYTES),
        cost_estimate=pl.CostEstimate(
            flops=micros * 10**9, bytes_accessed=10**6, transcendentals=0
        ),
        name=name,
        **options,
    )


def per_device(box_maps, face_slots):
    smem = pl.BlockSpec(memory_space=pltpu.SMEM)
    vmem = pl.BlockSpec(memory_space=pltpu.VMEM)
    mine, shared_rows, goals = kernel_call(
        select_kernel,
        [(8, 3, 8, 512), (2, 8, 4 * F), (16, 8, 6 * F)],
        "select_rows",
        2,
        in_specs=[smem, vmem],
        out_specs=[vmem] * 3,
    )(face_slots, box_maps[0])
    spread = [
        (64 * box + 16 * quarter + 4 * face + goal, 64 * goal + 16 * box + 4 * face + quarter)
        for box in range(4)
        for quarter in range(4)
        for face in range(4)
        for goal in range(4)
    ]

    line = lax.all_to_all(
        mine, ("box", "tile"), split_axis=0, concat_axis=0, tiled=True, axis_index_groups=LINES
    )
    shared_far = other_half(shared_rows, "z")

    squares, links = kernel_call(
        combine_kernel,
        [(16, 2, 2, 8, 512), (2, 6, 8, 512)],
        "combine_boxes",
        1,
        in_specs=[vmem],
        out_specs=[vmem] * 2,
    )(line)
    columns = jnp.stack([shared_rows, shared_far])
    columns_near = ring_near(columns, "y")
    links_near = ring_near(links, "x")
    squares_own = to_plane(squares)
    squares_own, columns_near, links_near, goals = lax.optimization_barrier(
        (squares_own, columns_near, links_near, goals)
    )
    row_goals = lax.all_to_all(
        goals, "tile", split_axis=0, concat_axis=0, tiled=True, axis_index_groups=QUARTERS
    )

    squares_other = other_half(squares_own, "core")
    columns_far = ring_far(*columns_near, "y", 0)
    links_far = ring_far(*links_near, "x", 0)
    squares_other, columns_far, links_far = lax.optimization_barrier(
        (squares_other, columns_far, links_far)
    )

    columns = ring_stack(columns, columns_near, columns_far, 0)
    links = ring_stack(links, links_near, links_far, 0)
    columns_near = ring_near(columns, "x")
    links_near = ring_near(links, "y")
    (inverse,) = kernel_call(
        pair_kernel,
        [(2, F, 512)],
        "invert_pairs",
        20,
        in_specs=[vmem] * 2,
        out_specs=[vmem],
        scratch_shapes=[
            pltpu.VMEM((2, 512, 512), jnp.float32),
            pltpu.VMEM((2, LANES, 512), jnp.float32),
        ],
    )(squares_own, squares_other)
    inverse, columns_near, links_near, row_goals = lax.optimization_barrier(
        (inverse, columns_near, links_near, row_goals)
    )
    row_parts = lax.ppermute(row_goals[:, :, : 2 * F], ("box", "tile"), spread)
    links_far = ring_far(*links_near, "y", 1)
    columns_far = ring_far(*columns_near, "x", 1)
    links_far, columns_far = lax.optimization_barrier((links_far, columns_far))
    links_own = ring_stack(links, links_near, links_far, 1).reshape(16, 2, 6, 8, 512)
    links_other = other_half(links_own, "core")
    links_other, row_goals = lax.optimization_barrier((links_other, row_goals))
    columns_own = ring_stack(columns, columns_near, columns_far, 1).reshape(16, 2, 2, 8, 4 * F)
    columns_other = other_half(columns_own, "core")
    own_rows = lax.ppermute(
        row_goals[:, :, 2 * F :],
        ("box", "tile"),
        [pair for pair in spread if pair[0] // 64 == pair[1] // 64],
    )
    system, weighted = kernel_call(
        build_kernel,
        [(2 * F, 2 * F), jax.ShapeDtypeStruct((2, 2 * F, 3 * 512), jnp.bfloat16)],
        "build_system",
        20,
        in_specs=[vmem] * 3,
        out_specs=[vmem] * 2,
        scratch_shapes=[pltpu.VMEM((2, 2 * F, 3 * 512), jnp.bfloat16)],
    )(links_own, links_other, inverse)
    first, second = kernel_call(
        merge_kernel,
        [(LANES, F)] * 2,
        "merge_pairs",
        30,
        in_specs=[vmem] * 4,
        out_specs=[vmem] * 2,
        scratch_shapes=[
            pltpu.VMEM((2 * F + LANES, 2 * F), jnp.float32),
            pltpu.VMEM((3 * LANES, 2 * F), jnp.bfloat16),
        ],
    )(system, weighted, inverse, row_parts)
    (out,) = kernel_call(
        output_kernel,
        [(112, 4 * F)],
        "final_map",
        6,
        grid=(7,),
        in_specs=[
            pl.BlockSpec((LANES, F), lambda i: (0, 0)),
            pl.BlockSpec((LANES, F), lambda i: (0, 0)),
            pl.BlockSpec((16, 2, 2, 8, 256), lambda i: (0, 0, 0, 0, i)),
            pl.BlockSpec((16, 2, 2, 8, 256), lambda i: (0, 0, 0, 0, i)),
            pl.BlockSpec((16, 8, 256), lambda i: (0, 0, i)),
        ],
        out_specs=[pl.BlockSpec((112, 256), lambda i: (0, i))],
        scratch_shapes=[pltpu.VMEM((2, 2, 3, 112, 256), jnp.bfloat16)],
    )(first, second, columns_own, columns_other, own_rows)
    return out


def solution(mesh):
    return jax.shard_map(
        per_device,
        mesh=mesh,
        in_specs=(P("box", None, "tile", None), P()),
        out_specs=P("tile", "box"),
        check_vma=False,
    )
```
